32 devices in a mesh: ctx: 16 (over z, y, core), fsdp: 2 (over x).
Axes of the slice: x: 2, y: 2, z: 4, core: 2. Of those that a mesh axis runs over, the one named last changes fastest.
Arguments:
- layer_input: bfloat16 [2, 4096, 768], P('fsdp', 'ctx'), may hold values from -6 to 6
- doc_lengths: int32 [2, 16], P('fsdp'), may hold values from 1 to 2048, 4096 in all within a row
- ln1_gain: bfloat16 [768], P('fsdp'), may hold values from 0.5 to 1.5
- ln1_bias: bfloat16 [768], P('fsdp'), may hold values from -3 to 3
- ln2_gain: bfloat16 [768], P('fsdp'), may hold values from 0.5 to 1.5
- ln2_bias: bfloat16 [768], P('fsdp'), may hold values from -3 to 3
- qkv_weight: bfloat16 [768, 896], P('fsdp'), may hold values from -0.21875 to 0.21875
- qkv_bias: bfloat16 [896], P('fsdp'), may hold values from -3 to 3
- out_weight: bfloat16 [768, 768], P('fsdp'), may hold values from -1 to 1
- out_bias: bfloat16 [768], P('fsdp'), may hold values from -3 to 3
- up_weight: bfloat16 [768, 3072], P('fsdp'), may hold values from -0.21875 to 0.21875
- up_bias: bfloat16 [3072], P('fsdp'), may hold values from -3 to 3
- down_weight: bfloat16 [3072, 768], P('fsdp'), may hold values from -0.109375 to 0.109375
- down_bias: bfloat16 [768], P('fsdp'), may hold values from -3 to 3
- out_grad: bfloat16 [2, 4096, 768], P('fsdp', 'ctx'), may hold values from -6 to 6
- kv_grad_later: float32 [2, 4096, 128], P('fsdp', 'ctx'), may hold values from -8 to 8
Outputs:
- layer_output: bfloat16 [2, 4096, 768], P('fsdp', 'ctx')
- x_grad: float32 [2, 4096, 768], P('fsdp', 'ctx')
- ln1_gain_grad: float32 [768], P('fsdp')
- ln1_bias_grad: float32 [768], P('fsdp')
- ln2_gain_grad: float32 [768], P('fsdp')
- ln2_bias_grad: float32 [768], P('fsdp')
- qkv_weight_grad: float32 [768, 896], P('fsdp')
- qkv_bias_grad: float32 [896], P('fsdp')
- out_weight_grad: float32 [768, 768], P('fsdp')
- out_bias_grad: float32 [768], P('fsdp')
- up_weight_grad: float32 [768, 3072], P('fsdp')
- up_bias_grad: float32 [3072], P('fsdp')
- down_weight_grad: float32 [3072, 768], P('fsdp')
- down_bias_grad: float32 [768], P('fsdp')
The draws below stay inside these ranges and needn't reach their ends.
Inputs may be any that keep to these rules, and one draw needn't show every extreme that they name: `doc_lengths`: each row lists the 16 documents of one stream in order; they fill its 4096 tokens and the longest has exactly 2048.
All inputs are finite; a program needn't handle non-finite values.
Results may differ from the reference program's by a relative error of at most 0.011.
Values may be sent and summed in bfloat16 or wider, within the bound.
No kernel may reach another device: no remote copies, remote signals or barrier semaphores. Data moves between devices by JAX's collectives and lax.ppermute only.
A program may use at most 192 MiB of HBM per device.

```python
import math
import jax
import jax.numpy as jnp
import numpy as np
from jax import lax

D = 768
HD = 64
FF = 3072
ROT = 16
TOK_DEV = 256
NDOC = 16
STREAMS = 2
STREAM = 4096
MAXDOC = 2048
N_CTX = 16


def steps_of(key, extent, shards, low, top_value):
    level, own = 1.0, jax.random.fold_in(key, 6)
    for axis_at, parts in shards:
        draws = jnp.exp(jax.random.uniform(jax.random.fold_in(own, axis_at), (parts,), jnp.float32, low / len(shards), top_value / len(shards)))
        level = level * jnp.repeat(draws, extent[axis_at] // parts).reshape([-1 if axis == axis_at else 1 for axis in range(len(extent))])
    return level


def split_up(count, total, reach, skew):
    loads = [(1 << 20) // math.isqrt(standing ** skew) + 1 for standing in range(2, count + 1)]
    spare, holding = total - reach - (count - 1), [1] * (count - 1)
    while spare > 0:
        movable = [i for i in range(count - 1) if holding[i] < reach]
        mass, left = sum([loads[i] for i in movable]), spare
        for i in movable:
            more = min(reach - holding[i], max(1, left * loads[i] // mass), spare)
            holding[i] = holding[i] + more
            spare = spare - more
    return np.array([reach] + holding)


def uneven(key, number_of, total, bound, lean):
    if number_of == 2:
        one = jax.random.randint(key, (), max(1, total - bound), min(bound, total - 1) + 1)
        return jnp.stack([one, total - one])
    tallies = jnp.asarray(split_up(number_of, total, bound, lean), jnp.int32)
    twos = (number_of - 1) // 2
    giver, receiver = tallies[1:1 + 2 * twos:2], tallies[2:2 + 2 * twos:2]
    slack = jnp.minimum(giver - 1, bound - receiver)
    moved = jax.random.randint(jax.random.fold_in(key, 1), (twos,), 0, 1 << 20) % (slack + 1)
    tallies = tallies.at[1:1 + 2 * twos:2].set(giver - moved).at[2:2 + 2 * twos:2].set(receiver + moved)
    return tallies[jax.random.permutation(jax.random.fold_in(key, 2), number_of)]


def bell_draw(stream_key, dims, spread, bound, shards=(), kind=jnp.bfloat16):
    array = jax.random.normal(stream_key, dims, jnp.float32) * spread
    if len(shards) > 0:
        array = steps_of(stream_key, dims, shards, -0.22, 0.18) * array
    return jnp.clip(array, min=-bound, max=bound).astype(kind)


def setup_inputs(seed: int = 0) -> dict:
    arg_keys = jax.random.split(jax.random.key(seed), 17)
    layer_input = bell_draw(arg_keys[0], (STREAMS, STREAM, D), 1.0, 6.0, ((0, 2), (1, 16)))
    doc_lengths = jax.vmap(lambda own: uneven(own, NDOC, STREAM, MAXDOC, 2))(jax.random.split(arg_keys[1], STREAMS)).reshape((STREAMS, NDOC)).astype(jnp.int32)
    ln1_gain = jnp.clip(1.0 + 0.1 * jax.random.normal(arg_keys[2], (D,), jnp.float32), 0.5, 1.5).astype(jnp.bfloat16)
    ln1_bias = bell_draw(arg_keys[3], (D,), 0.2, 3.0, ((0, 2),))
    ln2_gain = jnp.clip(1.0 + 0.1 * jax.random.normal(arg_keys[4], (D,), jnp.float32), 0.5, 1.5).astype(jnp.bfloat16)
    ln2_bias = bell_draw(arg_keys[5], (D,), 0.2, 3.0, ((0, 2),))
    qkv_weight = bell_draw(arg_keys[6], (D, D + 2 * HD), D ** -0.5, 0.21875, ((0, 2),))
    qkv_bias = bell_draw(arg_keys[7], (D + 2 * HD,), 0.2, 3.0, ((0, 2),))
    out_weight = bell_draw(arg_keys[8], (D, D), 32 ** -0.5, 1.0, ((0, 2),))
    out_bias = bell_draw(arg_keys[9], (D,), 0.2, 3.0, ((0, 2),))
    up_weight = bell_draw(arg_keys[10], (D, FF), D ** -0.5, 0.21875, ((0, 2),))
    up_bias = bell_draw(arg_keys[11], (FF,), 0.2, 3.0, ((0, 2),))
    down_weight = bell_draw(arg_keys[12], (FF, D), FF ** -0.5, 0.109375, ((0, 2),))
    down_bias = bell_draw(arg_keys[13], (D,), 0.2, 3.0, ((0, 2),))
    out_grad = bell_draw(arg_keys[14], (STREAMS, STREAM, D), 1.0, 6.0, ((0, 2), (1, 16)))
    kv_grad_later = bell_draw(arg_keys[15], (STREAMS, STREAM, 2 * HD), 2.0, 8.0, ((0, 2), (1, 16)), jnp.float32)
    return {"layer_input": layer_input, "doc_lengths": doc_lengths, "ln1_gain": ln1_gain, "ln1_bias": ln1_bias, "ln2_gain": ln2_gain, "ln2_bias": ln2_bias, "qkv_weight": qkv_weight, "qkv_bias": qkv_bias, "out_weight": out_weight, "out_bias": out_bias, "up_weight": up_weight, "up_bias": up_bias, "down_weight": down_weight, "down_bias": down_bias, "out_grad": out_grad, "kv_grad_later": kv_grad_later}


HIGH = lax.Precision.HIGHEST

@jax.custom_vjp
def low(v):
    return lax.optimization_barrier(v.astype(jnp.bfloat16)).astype(jnp.float32)

@jax.custom_vjp
def low_back(v):
    return v

def low_keep(v):
    return (low(v), None)

def low_pass(kept, grad):
    return (grad,)

def back_keep(v):
    return (v, None)

def back_low(kept, grad):
    return (low(grad),)
low.defvjp(low_keep, low_pass)
low_back.defvjp(back_keep, back_low)

def layer_norm(values, norm_gain, norm_shift):
    centred = values - lax.optimization_barrier(jnp.mean(values, axis=-1, keepdims=True))
    scaled = centred * lax.rsqrt(lax.optimization_barrier(jnp.mean(centred * centred, axis=-1, keepdims=True)) + 1e-05)
    return scaled * norm_gain + norm_shift

def rotate(values, places):
    half_rot = ROT // 2
    frequencies = 10000.0 ** (-jnp.arange(half_rot, dtype=jnp.float32) / half_rot)
    angles = places[:, None] * frequencies[None, :]
    cosine_table = jnp.concatenate([jnp.cos(angles), jnp.cos(angles)], axis=-1)[:, None, :]
    sine_table = jnp.concatenate([jnp.sin(angles), jnp.sin(angles)], axis=-1)[:, None, :]
    leading = values[..., :ROT]
    turned = leading * cosine_table + jnp.concatenate([-leading[..., half_rot:], leading[..., :half_rot]], axis=-1) * sine_table
    return jnp.concatenate([turned, values[..., ROT:]], axis=-1)

def attend_block(queries, q_places, q_starts, key_rows, values):
    key_places = jnp.arange(key_rows.shape[0], dtype=jnp.int32)
    scores = jnp.einsum('thd,kd->thk', queries, key_rows, precision=HIGH) * HD ** (-0.5)
    allowed = (key_places[None, :] <= q_places[:, None]) & (key_places[None, :] >= q_starts[:, None])
    scores = low_back(jnp.where(allowed[:, None, :], scores, -1e+30))
    row_peak = lax.optimization_barrier(jnp.max(scores, axis=-1, keepdims=True))
    weights = jnp.exp(scores - row_peak)
    row_total = lax.optimization_barrier(jnp.sum(weights, axis=-1, keepdims=True))
    return jnp.einsum('thk,kd->thd', low(weights), values, precision=HIGH) / row_total

def block_layer(params, stream_x, q_starts):
    first_gain, first_shift, second_gain, second_shift, w_qkv, bias_qkv, w_out, bias_out, w_up, bias_up, w_down, bias_down = params
    length = stream_x.shape[0]
    head_count = D // HD
    place_ids = jnp.arange(length, dtype=jnp.int32)
    places = place_ids.astype(jnp.float32)
    first_norm = low(layer_norm(stream_x, first_gain, first_shift))
    second_norm = low(layer_norm(stream_x, second_gain, second_shift))
    mixed = low_back(jnp.dot(first_norm, w_qkv, precision=HIGH, preferred_element_type=jnp.float32) + bias_qkv)
    queries = low(rotate(mixed[:, :D].reshape(length, head_count, HD), places))
    key_rows = low(rotate(mixed[:, D:D + HD].reshape(length, 1, HD), places)[:, 0])
    values = low(mixed[:, D + HD:])
    query_block = min(512, length)
    blocks = length // query_block

    def attend(pieces):
        return attend_block(pieces[0], pieces[1], pieces[2], key_rows, values)
    attended = lax.map(jax.checkpoint(attend), (queries.reshape(blocks, query_block, head_count, HD), place_ids.reshape(blocks, query_block), q_starts.reshape(blocks, query_block)))
    attended = low(low_back(attended.reshape(length, D)))
    attention = jnp.dot(attended, w_out, precision=HIGH, preferred_element_type=jnp.float32) + bias_out
    hidden = low_back(jnp.dot(second_norm, w_up, precision=HIGH, preferred_element_type=jnp.float32) + bias_up)
    activated = low(jax.nn.gelu(hidden, approximate=False))
    feed_forward = jnp.dot(activated, w_down, precision=HIGH, preferred_element_type=jnp.float32) + bias_down
    return (stream_x + attention + feed_forward, jnp.concatenate([key_rows, values], axis=-1))

def reference(layer_input, doc_lengths, ln1_gain, ln1_bias, ln2_gain, ln2_bias, qkv_weight, qkv_bias, out_weight, out_bias, up_weight, up_bias, down_weight, down_bias, out_grad, kv_grad_later):
    half_rows = TOK_DEV // 2
    row_ids = jnp.arange(STREAM, dtype=jnp.int32)
    slot_ids = row_ids // half_rows
    device_ids = slot_ids // 2
    stream_block = jnp.where(slot_ids % 2 == 0, device_ids, 2 * N_CTX - 1 - device_ids)
    place_of = (stream_block * half_rows + row_ids % half_rows).astype(jnp.int32)
    inverse = jnp.zeros((STREAM,), jnp.int32).at[place_of].set(row_ids)
    params = tuple((a.astype(jnp.float32) for a in (ln1_gain, ln1_bias, ln2_gain, ln2_bias, qkv_weight, qkv_bias, out_weight, out_bias, up_weight, up_bias, down_weight, down_bias)))
    totals = tuple((jnp.zeros(a.shape, jnp.float32) for a in params))
    output_rows = []
    input_grads = []
    for stream in range(STREAMS):
        lengths = doc_lengths[stream]
        doc_ends = jnp.cumsum(lengths)
        natural = jnp.arange(STREAM, dtype=jnp.int32)
        starts = lax.optimization_barrier(jnp.sum(jnp.where(doc_ends[None, :] <= natural[:, None], lengths[None, :], 0), axis=1)).astype(jnp.int32)
        stream_x = layer_input[stream].astype(jnp.float32)[inverse]
        cotangent = out_grad[stream].astype(jnp.float32)[inverse]
        later_grads = kv_grad_later[stream].astype(jnp.float32)[inverse]
        outputs, pull_back = jax.vjp(lambda prm, val: block_layer(prm, val, starts), params, stream_x)
        param_grads, input_grad = pull_back((cotangent, later_grads))
        output_rows.append(outputs[0].astype(jnp.bfloat16)[place_of])
        input_grads.append(input_grad[place_of])
        totals = tuple((t + g for t, g in zip(totals, param_grads)))
    return (jnp.stack(output_rows), jnp.stack(input_grads), totals[0], totals[1], totals[2], totals[3], totals[4], totals[5], totals[6], totals[7], totals[8], totals[9], totals[10], totals[11])
```

```python
from functools import partial

import jax
import jax.numpy as jnp
import numpy as np
from jax import lax
from jax.experimental import pallas as pl
from jax.experimental.pallas import tpu as pltpu
from jax.sharding import PartitionSpec as P

ROT = 16
BLOCK = 128
NT = (((1,), (1,)), ((), ()))
NN = (((1,), (0,)), ((), ()))
TN = (((0,), (0,)), ((), ()))
bf16 = jnp.bfloat16
f32 = jnp.float32


def mm(left, right, dims=NN):
    return lax.dot_general(left, right, dims, preferred_element_type=f32)


def vmem():
    return pl.BlockSpec(memory_space=pltpu.VMEM)


def smem():
    return pl.BlockSpec(memory_space=pltpu.SMEM)


def bit_reverse(index, count):
    out, left = index * 0, count
    while left > 1:
        out = out * 2 + index % 2
        index = index // 2
        left //= 2
    return out


def swap_x(value):
    return lax.ppermute(value, "fsdp", [(0, 1), (1, 0)])


def swap_ctx(value, stride, devices):
    return lax.ppermute(value, "ctx", [(i, i ^ stride) for i in range(devices)])


def in_order(bit, mine, theirs, axis=0):
    return jnp.where(
        bit == 0,
        jnp.concatenate([mine, theirs], axis=axis),
        jnp.concatenate([theirs, mine], axis=axis),
    )


def gather_bits(value, strides, devices):
    me = lax.axis_index("ctx")
    for stride in strides:
        value = in_order((me // stride) % 2, value, swap_ctx(value, stride, devices))
    return value


def scatter_bits(value, strides, devices):
    me = lax.axis_index("ctx")
    for stride in strides:
        bit = (me // stride) % 2
        half = value.shape[0] // 2
        keep = lax.dynamic_slice_in_dim(value, bit * half, half, 0)
        send = lax.dynamic_slice_in_dim(value, (1 - bit) * half, half, 0)
        value = keep.astype(f32) + swap_ctx(send.astype(bf16), stride, devices).astype(f32)
    return value


def up_strides(devices):
    out, stride = [], 1
    while stride < devices:
        out.append(stride)
        stride *= 2
    return out


def attn_kernel(
    n_dev, docs, ids_ref, len_ref, q_ref, kv_ref, g_ref, cos_ref, sin_ref,
    o_ref, dm_ref, dkv_ref, qz, gz, ot, dqt, st, bias, ds_sc, p_sc, acc,
):
    b = BLOCK
    kb = 2 * b
    width = q_ref.shape[1]
    pairs = width // 128
    me = ids_ref[0]
    low = lax.broadcasted_iota(jnp.int32, (b, 128), 1) < 64
    acc[...] = jnp.zeros_like(acc)

    def row_of(j):
        j = jnp.maximum(j, 0)
        dev = jnp.where(j < n_dev, j, 2 * n_dev - 1 - j)
        return (bit_reverse(dev, n_dev) * 2 + jnp.where(j < n_dev, 0, 1)) * b

    def half_turn(two):
        return pltpu.roll(two.astype(f32), 64, 1).astype(bf16)

    def side_step(side, carry):
        block = jnp.where(side == 0, me, 2 * n_dev - 1 - me)
        base = block * b
        rows = pl.ds(pl.multiple_of(side * b, b), b)
        qpos = base + lax.broadcasted_iota(jnp.int32, (1, b), 1)
        total = jnp.int32(0)
        qstart = jnp.zeros((1, b), jnp.int32)
        first = jnp.int32(0)
        for e in range(docs):
            size = len_ref[0, e]
            total = total + size
            qstart = qstart + jnp.where(total <= qpos, size, 0)
            first = first + jnp.where(total <= base, size, 0)
        steps = (base + b - first + kb - 1) // kb
        for p in range(pairs):
            cols = pl.ds(p * 128, 128)
            two = q_ref[rows, cols]
            zero = jnp.zeros_like(two)
            qz[pl.ds(p * 256, 128), :] = jnp.where(low, two, zero)
            qz[pl.ds(p * 256 + 128, 128), :] = jnp.where(low, half_turn(two), zero)
            two = g_ref[rows, cols]
            gz[pl.ds(p * 256, 128), :] = jnp.where(low, zero, half_turn(two))
            gz[pl.ds(p * 256 + 128, 128), :] = jnp.where(low, zero, two)
        ot[...] = jnp.zeros_like(ot)
        dqt[...] = jnp.zeros_like(dqt)
        st[0] = jnp.full(st.shape[1:], -1e30, f32)
        st[1] = jnp.zeros(st.shape[1:], f32)

        def load(t):
            hi = block - 2 * t
            r1 = pl.multiple_of(row_of(hi), b)
            r0 = pl.multiple_of(row_of(hi - 1), b)
            kvb = jnp.concatenate([kv_ref[pl.ds(r0, b), :], kv_ref[pl.ds(r1, b), :]], axis=0)
            kpos = (hi - 1) * b + lax.broadcasted_iota(jnp.int32, (kb, b), 0)
            ok = (kpos <= qpos) & (kpos >= qstart)
            bias[...] = jnp.where(ok, 0.0, -1e30)
            return kvb, r0, r1

        def forward(t, carry):
            kvb, _, _ = load(t)
            vt = kvb.astype(f32).T.astype(bf16)[64:]
            mask = bias[...]
            for p in range(pairs):
                s2 = mm(kvb, qz[pl.ds(p * 256, 256), :], NT)
                for i in range(2):
                    h = 2 * p + i
                    s = s2[:, i * 128 : (i + 1) * 128] + mask
                    old = st[0, h : h + 1, :]
                    new = jnp.maximum(old, jnp.max(s, axis=0, keepdims=True))
                    e = jnp.exp(s - new)
                    alpha = jnp.exp(old - new)
                    st[0, h : h + 1, :] = new
                    st[1, h : h + 1, :] = st[1, h : h + 1, :] * alpha + jnp.sum(e, axis=0, keepdims=True)
                    hs = pl.ds(h * 64, 64)
                    ot[hs, :] = ot[hs, :] * alpha + mm(vt, e.astype(bf16))
            return 0

        lax.fori_loop(0, steps, forward, 0)

        for p in range(pairs):
            cols = pl.ds(p * 128, 128)
            gt = g_ref[rows, cols].astype(f32).T
            halves = []
            for i in range(2):
                h = 2 * p + i
                l = st[1, h : h + 1, :]
                o = ot[pl.ds(h * 64, 64), :] / l
                halves.append(o)
                st[2, h : h + 1, :] = jnp.sum(o * gt[i * 64 : (i + 1) * 64], axis=0, keepdims=True)
                st[0, h : h + 1, :] = st[0, h : h + 1, :] + jnp.log(l)
            o_ref[rows, cols] = jnp.concatenate(halves, axis=0).T.astype(bf16)

        def backward(t, carry):
            kvb, r0, r1 = load(t)
            kt = kvb.astype(f32).T.astype(bf16)[:64]
            mask = bias[...]
            for p in range(pairs):
                s2 = mm(kvb, qz[pl.ds(p * 256, 256), :], NT)
                dp2 = mm(kvb, gz[pl.ds(p * 256, 256), :], NT)
                for i in range(2):
                    h = 2 * p + i
                    sl = slice(i * 128, (i + 1) * 128)
                    pr = jnp.exp((s2[:, sl] + mask) - st[0, h : h + 1, :])
                    ds = pr * (dp2[:, sl] - st[2, h : h + 1, :])
                    ds_sc[:, h * 128 : (h + 1) * 128] = ds.astype(bf16)
                    p_sc[:, h * 128 : (h + 1) * 128] = pr.astype(bf16)
            part = mm(ds_sc[...], qz[...]) + mm(p_sc[...], gz[...])
            acc[pl.ds(r0, b), :] += part[:b]
            acc[pl.ds(r1, b), :] += part[b:]
            dqt[...] += mm(kt, ds_sc[...])
            return 0

        lax.fori_loop(0, steps, backward, 0)

        cos = cos_ref[side]
        sin = sin_ref[side]
        for p in range(pairs):
            halves = []
            for i in range(2):
                h = 2 * p + i
                g = dqt[:, h * 128 : (h + 1) * 128] * 0.125
                g0, g1 = g[:8], g[8:16]
                halves += [g0 * cos + g1 * sin, g1 * cos - g0 * sin, g[16:]]
            dm_ref[rows, pl.ds(p * 128, 128)] = jnp.concatenate(halves, axis=0).T.astype(bf16)
        return 0

    lax.fori_loop(0, 2, side_step, 0)
    dkv_ref[...] = acc[...].astype(dkv_ref.dtype)


def attention(n_dev, me, lengths, q, kv, g, cos, sin):
    tokens, width = q.shape
    stream = kv.shape[0]
    rows = width // 64 * 128
    return pl.pallas_call(
        partial(attn_kernel, n_dev, lengths.shape[1]),
        out_shape=(
            jax.ShapeDtypeStruct((tokens, width), bf16),
            jax.ShapeDtypeStruct((tokens, width), bf16),
            jax.ShapeDtypeStruct((stream, 128), bf16),
        ),
        in_specs=[smem(), smem(), vmem(), vmem(), vmem(), vmem(), vmem()],
        out_specs=(vmem(), vmem(), vmem()),
        scratch_shapes=[
            pltpu.VMEM((rows, 128), bf16),
            pltpu.VMEM((rows, 128), bf16),
            pltpu.VMEM((width, 128), f32),
            pltpu.VMEM((64, rows), f32),
            pltpu.VMEM((3, 16, 128), f32),
            pltpu.VMEM((256, 128), f32),
            pltpu.VMEM((256, rows), bf16),
            pltpu.VMEM((256, rows), bf16),
            pltpu.VMEM((stream, 128), f32),
        ],
        cost_estimate=pl.CostEstimate(flops=20_000_000_000, transcendentals=10_000_000, bytes_accessed=4_000_000),
        name="attn",
    )(me, lengths, q, kv, g, cos, sin)


def project_kernel(scale, a_ref, w_ref, b_ref, c_ref, s1_ref, s2_ref, o_ref):
    for p in range(o_ref.shape[1] // 128):
        cols = pl.ds(p * 128, 128)
        m = mm(a_ref[...], w_ref[:, cols]) + b_ref[:, cols]
        turned = (
            m * c_ref[...]
            + pltpu.roll(m, 120, 1) * s1_ref[...]
            + pltpu.roll(m, 8, 1) * s2_ref[...]
        )
        low = turned.astype(bf16)
        o_ref[:, cols] = low if scale == 1.0 else (low.astype(f32) * scale).astype(bf16)


def project(a, w, bias, tables, scale, name):
    return pl.pallas_call(
        partial(project_kernel, scale),
        out_shape=jax.ShapeDtypeStruct((a.shape[0], w.shape[1]), bf16),
        in_specs=[vmem()] * 6,
        out_specs=vmem(),
        name=name,
    )(a, w, bias, *tables)


def layer_stats(values):
    centred = values - jnp.mean(values, axis=-1, keepdims=True)
    root = lax.rsqrt(jnp.mean(centred * centred, axis=-1, keepdims=True) + 1e-05)
    return centred * root, root


def norm_back(grad_norm, normed, root, gain):
    upstream = grad_norm * gain
    return root * (
        upstream
        - jnp.mean(upstream, axis=-1, keepdims=True)
        - normed * jnp.mean(upstream * normed, axis=-1, keepdims=True)
    )


def gelu_parts(values):
    phi = 0.5 * (1.0 + lax.erf(values * 0.7071067811865476))
    slope = phi + values * jnp.exp(-0.5 * values * values) * 0.3989422804014327
    return values * phi, slope


def body(
    layer_input, doc_lengths, ln1_gain, ln1_bias, ln2_gain, ln2_bias, qkv_weight, qkv_bias,
    out_weight, out_bias, up_weight, up_bias, down_weight, down_bias, out_grad, kv_grad_later,
):
    devices = lax.axis_size("ctx")
    me = lax.axis_index("ctx")
    side = lax.axis_index("fsdp")
    tokens, width = layer_input.shape[1:]
    half_rows = tokens // 2
    half = width // 2
    head = kv_grad_later.shape[2] // 2
    wide = up_weight.shape[1] // 2
    strides = up_strides(devices)
    near = strides[:2]

    def other_half(value, axis, size):
        return lax.dynamic_slice_in_dim(value, (1 - side) * size, size, axis)

    def own_half(value, axis, size):
        return lax.dynamic_slice_in_dim(value, side * size, size, axis)

    def fetch(value):
        part = value.shape[0] // 4
        piece = bit_reverse(me % 4, 4) * part
        return gather_bits(swap_x(lax.dynamic_slice_in_dim(value, piece, part, 0)), near[::-1], devices)

    vectors = (ln1_gain, ln1_bias, ln2_gain, ln2_bias, qkv_bias, out_bias, up_bias, down_bias)
    packed = jnp.concatenate(vectors)
    packed = jnp.pad(packed, (0, -packed.shape[0] % 1024)).reshape(-1, 128)
    packed_other = swap_x(packed).reshape(-1)
    full, at = [], 0
    for vec in vectors:
        size = vec.shape[0]
        full.append(in_order(side, vec, packed_other[at : at + size]).astype(f32)[None])
        at += size
    gain1, shift1, gain2, shift2, bias_qkv, bias_out, bias_up, bias_down = full

    w_kv = in_order(side, qkv_weight[:, width:], swap_x(qkv_weight[:, width:]))
    x_own = layer_input[0]
    x_other = swap_x(x_own)
    dy_own = out_grad[0]
    dy_other = swap_x(dy_own)
    up_other = fetch(other_half(up_weight, 1, wide))
    w_up = in_order(side, own_half(up_weight, 1, wide), up_other)
    w_q = in_order(side, qkv_weight[:, :width], fetch(qkv_weight[:, :width]))

    offsets = jnp.arange(half_rows, dtype=jnp.int32)
    places = jnp.concatenate([me * half_rows + offsets, (2 * devices - 1 - me) * half_rows + offsets]).astype(f32)
    half_rot = ROT // 2
    freq = 10000.0 ** (-jnp.arange(half_rot, dtype=f32) / half_rot)
    lane = np.arange(128)
    lane_freq = jnp.tile(freq, 128 // half_rot)[None, :]
    angles = places[:, None] * lane_freq
    cosine, sine = jnp.cos(angles), jnp.sin(angles)
    q_tables = (
        jnp.where(lane % 64 < 16, cosine, 1.0),
        jnp.where(lane % 64 < 8, -sine, 0.0),
        jnp.where((lane % 64 >= 8) & (lane % 64 < 16), sine, 0.0),
    )
    kv_tables = tuple(jnp.where(lane < 64, t, v) for t, v in zip(q_tables, (1.0, 0.0, 0.0)))
    t_angles = places.reshape(2, 1, half_rows) * freq[None, :, None]
    cos_t, sin_t = jnp.cos(t_angles), jnp.sin(t_angles)

    own_float = x_own.astype(f32)
    hat, root = layer_stats(own_float)
    hat_other, _ = layer_stats(x_other.astype(f32))
    first_own = (hat * gain1 + shift1).astype(bf16)
    first_other = (hat_other * gain1 + shift1).astype(bf16)
    second = jnp.concatenate([hat * gain2 + shift2, hat_other * gain2 + shift2], axis=0).astype(bf16)
    dy = jnp.concatenate([dy_own, dy_other], axis=0)

    kv = project(first_own, w_kv, bias_qkv[:, width:], kv_tables, 1.0, "kv")
    kv_all = gather_bits(kv, strides[::-1], devices)
    q = project(first_own, w_q, bias_qkv[:, :width], q_tables, 0.125, "q")

    d_o = mm(dy, out_weight, NT).astype(bf16)
    d_o_full = in_order(side, d_o[:tokens], swap_x(d_o[tokens:]), axis=1)

    hidden = mm(second, w_up) + own_half(bias_up, 1, wide)
    act, slope = gelu_parts(hidden)
    act = act.astype(bf16)
    d_hidden = (mm(dy, down_weight, NT) * slope).astype(bf16)
    ff = mm(act, down_weight)
    d_second = mm(d_hidden, w_up, NT)
    g_down = mm(act, dy, TN).astype(bf16)
    g_up = mm(second, d_hidden, TN).astype(bf16)
    g_up_bias = jnp.sum(d_hidden.astype(f32), axis=0)
    d_second_own = d_second[:tokens] + swap_x(d_second[tokens:].astype(bf16)).astype(f32)

    g_down_part = lax.psum_scatter(g_down, "ctx", scatter_dimension=0, tiled=True)
    g_up_part = lax.psum_scatter(g_up.reshape(2, half, wide), "ctx", scatter_dimension=1, tiled=True)
    mine = lax.dynamic_index_in_dim(g_up_part, side, 0, keepdims=False)
    theirs = swap_x(lax.dynamic_index_in_dim(g_up_part, 1 - side, 0, keepdims=False))
    g_up_part = in_order(side, mine, theirs, axis=1)
    g_down_all = lax.all_gather(g_down_part, "ctx", axis=0, tiled=True).astype(f32)
    g_up_all = lax.all_gather(g_up_part, "ctx", axis=0, tiled=True).astype(f32)

    attended, dm_q, d_kv = attention(
        devices, me.reshape(1).astype(jnp.int32), doc_lengths, q, kv_all, d_o_full, cos_t, sin_t
    )
    kv_part = scatter_bits(d_kv, strides, devices) + kv_grad_later[0]
    dk = kv_part[:, :head]
    cos_k, sin_k = cosine[:, :half_rot], sine[:, :half_rot]
    dk0, dk1 = dk[:, :half_rot], dk[:, half_rot:ROT]
    dm_kv = jnp.concatenate(
        [dk0 * cos_k + dk1 * sin_k, dk1 * cos_k - dk0 * sin_k, kv_part[:, ROT:]], axis=1
    ).astype(bf16)

    attended_other = swap_x(other_half(attended, 1, half))
    attended_half = jnp.concatenate([own_half(attended, 1, half), attended_other], axis=0)
    mixed = ff + mm(attended_half, out_weight)
    summed = mixed[:tokens] + swap_x(mixed[tokens:].astype(bf16)).astype(f32)
    result = (own_float + summed + bias_out + bias_down).astype(bf16)

    first_half = jnp.concatenate([own_half(first_own, 1, half), own_half(first_other, 1, half)], axis=0)
    dm_q_all = jnp.concatenate([dm_q, swap_x(dm_q)], axis=0)
    g_out = mm(attended_half, dy, TN)
    g_q = mm(first_half, dm_q_all, TN)
    pair = jnp.concatenate([g_q, g_out], axis=1)
    pair_part = scatter_bits(pair, strides, devices).astype(bf16)
    pair_all = gather_bits(pair_part, strides[::-1], devices).astype(f32)

    dm_kv_all = jnp.concatenate([dm_kv, swap_x(dm_kv)], axis=0)
    g_kv = mm(first_half, dm_kv_all, TN)

    d_first = mm(dm_q, w_q, NT) + mm(dm_kv, w_kv, NT)
    grad_inputs = dy_own.astype(f32) + norm_back(d_first, hat, root, gain1) + norm_back(d_second_own, hat, root, gain2)
    norms = jnp.stack(
        [
            jnp.sum(d_first * hat, axis=0),
            jnp.sum(d_first, axis=0),
            jnp.sum(d_second_own * hat, axis=0),
            jnp.sum(d_second_own, axis=0),
        ]
    )
    norms = own_half(norms, 1, half) + swap_x(other_half(norms, 1, half))
    g_dy = jnp.sum(own_half(dy, 1, half).astype(f32), axis=0)
    g_qkv_bias = jnp.concatenate(
        [jnp.sum(dm_q_all.astype(f32), axis=0), jnp.sum(dm_kv_all.astype(f32), axis=0)]
    )
    g_qkv_bias = own_half(g_qkv_bias, 0, g_qkv_bias.shape[0] // 2)
    small = jnp.concatenate([norms.reshape(-1), g_dy, g_qkv_bias, g_up_bias])
    count = small.shape[0]
    small = jnp.pad(small, (0, -count % 1024)).reshape(-1, 128)
    tail = jnp.concatenate([g_kv, small], axis=0)
    for stride in strides:
        tail = tail + swap_ctx(tail, stride, devices)
    g_kv = tail[:half]
    small = tail[half:].reshape(-1)
    norm_grads = [small[i * half : (i + 1) * half] for i in range(4)]
    at = 4 * half
    g_dy = small[at : at + half]
    at += half
    g_qkv_bias = small[at : at + qkv_bias.shape[0]]
    at += qkv_bias.shape[0]
    g_up_bias = small[at : at + wide]
    g_qkv = jnp.concatenate([pair_all[:, :width], g_kv], axis=1)
    return (
        result[None],
        grad_inputs[None],
        *norm_grads,
        g_qkv,
        g_qkv_bias,
        pair_all[:, width:],
        g_dy,
        g_up_all,
        g_up_bias,
        g_down_all,
        g_dy,
    )


def solution(mesh):
    token = P("fsdp", "ctx", None)
    vec = P("fsdp")
    mat = P("fsdp", None)
    return jax.shard_map(
        body,
        mesh=mesh,
        in_specs=(token, mat, vec, vec, vec, vec, mat, vec, mat, vec, mat, vec, mat, vec, token, token),
        out_specs=(token, token, vec, vec, vec, vec, mat, vec, mat, vec, mat, vec, mat, vec),
        check_vma=False,
    )
```

```python
from functools import partial

import jax
import jax.numpy as jnp
import numpy as np
from jax import lax
from jax.experimental import pallas as pl
from jax.experimental.pallas import tpu as pltpu
from jax.sharding import PartitionSpec as P

ROT = 16
BLOCK = 128
LOW = 16
NT = (((1,), (1,)), ((), ()))
NN = (((1,), (0,)), ((), ()))
TN = (((0,), (0,)), ((), ()))
bf16 = jnp.bfloat16
f32 = jnp.float32
TINY = pl.CostEstimate(flops=1, transcendentals=0, bytes_accessed=1)


def mm(left, right, dims=NN):
    return lax.dot_general(left, right, dims, preferred_element_type=f32)


def vmem():
    return pl.BlockSpec(memory_space=pltpu.VMEM)


def smem():
    return pl.BlockSpec(memory_space=pltpu.SMEM)


class Near:
    def __init__(self, value):
        self.value = value


class Raw(Near):
    pass


def near(*values):
    return tuple(Near(v) for v in values)


def call(kernel, name, outs, args, scratch=(), room=2):
    specs = [vmem() for _ in args]
    values = list(args)
    for i, v in enumerate(args):
        if isinstance(v, Raw):
            values[i] = v.value
            specs[i] = pl.BlockSpec(memory_space=pl.ANY)
        elif isinstance(v, Near):
            values[i] = pltpu.with_memory_space_constraint(v.value, pltpu.VMEM)
        elif v.dtype == jnp.int32:
            specs[i] = smem()
    return pl.pallas_call(
        kernel,
        out_shape=tuple(pltpu.VMEM(s, d) if n else jax.ShapeDtypeStruct(s, d) for s, d, n in outs),
        in_specs=specs,
        out_specs=tuple(vmem() for _ in outs),
        scratch_shapes=list(scratch),
        name=name,
        cost_estimate=TINY,
        compiler_params=pltpu.CompilerParams(vmem_limit_bytes=room << 20),
    )(*values)


def lanes(start, size):
    return pl.ds(pl.multiple_of(start, 128), size)


def swap_x(value):
    return lax.ppermute(value, "fsdp", [(0, 1), (1, 0)])


def swap_ctx(value, mask):
    devices = lax.axis_size("ctx")
    return lax.ppermute(value, "ctx", [(i, i ^ mask) for i in range(devices)])


def stages_of(devices):
    out, stride = [], 1
    while stride < devices:
        out.append((stride, 2))
        stride *= 2
    return out[::-1]


CHUNKS = [int(f"{k:03b}"[::-1], 2) for k in range(8)]


def slot_of(relative, stages):
    slot, count = relative * 0, 1
    for stride, size in stages:
        slot = slot + relative // stride % size * count
        count *= size
    return slot


def join_kernel(*refs):
    out = refs[-1]
    rows = refs[0].shape[0]
    for k, ref in enumerate(refs[:-1]):
        out[k * rows : (k + 1) * rows] = ref[...]


def join(first, second, name):
    shape = (2 * first.shape[0],) + first.shape[1:]
    return call(join_kernel, name, [(shape, first.dtype, True)], near(first, second))[0]


def gather_step(value, mask, name):
    return join(value, swap_ctx(value, mask), name)


def after(value, *others):
    return lax.optimization_barrier((value, *others))[0]


def add_split_kernel(a_ref, b_ref, keep, send):
    half = a_ref.shape[0] // 2
    for ref, part in ((keep, slice(0, half)), (send, slice(half, 2 * half))):
        ref[...] = (a_ref[part].astype(f32) + b_ref[part].astype(f32)).astype(ref.dtype)


def scatter_step(keep, send, mask, name):
    shape = (keep.shape[0] // 2,) + keep.shape[1:]
    out = (shape, keep.dtype, True)
    return call(add_split_kernel, name, [out, out], near(keep, swap_ctx(send, mask)))


def scatter(keep, send, devices, name, stride=1):
    while 2 * stride < devices:
        keep, send = scatter_step(keep, send, stride, name)
        stride *= 2
    return keep, swap_ctx(send, stride)


def high_sum(value):
    devices = lax.axis_size("ctx")
    if devices <= LOW:
        return value
    groups = [[h * LOW + l for h in range(devices // LOW)] for l in range(LOW)]
    return lax.psum(value, "ctx", axis_index_groups=groups)


def pack_kernel(ids, kv_w, q_w, up_w, g1, b1, g2, b2, ob, db, qb, small, q_out, up_out):
    small[:384, :] = kv_w[...]
    small[384:, :] = jnp.zeros((32, 128), bf16)
    row = 384
    for ref in (g1, b1, g2, b2, ob, db):
        v = ref[...].astype(f32).reshape(1, 384)
        for k in range(3):
            small[row : row + 1, :] = v[:, k * 128 : (k + 1) * 128].astype(bf16)
            row += 1
    v = qb[...].astype(f32).reshape(1, 448)
    for k in range(3):
        small[row + k : row + k + 1, :] = v[:, k * 128 : (k + 1) * 128].astype(bf16)
        small[row + 5 + k : row + 6 + k, :] = v[:, 64 + k * 128 : 64 + (k + 1) * 128].astype(bf16)
    small[row + 3 : row + 4, 0:64] = v[:, 384:448].astype(bf16)
    small[row + 4 : row + 5, 64:128] = v[:, 0:64].astype(bf16)
    q_out[...] = q_w[...]
    up_out[...] = up_w[...]


def pack(ids, qkv_weight, up_weight, vectors):
    half, width = qkv_weight.shape[0], 2 * qkv_weight.shape[0]
    wide = up_weight.shape[1] // 2
    whole = [pl.BlockSpec(v.shape, lambda i, s: (0,)) for v in vectors]
    outs = ((half + 32, 128), (half, width // 2), (half, wide // 4))
    return pl.pallas_call(
        pack_kernel,
        out_shape=tuple(jax.ShapeDtypeStruct(s, bf16) for s in outs),
        grid_spec=pltpu.PrefetchScalarGridSpec(
            num_scalar_prefetch=1,
            grid=(1,),
            in_specs=[
                pl.BlockSpec((half, 128), lambda i, s: (0, width // 128)),
                pl.BlockSpec((half, width // 2), lambda i, s: (0, s[2])),
                pl.BlockSpec((half, wide // 4), lambda i, s: (0, (1 - s[1]) * 4 + s[2] * 2 + s[3])),
            ]
            + whole,
            out_specs=[pl.BlockSpec(s, lambda i, s: (0, 0)) for s in outs],
        ),
        name="pack",
        cost_estimate=TINY,
    )(ids, qkv_weight, qkv_weight, up_weight, *vectors)


def row_vector(block, first, count=3):
    return jnp.concatenate([block[first + k : first + k + 1] for k in range(count)], axis=1)


def natural(side, own, other):
    return jnp.concatenate(
        [jnp.where(side == 0, own, other), jnp.where(side == 0, other, own)], axis=1
    )


def model_vector(side, own, other, index):
    return natural(side, row_vector(own, 3 * index), row_vector(other, 3 * index))


def qkv_bias_tiles(side, own, other):
    low = jnp.where(side == 0, own[18:22], other[18:22])
    high = jnp.where(side == 0, other[22:26], own[22:26])
    tiles = [low[0:1], low[1:2], low[2:3], low[3:4] + high[0:1], high[1:2], high[2:3], high[3:4]]
    return tiles


def normalize(values):
    centred = values - jnp.mean(values, axis=-1, keepdims=True)
    root = lax.rsqrt(jnp.mean(centred * centred, axis=-1, keepdims=True) + 1e-05)
    return centred * root, root


def turn(m, c, s1, s2):
    return m * c + pltpu.roll(m, 120, 1) * s1 + pltpu.roll(m, 8, 1) * s2


def kv_tables(c, s1, s2):
    key = lax.broadcasted_iota(jnp.int32, c.shape, 1) < 64
    return jnp.where(key, c, 1.0), jnp.where(key, s1, 0.0), jnp.where(key, s2, 0.0)


def front_kernel(ids, x, p_own, p_oth, c, s1, s2, first, kv, p_copy):
    p_copy[...] = p_oth[...]
    side = ids[1]
    half = x.shape[1] // 2
    own, other = p_own[half:].astype(f32), p_oth[half:].astype(f32)
    hat, _ = normalize(x[...].astype(f32))
    first[...] = (hat * model_vector(side, own, other, 0) + model_vector(side, own, other, 1)).astype(bf16)
    m = mm(first[:, lanes(side * half, half)], p_own[:half])
    m += mm(first[:, lanes((1 - side) * half, half)], p_oth[:half])
    m += qkv_bias_tiles(side, own, other)[6]
    kv[...] = turn(m, *kv_tables(c[...], s1[...], s2[...])).astype(bf16)


def query_kernel(ids, first, w, w_mine, w_theirs, p_own, p_oth, c, s1, s2, q, mine_copy, theirs_copy, bias):
    mine_copy[...] = w_mine[...]
    theirs_copy[...] = w_theirs[...]
    side, core = ids[1], ids[2]
    half = first.shape[1] // 2
    tiles = qkv_bias_tiles(side, p_own[half:].astype(f32), p_oth[half:].astype(f32))
    bias[...] = jnp.concatenate(tiles[:6], axis=1)
    for ref, cb in ((w_mine, core), (w_theirs, 1 - core)):
        col = cb * half
        m = mm(first[:, lanes(side * half, half)], w[:, lanes(col, half)])
        m += mm(first[:, lanes((1 - side) * half, half)], ref[...])
        m += bias[:, lanes(col, half)]
        for k in range(half // 128):
            low = turn(m[:, k * 128 : (k + 1) * 128], c[...], s1[...], s2[...]).astype(bf16)
            q[:, lanes(col + k * 128, 128)] = (low.astype(f32) * 0.125).astype(bf16)


def cotangent_kernel(dy_own, dy_oth, w, g_own, g_oth):
    g_own[...] = mm(dy_own[...], w[...], NT).astype(bf16)
    g_oth[...] = mm(dy_oth[...], w[...], NT).astype(bf16)


def ff_kernel(
    ids, x_own, x_oth, dy_own, dy_oth, up, up0, up1, up2, up3, down, up_bias, p_own, p_oth,
    keep_a, send_a, keep_b, send_b, ff_own, ff_oth, ds_own, ds_oth, first_oth, hat_half, dy_copy, up_sum,
    n_mine, n_send,
    a2, dy, act, dh, bias, sums, g_down, g_up, up_buf, down_buf, up_sem, down_sem,
):
    side, core, near_y = ids[1], ids[2], ids[3]
    tokens, width = x_own.shape
    half = width // 2
    wide = act.shape[1]
    step = wide // 4
    pieces = [
        (ref, (jnp.bitwise_xor(core, a) * 2 + jnp.bitwise_xor(near_y, b)), a, b)
        for ref, a, b in ((up0, 0, 0), (up1, 0, 1), (up2, 1, 0), (up3, 1, 1))
    ]

    def up_copy(i, piece):
        at = lanes(side * wide + piece * step, step)
        return pltpu.make_async_copy(up.at[:, at], up_buf.at[i], up_sem.at[i])

    def down_copy(i, piece):
        at = pl.ds(pl.multiple_of(piece * step, step), step)
        return pltpu.make_async_copy(down.at[at, :], down_buf.at[i], down_sem.at[i])

    for i, (_, piece, _, _) in enumerate(pieces):
        up_copy(i, piece).start()
        down_copy(i, piece).start()
    own, other = p_own[half:].astype(f32), p_oth[half:].astype(f32)
    gain1, shift1 = model_vector(side, own, other, 0), model_vector(side, own, other, 1)
    gain2, shift2 = model_vector(side, own, other, 2), model_vector(side, own, other, 3)
    mine, theirs = lanes(side * half, half), lanes((1 - side) * half, half)
    hat_own, _ = normalize(x_own[...].astype(f32))
    a2[:tokens] = (hat_own * gain2 + shift2).astype(bf16)
    hat_oth, _ = normalize(x_oth[...].astype(f32))
    a2[tokens:] = (hat_oth * gain2 + shift2).astype(bf16)
    first_oth[...] = (hat_oth * gain1 + shift1).astype(bf16)
    hat_half[...] = jnp.where(side == 0, hat_oth[:, :half], hat_oth[:, half:])
    dy[:tokens] = dy_own[...]
    dy[tokens:] = dy_oth[...]
    dy_copy[...] = dy_oth[...]
    bias[...] = up_bias[...].astype(f32).reshape(1, wide)
    rows = half // 4
    far = ids[0] // 4 % 4
    for i, (ref, piece, a, b) in enumerate(pieces):
        up_copy(i, piece).wait()
        down_copy(i, piece).wait()
        cols = lanes(piece * step, step)
        h = mm(a2[:, mine], up_buf[i])
        h += mm(a2[:, theirs], ref[...])
        h += bias[:, cols]
        phi = 0.5 * (1.0 + lax.erf(h * 0.7071067811865476))
        slope = phi + h * jnp.exp(-0.5 * h * h) * 0.3989422804014327
        g = (h * phi).astype(bf16)
        act[:, i * step : (i + 1) * step] = g
        d = mm(dy[...], down_buf[i], NT)
        e = (d * slope).astype(bf16)
        dh[:, i * step : (i + 1) * step] = e
        up_sum[:, cols] = jnp.sum(e.astype(f32), axis=0, keepdims=True)
        g_down[...] = mm(g, dy[...], TN).astype(bf16)
        g_up[:, :half] = mm(a2[:, mine], e, TN).astype(bf16)
        g_up[:, half:] = mm(a2[:, theirs], e, TN).astype(bf16)
        for k in range(4):
            z = jnp.bitwise_xor(far, (k & 1) * 2 + (k >> 1))
            at = pl.ds(pl.multiple_of(z * rows, rows), rows)
            slot = b * 4 + k
            (send_a if a else keep_a)[slot] = g_down[at, :]
            (send_b if a else keep_b)[slot] = g_up[at, :]
    out = sum(mm(act[:, i * step : (i + 1) * step], down_buf[i]) for i in range(4))
    ff_own[...] = out[:tokens]
    ff_oth[...] = out[tokens:]
    ds_mine = sum(mm(dh[:, i * step : (i + 1) * step], up_buf[i], NT) for i in range(4))
    ds_theirs = sum(mm(dh[:, i * step : (i + 1) * step], ref[...], NT) for i, (ref, _, _, _) in enumerate(pieces))
    low = jnp.where(side == 0, ds_mine, ds_theirs)
    high = jnp.where(side == 0, ds_theirs, ds_mine)
    for part, ds in ((slice(0, half), low), (slice(half, width), high)):
        ds_own[:, part] = ds[:tokens]
        ds_oth[:, part] = ds[tokens:].astype(bf16)
        moved = ds[:tokens] * hat_own[:, part] + ds[tokens:] * hat_oth[:, part]
        sums[0:1, part] = jnp.sum(moved, axis=0, keepdims=True)
        sums[1:2, part] = jnp.sum(ds, axis=0, keepdims=True)
    split_rows(sums, 2, side, half, n_mine, n_send)


def split_rows(sums, count, side, half, mine, send):
    for ref, owner in ((mine, side), (send, 1 - side)):
        ref[...] = jnp.zeros_like(ref)
        for i in range(count):
            for k in range(half // 128):
                at = i * (half // 128) + k
                ref[at : at + 1, :] = sums[i : i + 1, lanes(owner * half + k * 128, 128)]


def attn_kernel(
    stages, n_dev, docs, ids, len_ref, q_ref, kv_mine, kv_theirs, g_own, g_oth, cos_ref, sin_ref,
    o_own, o_oth, dm_ref, dkv_keep, dkv_send, kv_ref, qz, gz, ot, dqt, st, bias, ds_sc, p_sc, acc,
):
    b = BLOCK
    kb = 2 * b
    width = q_ref.shape[1]
    half = width // 2
    pairs = width // 128
    me, fsdp = ids[0], ids[1]
    low = lax.broadcasted_iota(jnp.int32, (b, 128), 1) < 64
    middle = kv_mine.shape[0]
    kv_ref[:middle] = kv_mine[...]
    kv_ref[middle:] = kv_theirs[...]
    acc[...] = jnp.zeros_like(acc)

    def row_of(j):
        j = jnp.maximum(j, 0)
        dev = jnp.where(j < n_dev, j, 2 * n_dev - 1 - j)
        slot = slot_of(jnp.bitwise_xor(dev, me), stages)
        return (slot * 2 + jnp.where(j < n_dev, 0, 1)) * b

    def half_turn(two):
        return pltpu.roll(two.astype(f32), 64, 1).astype(bf16)

    def pair_at(p):
        near = p < pairs // 2
        local = (p % (pairs // 2)) * 128
        col = (fsdp if near else 1 - fsdp) * half + local
        return (g_own if near else g_oth), (o_own if near else o_oth), local, lanes(col, 128)

    def side_step(side, carry):
        block = jnp.where(side == 0, me, 2 * n_dev - 1 - me)
        base = block * b
        rows = pl.ds(pl.multiple_of(side * b, b), b)
        qpos = base + lax.broadcasted_iota(jnp.int32, (1, b), 1)
        total = jnp.int32(0)
        qstart = jnp.zeros((1, b), jnp.int32)
        first = jnp.int32(0)
        for e in range(docs):
            size = len_ref[0, e]
            total = total + size
            qstart = qstart + jnp.where(total <= qpos, size, 0)
            first = first + jnp.where(total <= base, size, 0)
        steps = (base + b - first + kb - 1) // kb
        for p in range(pairs):
            g_ref, _, local, cols = pair_at(p)
            two = q_ref[rows, cols]
            zero = jnp.zeros_like(two)
            qz[pl.ds(p * 256, 128), :] = jnp.where(low, two, zero)
            qz[pl.ds(p * 256 + 128, 128), :] = jnp.where(low, half_turn(two), zero)
            two = g_ref[rows, pl.ds(local, 128)]
            gz[pl.ds(p * 256, 128), :] = jnp.where(low, zero, half_turn(two))
            gz[pl.ds(p * 256 + 128, 128), :] = jnp.where(low, zero, two)
        ot[...] = jnp.zeros_like(ot)
        dqt[...] = jnp.zeros_like(dqt)
        st[0] = jnp.full(st.shape[1:], -1e30, f32)
        st[1] = jnp.zeros(st.shape[1:], f32)

        def load(t):
            hi = block - 2 * t
            r1 = pl.multiple_of(row_of(hi), b)
            r0 = pl.multiple_of(row_of(hi - 1), b)
            kvb = jnp.concatenate([kv_ref[pl.ds(r0, b), :], kv_ref[pl.ds(r1, b), :]], axis=0)
            kpos = (hi - 1) * b + lax.broadcasted_iota(jnp.int32, (kb, b), 0)
            ok = (kpos <= qpos) & (kpos >= qstart)
            bias[...] = jnp.where(ok, 0.0, -1e30)
            return kvb, r0, r1

        def forward(t, carry):
            kvb, _, _ = load(t)
            vt = kvb.astype(f32).T.astype(bf16)[64:]
            mask = bias[...]
            for p in range(pairs):
                s2 = mm(kvb, qz[pl.ds(p * 256, 256), :], NT)
                for i in range(2):
                    h = 2 * p + i
                    s = s2[:, i * 128 : (i + 1) * 128] + mask
                    old = st[0, h : h + 1, :]
                    new = jnp.maximum(old, jnp.max(s, axis=0, keepdims=True))
                    e = jnp.exp(s - new)
                    alpha = jnp.exp(old - new)
                    st[0, h : h + 1, :] = new
                    st[1, h : h + 1, :] = st[1, h : h + 1, :] * alpha + jnp.sum(e, axis=0, keepdims=True)
                    hs = pl.ds(h * 64, 64)
                    ot[hs, :] = ot[hs, :] * alpha + mm(vt, e.astype(bf16))
            return 0

        lax.fori_loop(0, steps, forward, 0)

        for p in range(pairs):
            g_ref, o_ref, local, _ = pair_at(p)
            gt = g_ref[rows, pl.ds(local, 128)].astype(f32).T
            halves = []
            for i in range(2):
                h = 2 * p + i
                l = st[1, h : h + 1, :]
                o = ot[pl.ds(h * 64, 64), :] / l
                halves.append(o)
                st[2, h : h + 1, :] = jnp.sum(o * gt[i * 64 : (i + 1) * 64], axis=0, keepdims=True)
                st[0, h : h + 1, :] = st[0, h : h + 1, :] + jnp.log(l)
            o_ref[rows, pl.ds(local, 128)] = jnp.concatenate(halves, axis=0).T.astype(bf16)

        def backward(t, carry):
            kvb, r0, r1 = load(t)
            kt = kvb.astype(f32).T.astype(bf16)[:64]
            mask = bias[...]
            for p in range(pairs):
                s2 = mm(kvb, qz[pl.ds(p * 256, 256), :], NT)
                dp2 = mm(kvb, gz[pl.ds(p * 256, 256), :], NT)
                for i in range(2):
                    h = 2 * p + i
                    sl = slice(i * 128, (i + 1) * 128)
                    pr = jnp.exp((s2[:, sl] + mask) - st[0, h : h + 1, :])
                    ds = pr * (dp2[:, sl] - st[2, h : h + 1, :])
                    ds_sc[:, h * 128 : (h + 1) * 128] = ds.astype(bf16)
                    p_sc[:, h * 128 : (h + 1) * 128] = pr.astype(bf16)
            part = mm(ds_sc[...], qz[...]) + mm(p_sc[...], gz[...])
            acc[pl.ds(r0, b), :] += part[:b]
            acc[pl.ds(r1, b), :] += part[b:]
            dqt[...] += mm(kt, ds_sc[...])
            return 0

        lax.fori_loop(0, steps, backward, 0)

        cos = cos_ref[side]
        sin = sin_ref[side]
        for p in range(pairs):
            halves = []
            for i in range(2):
                h = 2 * p + i
                g = dqt[:, h * 128 : (h + 1) * 128] * 0.125
                g0, g1 = g[:8], g[8:16]
                halves += [g0 * cos + g1 * sin, g1 * cos - g0 * sin, g[16:]]
            dm_ref[rows, pair_at(p)[3]] = jnp.concatenate(halves, axis=0).T.astype(bf16)
        return 0

    lax.fori_loop(0, 2, side_step, 0)
    dkv_keep[...] = acc[:middle].astype(bf16)
    dkv_send[...] = acc[middle:].astype(bf16)


def attention(stages, n_dev, ids, lengths, q, kv_mine, kv_theirs, g_own, g_oth, cos, sin):
    tokens, width = q.shape
    middle = kv_mine.shape[0]
    rows = width // 64 * 128
    small = n_dev <= LOW
    kv_args = near(kv_mine, kv_theirs) if small else (kv_mine, kv_theirs)
    return call(
        partial(attn_kernel, stages, n_dev, lengths.shape[1]),
        "attn",
        [
            ((tokens, width // 2), bf16, False),
            ((tokens, width // 2), bf16, True),
            ((tokens, width), bf16, True),
            ((middle, 128), bf16, small),
            ((middle, 128), bf16, small),
        ],
        (ids, lengths, *near(q), *kv_args, g_own, *near(g_oth), cos, sin),
        scratch=[
            pltpu.VMEM((2 * middle, 128), bf16),
            pltpu.VMEM((rows, 128), bf16),
            pltpu.VMEM((rows, 128), bf16),
            pltpu.VMEM((width, 128), f32),
            pltpu.VMEM((64, rows), f32),
            pltpu.VMEM((3, 16, 128), f32),
            pltpu.VMEM((256, 128), f32),
            pltpu.VMEM((256, rows), bf16),
            pltpu.VMEM((256, rows), bf16),
            pltpu.VMEM((2 * middle, 128), f32),
        ],
        room=8 + 2 * middle * 128 * (6 if small else 10) // 2**20,
    )


def mix_kernel(ff, o, w, out):
    out[...] = (ff[...] + mm(o[...], w[...])).astype(bf16)


def result_kernel(ids, x, ff, o, w, recv, p_own, p_oth, out):
    side = ids[1]
    half = x.shape[1] // 2
    own, other = p_own[half:].astype(f32), p_oth[half:].astype(f32)
    y = x[...].astype(f32) + (ff[...] + mm(o[...], w[...])) + recv[...].astype(f32)
    y += model_vector(side, own, other, 4) + model_vector(side, own, other, 5)
    out[...] = y.astype(bf16)


def dm_kv_kernel(*refs):
    later, c, s1, s2, out = refs[-5:]
    total = later[...]
    for ref in refs[:-5]:
        total = total + ref[...].astype(f32)
    c, s1, s2 = kv_tables(c[...], s1[...], s2[...])
    out[...] = turn(total, c, -s1, -s2).astype(bf16)


def x_grad_kernel(ids, x, dy, dm, dm_kv, w, w_mine, w_theirs, p_own, p_oth, ds, ds_recv, out, da):
    side, core = ids[1], ids[2]
    width = x.shape[1]
    half = width // 2
    own, other = p_own[half:].astype(f32), p_oth[half:].astype(f32)
    mine, theirs = lanes(side * half, half), lanes((1 - side) * half, half)
    da[:, mine] = mm(dm[...], w[:, :width], NT) + mm(dm_kv[...], p_own[:half], NT)
    da[:, theirs] = (
        mm(dm[:, lanes(core * half, half)], w_mine[...], NT)
        + mm(dm[:, lanes((1 - core) * half, half)], w_theirs[...], NT)
        + mm(dm_kv[...], p_oth[:half], NT)
    )
    hat, root = normalize(x[...].astype(f32))
    total = dy[...].astype(f32)
    for i, grad in enumerate((da[...], ds[...] + ds_recv[...].astype(f32))):
        up = grad * model_vector(side, own, other, 2 * i)
        total += root * (
            up - jnp.mean(up, axis=-1, keepdims=True) - hat * jnp.mean(up * hat, axis=-1, keepdims=True)
        )
    out[...] = total


def pair_kernel(
    ids, f_own, f_oth, dm_own, dm_oth, o_own, o_oth, dy_own, dy_oth, kv_own, kv_oth, n_mine, n_recv, up_sum,
    x_own, hat_half, w, p_own, keep, send, gq, go, tail, hat,
):
    side, core = ids[1], ids[2]
    half = f_own.shape[1] // 2
    mine = lanes(side * half, half)
    gq[...] = mm(f_own[:, mine], dm_own[...], TN) + mm(f_oth[:, mine], dm_oth[...], TN)
    go[...] = mm(o_own[...], dy_own[...], TN) + mm(o_oth[...], dy_oth[...], TN)
    tail[:half] = mm(f_own[:, mine], kv_own[...], TN) + mm(f_oth[:, mine], kv_oth[...], TN)
    tail[half:] = jnp.zeros((128, 128), f32)
    gain = shift = 0.0
    hat[...] = normalize(x_own[...].astype(f32))[0]
    for x, dm, kv in ((hat[:, mine], dm_own, kv_own), (hat_half[...], dm_oth, kv_oth)):
        grad = mm(dm[...], w[:, : 2 * half], NT) + mm(kv[...], p_own[:half], NT)
        gain += jnp.sum(grad * x, axis=0, keepdims=True)
        shift += jnp.sum(grad, axis=0, keepdims=True)
    row = half
    for v in (gain, shift):
        for k in range(3):
            tail[row + k : row + k + 1, :] = v[:, k * 128 : (k + 1) * 128]
        row += 3
    v = n_mine[...] + n_recv[...]
    tail[row : row + 6] = v[:6]
    row += 6

    def total(a, b):
        return jnp.sum(a.astype(f32), axis=0, keepdims=True) + jnp.sum(b.astype(f32), axis=0, keepdims=True)

    v = total(dy_own[:, mine], dy_oth[:, mine])
    for k in range(3):
        tail[row + k : row + k + 1, :] = v[:, k * 128 : (k + 1) * 128]
    row += 3
    v = jnp.concatenate([total(dm_own[...], dm_oth[...]), total(kv_own[...], kv_oth[...])], axis=1)
    moved = jnp.concatenate([v[:, 448:], v[:, :448]], axis=1)
    v = jnp.where(side == 0, v, moved)
    for k in range(4):
        tail[row + k : row + k + 1, :] = v[:, k * 128 : (k + 1) * 128]
    row += 4
    for k in range(12):
        tail[row + k : row + k + 1, :] = up_sum[:, k * 128 : (k + 1) * 128]
    rows = half // 8
    near = ids[0] % LOW
    for ref, cb in ((keep, core), (send, 1 - core)):
        cols = lanes(cb * half, half)
        for k in range(8):
            at = pl.ds(pl.multiple_of(jnp.bitwise_xor(near // 2, CHUNKS[k]) * rows, rows), rows)
            base = k * (rows + 16)
            ref[base : base + rows, 0:half] = gq[at, cols].astype(bf16)
            ref[base : base + rows, half:] = go[at, cols].astype(bf16)
            chunk = jnp.bitwise_xor(near // 2, CHUNKS[k]) * 2 + cb
            for j in range(2):
                at = pl.ds(pl.multiple_of(chunk * 32 + j * 16, 16), 16)
                ref[base + rows : base + rows + 16, j * 128 : (j + 1) * 128] = tail[at, :].astype(bf16)
            ref[base + rows : base + rows + 16, 256:] = jnp.zeros((16, 2 * half - 256), bf16)


def sum_kernel(*refs):
    total = refs[0][...].astype(f32)
    for ref in refs[1:-1]:
        total = total + ref[...].astype(f32)
    refs[-1][...] = total.astype(refs[-1].dtype)


def sum_of(first, second, name):
    return call(sum_kernel, name, [(first.shape, first.dtype, True)], near(first, second))[0]


def up_part_kernel(a, b, own, other):
    half = own.shape[-1]
    total = a[...].astype(f32) + b[...].astype(f32)
    own[...] = total[..., :half].astype(bf16)
    other[...] = total[..., half:].astype(bf16)


def up_join_kernel(own, other, out):
    half = own.shape[-1]
    out[..., :half] = own[...]
    out[..., half:] = other[...]


def chunk_of(ids, other_core, slot):
    core, near_y, far = ids[2], ids[3], ids[0] // 4 % 4
    piece = jnp.bitwise_xor(core, other_core) * 2 + jnp.bitwise_xor(near_y, slot >> 2)
    return piece, jnp.bitwise_xor(far, (slot & 1) * 2 + (slot >> 1 & 1))


def down_out_kernel(ids, mine, theirs, out):
    rows = mine.shape[1]
    for a, ref in enumerate((mine, theirs)):
        for k in range(8):
            piece, z = chunk_of(ids, a, k)
            out[pl.ds(pl.multiple_of((piece * 4 + z) * rows, rows), rows), :] = ref[k].astype(f32)


def up_out_kernel(ids, mine, theirs, out):
    side = ids[1]
    rows = mine.shape[1]
    half = mine.shape[2] // 2
    wide = out.shape[1] // 2
    for a, ref in enumerate((mine, theirs)):
        for k in range(8):
            piece, z = chunk_of(ids, a, k)
            at = pl.ds(pl.multiple_of(z * rows, rows), rows)
            for j, owner in ((0, side), (1, 1 - side)):
                part = ref[k, :, j * half : (j + 1) * half].astype(f32)
                out[at, lanes(owner * wide + piece * half, half)] = part


def attn_out_kernel(ids, p_mine, p_theirs, g_qkv, g_out, n0, n1, n2, n3, qb, ob, ub, db, tail):
    core = ids[2]
    near = ids[0] % LOW
    half = g_qkv.shape[0]
    rows = half // 8
    for ref, cb in ((p_mine, core), (p_theirs, 1 - core)):
        cols = lanes(cb * half, half)
        for k in range(8):
            at = pl.ds(pl.multiple_of(jnp.bitwise_xor(near // 2, CHUNKS[k]) * rows, rows), rows)
            base = k * (rows + 16)
            part = ref[base : base + rows, :].astype(f32)
            g_qkv[at, cols] = part[:, :half]
            g_out[at, cols] = part[:, half:]
            chunk = jnp.bitwise_xor(near // 2, CHUNKS[k]) * 2 + cb
            for j in range(2):
                at = pl.ds(pl.multiple_of(chunk * 32 + j * 16, 16), 16)
                tail[at, :] = ref[base + rows : base + rows + 16, j * 128 : (j + 1) * 128].astype(f32)
    g_qkv[:, 2 * half :] = tail[:half]
    small = tail[half : half + 32]
    for i, ref in enumerate((n0, n1, n2, n3, ob)):
        ref[...] = row_vector(small, 3 * i).reshape(half)
    db[...] = row_vector(small, 12).reshape(half)
    qb[...] = row_vector(small, 15, 4)[:, : qb.shape[0]].reshape(qb.shape[0])
    ub[...] = row_vector(small, 19, 12).reshape(ub.shape[0])


def body(
    layer_input, doc_lengths, ln1_gain, ln1_bias, ln2_gain, ln2_bias, qkv_weight, qkv_bias,
    out_weight, out_bias, up_weight, up_bias, down_weight, down_bias, out_grad, kv_grad_later,
):
    devices = lax.axis_size("ctx")
    me = lax.axis_index("ctx").astype(jnp.int32)
    side = lax.axis_index("fsdp").astype(jnp.int32)
    ids = jnp.stack([me, side, me % 2, me // 2 % 2])
    tokens, width = layer_input.shape[1:]
    half_rows = tokens // 2
    half = width // 2
    wide = up_weight.shape[1] // 2
    stages = stages_of(devices)
    x_own, dy_own = layer_input[0], out_grad[0]

    vectors = (ln1_gain, ln1_bias, ln2_gain, ln2_bias, out_bias, down_bias, qkv_bias)
    p_own, q_send, up_send = pack(ids, qkv_weight, up_weight, vectors)
    p_oth = swap_x(p_own)
    x_oth = swap_x(x_own)
    ups = [swap_x(after(up_send, p_oth))]
    ups += [swap_ctx(ups[0], mask) for mask in (2, 1)]
    ups += [swap_ctx(ups[1], 1)]
    dy_oth = swap_x(after(dy_own, p_oth))
    q_mine = swap_x(after(q_send, x_oth))
    q_theirs = swap_ctx(q_mine, 1)

    offsets = jnp.arange(half_rows, dtype=jnp.int32)
    places = jnp.concatenate([me * half_rows + offsets, (2 * devices - 1 - me) * half_rows + offsets]).astype(f32)
    half_rot = ROT // 2
    freq = 10000.0 ** (-jnp.arange(half_rot, dtype=f32) / half_rot)
    lane = np.arange(128)
    angles = places[:, None] * jnp.tile(freq, 128 // half_rot)[None, :]
    cosine, sine = jnp.cos(angles), jnp.sin(angles)
    tables = (
        jnp.where(lane % 64 < 16, cosine, 1.0),
        jnp.where(lane % 64 < 8, -sine, 0.0),
        jnp.where((lane % 64 >= 8) & (lane % 64 < 16), sine, 0.0),
    )
    t_angles = places.reshape(2, 1, half_rows) * freq[None, :, None]
    cos_t, sin_t = jnp.cos(t_angles), jnp.sin(t_angles)

    first_own, kv, p_oth_far = call(
        front_kernel,
        "front",
        [((tokens, width), bf16, False), ((tokens, 128), bf16, True), (p_own.shape, bf16, False)],
        (ids, x_own, p_own, *near(p_oth), *tables),
    )
    for stride, _ in stages[:-2]:
        kv = gather_step(kv, stride, "kv_join")
    kv_mine = gather_step(kv, 2, "kv_join")
    kv_theirs = swap_ctx(kv_mine, 1)

    g_own, g_send = call(
        cotangent_kernel,
        "cotangent",
        [((tokens, half), bf16, False), ((tokens, half), bf16, True)],
        (dy_own, *near(dy_oth), out_weight),
    )
    g_oth = swap_x(g_send)

    rows = half // 4
    step = wide // 4
    chunks = ((8, rows, width), bf16, True)
    token_f32, token_low = ((tokens, width), f32, False), ((tokens, width), bf16, False)
    (
        keep_a, send_a, keep_b, send_b, ff_own, ff_oth, ds_own, ds_oth, first_oth, hat_half, dy_far, up_sum,
        n_mine, n_send,
    ) = call(
        ff_kernel,
        "ff",
        [
            chunks, chunks, chunks, chunks, token_f32, token_f32, token_f32, token_low, token_low,
            ((tokens, half), f32, False), token_low, ((1, wide), f32, False), ((8, 128), f32, False),
            ((8, 128), f32, False),
        ],
        (
            ids, x_own, *near(after(x_oth, kv)), dy_own, *near(dy_oth), Raw(up_weight), *near(*ups), Raw(down_weight),
            up_bias, p_own, p_oth_far,
        ),
        scratch=[
            pltpu.VMEM((2 * tokens, width), bf16),
            pltpu.VMEM((2 * tokens, width), bf16),
            pltpu.VMEM((2 * tokens, wide), bf16),
            pltpu.VMEM((2 * tokens, wide), bf16),
            pltpu.VMEM((1, wide), f32),
            pltpu.VMEM((8, width), f32),
            pltpu.VMEM((half, width), bf16),
            pltpu.VMEM((half, width), bf16),
            pltpu.VMEM((4, half, step), bf16),
            pltpu.VMEM((4, step, width), bf16),
            pltpu.SemaphoreType.DMA((4,)),
            pltpu.SemaphoreType.DMA((4,)),
        ],
        room=22,
    )
    n_recv = swap_x(n_send)
    ds_recv = swap_x(ds_oth)
    low = min(LOW, devices)
    keep_a, send_a = scatter_step(keep_a, send_a, 1, "down_add")
    keep_b, send_b = scatter_step(keep_b, send_b, 1, "up_add")
    down_part = high_sum(sum_of(*scatter(keep_a, send_a, low, "down_add", 2), "down_sum"))
    up_sum_parts = scatter(keep_b, send_b, low, "up_add", 2)
    up_own, up_send = call(
        up_part_kernel,
        "up_part",
        [((1, rows, half), bf16, True), ((1, rows, half), bf16, True)],
        near(*up_sum_parts),
    )
    up_own, up_send = high_sum(up_own), high_sum(up_send)
    up_part = call(up_join_kernel, "up_join", [((1, rows, width), bf16, True)], near(up_own, swap_x(up_send)))[0]

    q, q_mine_far, q_theirs_far = call(
        query_kernel,
        "query",
        [((tokens, width), bf16, True), ((half, half), bf16, False), ((half, half), bf16, False)],
        (ids, first_own, qkv_weight, *near(q_mine, q_theirs), p_own, p_oth_far, *tables),
        scratch=[pltpu.VMEM((1, width), f32)],
    )
    o_own, o_send, dm_own, dkv_keep, dkv_send = attention(
        stages, devices, ids, doc_lengths, after(q, send_a, send_b), kv_mine, kv_theirs, g_own, g_oth, cos_t, sin_t
    )
    kv_pieces = scatter(dkv_keep, dkv_send, devices, "kv_add")
    o_oth = swap_x(o_send)
    dm_oth = swap_x(dm_own)

    y_send = call(mix_kernel, "mix", [((tokens, width), bf16, True)], (ff_oth, *near(o_oth), out_weight))[0]
    y_recv = swap_x(y_send)
    result = call(
        result_kernel,
        "result",
        [((tokens, width), bf16, False)],
        (ids, x_own, ff_own, o_own, out_weight, *near(y_recv), p_own, p_oth_far),
    )[0]

    kv_pieces = (after(kv_pieces[0], ds_recv, n_recv), kv_pieces[1])
    dm_kv = call(
        dm_kv_kernel, "dm_kv", [((tokens, 128), bf16, True)], (*near(*kv_pieces), kv_grad_later[0], *tables)
    )[0]
    dm_kv_oth = swap_x(dm_kv)
    grad_inputs = call(
        x_grad_kernel,
        "x_grad",
        [((tokens, width), f32, False)],
        (
            ids, x_own, dy_own, *near(dm_own, dm_kv), qkv_weight, q_mine_far, q_theirs_far, p_own, p_oth_far, ds_own,
            *near(ds_recv),
        ),
        scratch=[pltpu.VMEM((tokens, width), f32)],
        room=8,
    )[0]
    size = half + 128
    keep, send = call(
        pair_kernel,
        "pair",
        [((size, width), bf16, True), ((size, width), bf16, True)],
        (
            ids, first_own, first_oth, *near(dm_own, dm_oth), o_own, *near(after(o_oth, y_send)), dy_own, dy_far,
            *near(dm_kv, dm_kv_oth), n_mine, *near(n_recv), up_sum, x_own, hat_half, qkv_weight, p_own,
        ),
        scratch=[
            pltpu.VMEM((half, width), f32),
            pltpu.VMEM((half, width), f32),
            pltpu.VMEM((size, 128), f32),
            pltpu.VMEM((tokens, width), f32),
        ],
        room=12,
    )
    pieces = scatter(keep, send, low, "pair_add")
    pair = high_sum(sum_of(after(pieces[0], result, grad_inputs), pieces[1], "pair_sum"))

    outs = []
    for value, name in ((down_part, "down_join"), (up_part, "up_join"), (pair, "pair_join")):
        for stride, _ in stages_of(low)[:-1]:
            value = gather_step(value, stride, name)
        outs.append(near(value, swap_ctx(value, 1)))
    g_down = call(down_out_kernel, "down_out", [((wide, width), f32, False)], (ids, *outs[0]), room=8)[0]
    g_up = call(up_out_kernel, "up_out", [((half, 2 * wide), f32, False)], (ids, *outs[1]), room=8)[0]
    vec = ((half,), f32, False)
    g_qkv, g_out, *small = call(
        attn_out_kernel,
        "attn_out",
        [
            ((half, width + 128), f32, False), ((half, width), f32, False), vec, vec, vec, vec,
            (qkv_bias.shape, f32, False), vec, (up_bias.shape, f32, False), vec,
        ],
        (ids, *outs[2]),
        scratch=[pltpu.VMEM((size, 128), f32)],
        room=6,
    )
    n0, n1, n2, n3, qb, ob, ub, db = small
    return (result[None], grad_inputs[None], n0, n1, n2, n3, g_qkv, qb, g_out, ob, g_up, ub, g_down, db)


def solution(mesh):
    token = P("fsdp", "ctx", None)
    vec = P("fsdp")
    mat = P("fsdp", None)
    return jax.shard_map(
        body,
        mesh=mesh,
        in_specs=(token, mat, vec, vec, vec, vec, mat, vec, mat, vec, mat, vec, mat, vec, token, token),
        out_specs=(token, token, vec, vec, vec, vec, mat, vec, mat, vec, mat, vec, mat, vec),
        check_vma=False,
    )
```

```python
from functools import partial

import jax
import jax.numpy as jnp
import numpy as np
from jax import lax
from jax.experimental import pallas as pl
from jax.experimental.pallas import tpu as pltpu
from jax.sharding import PartitionSpec as P

ROT = 16
BLOCK = 128
LOW = 16
NT = (((1,), (1,)), ((), ()))
NN = (((1,), (0,)), ((), ()))
TN = (((0,), (0,)), ((), ()))
bf16 = jnp.bfloat16
f32 = jnp.float32
WEIGHT = {'kv_add': 6.0, 'dm_kv': 0.0, 'tail': 3.0, 'tail_sum': 6.0, 'pair': 4.0, 'pair_add': 7.0, 'pair_sum': 7.0, 'pair_join': 7.0, 'both': 7.0, 'both_join': 7.0, 'down_join': 3.0, 'up_out': 0.0, 'up_join': 0.0, 'cotangent': 0.0, 'query': 6.0, 'ff': 0.0, 'attn_backward': 13.0, 'front': 13.0, 'attn_forward': 1.0, 'down_add': 0.0}
TINY = pl.CostEstimate(flops=1, transcendentals=0, bytes_accessed=1)


def mm(left, right, dims=NN):
    return lax.dot_general(left, right, dims, preferred_element_type=f32)


def vmem():
    return pl.BlockSpec(memory_space=pltpu.VMEM)


def smem():
    return pl.BlockSpec(memory_space=pltpu.SMEM)


class Near:
    def __init__(self, value):
        self.value = value


class Raw(Near):
    pass


def near(*values):
    return tuple(Near(v) for v in values)


def call(kernel, name, outs, args, scratch=(), room=2):
    specs = [vmem() for _ in args]
    values = list(args)
    for i, v in enumerate(args):
        if isinstance(v, Raw):
            values[i] = v.value
            specs[i] = pl.BlockSpec(memory_space=pl.ANY)
        elif isinstance(v, Near):
            values[i] = pltpu.with_memory_space_constraint(v.value, pltpu.VMEM)
        elif v.dtype == jnp.int32:
            specs[i] = smem()
    return pl.pallas_call(
        kernel,
        out_shape=tuple(pltpu.VMEM(s, d) if n else jax.ShapeDtypeStruct(s, d) for s, d, n in outs),
        in_specs=specs,
        out_specs=tuple(vmem() for _ in outs),
        scratch_shapes=list(scratch),
        name=name,
        cost_estimate=pl.CostEstimate(
            flops=int(WEIGHT.get(name, 0) * 1e9) + 1, transcendentals=0, bytes_accessed=1
        ),
        compiler_params=pltpu.CompilerParams(vmem_limit_bytes=room << 20),
    )(*values)


def lanes(start, size):
    return pl.ds(pl.multiple_of(start, 128), size)


def swap_x(value):
    return lax.ppermute(value, "fsdp", [(0, 1), (1, 0)])


def swap_ctx(value, mask):
    devices = lax.axis_size("ctx")
    return lax.ppermute(value, "ctx", [(i, i ^ mask) for i in range(devices)])


def stages_of(devices):
    out, stride = [], 1
    while stride < devices:
        out.append((stride, 2))
        stride *= 2
    return out[::-1]


CHUNKS = [int(f"{k:03b}"[::-1], 2) for k in range(8)]


def slot_of(relative, stages):
    slot, count = relative * 0, 1
    for stride, size in stages:
        slot = slot + relative // stride % size * count
        count *= size
    return slot


def join_kernel(*refs):
    out = refs[-1]
    rows = refs[0].shape[0]
    for k, ref in enumerate(refs[:-1]):
        out[k * rows : (k + 1) * rows] = ref[...]


def join(first, second, name):
    shape = (2 * first.shape[0],) + first.shape[1:]
    return call(join_kernel, name, [(shape, first.dtype, True)], near(first, second))[0]


def gather_step(value, mask, name):
    return join(value, swap_ctx(value, mask), name)


def after(value, *others):
    return lax.optimization_barrier((value, *others))[0]


def add_split_kernel(a_ref, b_ref, keep, send):
    half = a_ref.shape[0] // 2
    for ref, part in ((keep, slice(0, half)), (send, slice(half, 2 * half))):
        ref[...] = (a_ref[part].astype(f32) + b_ref[part].astype(f32)).astype(ref.dtype)


def scatter_step(keep, send, mask, name):
    shape = (keep.shape[0] // 2,) + keep.shape[1:]
    out = (shape, keep.dtype, True)
    return call(add_split_kernel, name, [out, out], near(keep, swap_ctx(send, mask)))


def scatter(keep, send, devices, name, stride=1):
    while 2 * stride < devices:
        keep, send = scatter_step(keep, send, stride, name)
        stride *= 2
    return keep, swap_ctx(send, stride)


def high_sum(value):
    devices = lax.axis_size("ctx")
    if devices <= LOW:
        return value
    groups = [[h * LOW + l for h in range(devices // LOW)] for l in range(LOW)]
    return lax.psum(value, "ctx", axis_index_groups=groups)


def pack_kernel(ids, x, dy, kv_w, q_w, up_w, g1, b1, g2, b2, ob, db, qb, small, first, second):
    small[:384, :] = kv_w[...]
    small[384:, :] = jnp.zeros((32, 128), bf16)
    row = 384
    for ref in (g1, b1, g2, b2, ob, db):
        v = ref[...].astype(f32).reshape(1, 384)
        for k in range(3):
            small[row : row + 1, :] = v[:, k * 128 : (k + 1) * 128].astype(bf16)
            row += 1
    v = qb[...].astype(f32).reshape(1, 448)
    for k in range(3):
        small[row + k : row + k + 1, :] = v[:, k * 128 : (k + 1) * 128].astype(bf16)
        small[row + 5 + k : row + 6 + k, :] = v[:, 64 + k * 128 : 64 + (k + 1) * 128].astype(bf16)
    small[row + 3 : row + 4, 0:64] = v[:, 384:448].astype(bf16)
    small[row + 4 : row + 5, 64:128] = v[:, 0:64].astype(bf16)
    first[:416, :] = small[...]
    for k in range(3):
        first[416 + 384 * k : 800 + 384 * k, :] = up_w[:, k * 128 : (k + 1) * 128]
    tokens = x.shape[0]
    second[:tokens] = x[...]
    second[tokens : 2 * tokens] = dy[...]
    rows = q_w.shape[0] // 2
    second[2 * tokens :, : 2 * rows] = q_w[:rows]
    second[2 * tokens :, 2 * rows :] = q_w[rows:]


def pack(ids, x, dy, qkv_weight, up_weight, vectors):
    half, width = qkv_weight.shape[0], 2 * qkv_weight.shape[0]
    tokens = x.shape[0]
    step = up_weight.shape[1] // 8
    token = pl.BlockSpec(x.shape, lambda i, s: (0, 0))
    whole = [pl.BlockSpec(v.shape, lambda i, s: (0,)) for v in vectors]
    outs = ((half + 32, 128), (half + 32 + 3 * half, 128), (2 * tokens + half // 2, width))
    return pl.pallas_call(
        pack_kernel,
        out_shape=tuple(jax.ShapeDtypeStruct(s, bf16) for s in outs),
        grid_spec=pltpu.PrefetchScalarGridSpec(
            num_scalar_prefetch=1,
            grid=(1,),
            in_specs=[
                token,
                token,
                pl.BlockSpec((half, 128), lambda i, s: (0, width // 128)),
                pl.BlockSpec((half, half), lambda i, s: (0, s[2])),
                pl.BlockSpec((half, step), lambda i, s: (0, (1 - s[1]) * 4 + s[2] * 2 + s[3])),
            ]
            + whole,
            out_specs=[pl.BlockSpec(s, lambda i, s: (0, 0)) for s in outs],
        ),
        name="pack",
        cost_estimate=TINY,
    )(ids, x, dy, qkv_weight, qkv_weight, up_weight, *vectors)


def row_vector(block, first, count=3):
    return jnp.concatenate([block[first + k : first + k + 1] for k in range(count)], axis=1)


def natural(side, own, other):
    return jnp.concatenate(
        [jnp.where(side == 0, own, other), jnp.where(side == 0, other, own)], axis=1
    )


def model_vector(side, own, other, index):
    return natural(side, row_vector(own, 3 * index), row_vector(other, 3 * index))


def qkv_bias_tiles(side, own, other):
    low = jnp.where(side == 0, own[18:22], other[18:22])
    high = jnp.where(side == 0, other[22:26], own[22:26])
    tiles = [low[0:1], low[1:2], low[2:3], low[3:4] + high[0:1], high[1:2], high[2:3], high[3:4]]
    return tiles


def normalize(values):
    centred = values - jnp.mean(values, axis=-1, keepdims=True)
    root = lax.rsqrt(jnp.mean(centred * centred, axis=-1, keepdims=True) + 1e-05)
    return centred * root, root


def turn(m, c, s1, s2):
    return m * c + pltpu.roll(m, 120, 1) * s1 + pltpu.roll(m, 8, 1) * s2


def kv_tables(c, s1, s2):
    key = lax.broadcasted_iota(jnp.int32, c.shape, 1) < 64
    return jnp.where(key, c, 1.0), jnp.where(key, s1, 0.0), jnp.where(key, s2, 0.0)


def front_kernel(ids, x, p_own, pu, c, s1, s2, first, kv, p_copy, up0):
    p_oth = pu.at[: p_own.shape[0]]
    p_copy[...] = p_oth[...]
    for k in range(3):
        up0[:, k * 128 : (k + 1) * 128] = pu[416 + 384 * k : 800 + 384 * k, :]
    side = ids[1]
    half = x.shape[1] // 2
    own, other = p_own[half:].astype(f32), p_oth[half:].astype(f32)
    hat, _ = normalize(x[...].astype(f32))
    first[...] = (hat * model_vector(side, own, other, 0) + model_vector(side, own, other, 1)).astype(bf16)
    m = mm(first[:, lanes(side * half, half)], p_own[:half])
    m += mm(first[:, lanes((1 - side) * half, half)], p_oth[:half])
    m += qkv_bias_tiles(side, own, other)[6]
    kv[...] = turn(m, *kv_tables(c[...], s1[...], s2[...])).astype(bf16)


def query_kernel(ids, first, w, w_mine, w_theirs, p_own, p_oth, c, s1, s2, q, w_copy, bias):
    side, core = ids[1], ids[2]
    half = first.shape[1] // 2
    tiles = qkv_bias_tiles(side, p_own[half:].astype(f32), p_oth[half:].astype(f32))
    bias[...] = jnp.concatenate(tiles[:6], axis=1)
    for ref, cb in ((w_mine, core), (w_theirs, 1 - core)):
        col = cb * half
        w_copy[:, lanes(col, half)] = ref[...]
        m = mm(first[:, lanes(side * half, half)], w[:, lanes(col, half)])
        m += mm(first[:, lanes((1 - side) * half, half)], ref[...])
        m += bias[:, lanes(col, half)]
        for k in range(half // 128):
            low = turn(m[:, k * 128 : (k + 1) * 128], c[...], s1[...], s2[...]).astype(bf16)
            q[:, lanes(col + k * 128, 128)] = (low.astype(f32) * 0.125).astype(bf16)


def cotangent_kernel(dy_own, xd, w, g_own, g_oth, q_mine):
    rows = q_mine.shape[0] // 2
    q_mine[:rows] = xd[2 * dy_own.shape[0] :, : 2 * rows]
    q_mine[rows:] = xd[2 * dy_own.shape[0] :, 2 * rows :]
    g_own[...] = mm(dy_own[...], w[...], NT).astype(bf16)
    g_oth[...] = mm(xd[dy_own.shape[0] : 2 * dy_own.shape[0]], w[...], NT).astype(bf16)


def ff_kernel(
    ids, x_own, xd, dy_own, up, up0, up1, up2, up3, down, up_bias, p_own, p_oth,
    keep_a, send_a, keep_b, send_b, act, dh, hat_oth, first_oth, hat_half, dy_copy, up_sum,
    a2, dy, bias, g_down, g_up, up_buf, down_buf, up_sem, down_sem,
):
    side, core, near_y = ids[1], ids[2], ids[3]
    tokens, width = x_own.shape
    x_oth, dy_oth = xd.at[:tokens], xd.at[tokens : 2 * tokens]
    half = width // 2
    wide = act.shape[1]
    step = wide // 4
    pieces = [
        (ref, (jnp.bitwise_xor(core, a) * 2 + jnp.bitwise_xor(near_y, b)), a, b)
        for ref, a, b in ((up0, 0, 0), (up1, 0, 1), (up2, 1, 0), (up3, 1, 1))
    ]

    def up_copy(i, piece):
        at = lanes(side * wide + piece * step, step)
        return pltpu.make_async_copy(up.at[:, at], up_buf.at[i], up_sem.at[i])

    def down_copy(i, piece):
        at = pl.ds(pl.multiple_of(piece * step, step), step)
        return pltpu.make_async_copy(down.at[at, :], down_buf.at[i], down_sem.at[i])

    for i, (_, piece, _, _) in enumerate(pieces):
        up_copy(i, piece).start()
        down_copy(i, piece).start()
    own, other = p_own[half:].astype(f32), p_oth[half:].astype(f32)
    gain1, shift1 = model_vector(side, own, other, 0), model_vector(side, own, other, 1)
    gain2, shift2 = model_vector(side, own, other, 2), model_vector(side, own, other, 3)
    mine, theirs = lanes(side * half, half), lanes((1 - side) * half, half)
    hat_own, _ = normalize(x_own[...].astype(f32))
    a2[:tokens] = (hat_own * gain2 + shift2).astype(bf16)
    hat_other, _ = normalize(x_oth[...].astype(f32))
    hat_oth[...] = hat_other
    a2[tokens:] = (hat_other * gain2 + shift2).astype(bf16)
    first_oth[...] = (hat_other * gain1 + shift1).astype(bf16)
    hat_half[...] = jnp.where(side == 0, hat_other[:, :half], hat_other[:, half:])
    dy[:tokens] = dy_own[...]
    dy[tokens:] = dy_oth[...]
    dy_copy[...] = dy_oth[...]
    bias[...] = up_bias[...].astype(f32).reshape(1, wide)
    rows = half // 4
    far = ids[0] // 4 % 4
    for i, (ref, piece, a, b) in enumerate(pieces):
        up_copy(i, piece).wait()
        down_copy(i, piece).wait()
        cols = lanes(piece * step, step)
        h = mm(a2[:, mine], up_buf[i])
        h += mm(a2[:, theirs], ref[...])
        h += bias[:, cols]
        phi = 0.5 * (1.0 + lax.erf(h * 0.7071067811865476))
        slope = phi + h * jnp.exp(-0.5 * h * h) * 0.3989422804014327
        g = (h * phi).astype(bf16)
        act[:, i * step : (i + 1) * step] = g
        d = mm(dy[...], down_buf[i], NT)
        e = (d * slope).astype(bf16)
        dh[:, i * step : (i + 1) * step] = e
        up_sum[:, cols] = jnp.sum(e.astype(f32), axis=0, keepdims=True)
        g_down[...] = mm(g, dy[...], TN).astype(bf16)
        g_up[:, :half] = mm(a2[:, mine], e, TN).astype(bf16)
        g_up[:, half:] = mm(a2[:, theirs], e, TN).astype(bf16)
        for k in range(4):
            z = jnp.bitwise_xor(far, (k & 1) * 2 + (k >> 1))
            at = pl.ds(pl.multiple_of(z * rows, rows), rows)
            slot = b * 4 + k
            (send_a if a else keep_a)[slot] = g_down[at, :]
            (send_b if a else keep_b)[slot] = g_up[at, :]


def ff_rest_kernel(
    ids, act, dh, x_own, hat_oth, up, up0, up1, up2, up3, down,
    ff_own, ff_oth, ds_own, ds_oth, n_mine, n_send, sums, up_buf, down_buf, up_sem, down_sem,
):
    side, core, near_y = ids[1], ids[2], ids[3]
    tokens, width = x_own.shape
    half = width // 2
    wide = act.shape[1]
    step = wide // 4
    order = ((0, 0), (0, 1), (1, 0), (1, 1))
    pieces = [jnp.bitwise_xor(core, a) * 2 + jnp.bitwise_xor(near_y, b) for a, b in order]
    copies = []
    for i, piece in enumerate(pieces):
        at = pl.ds(pl.multiple_of(piece * step, step), step)
        copies.append(pltpu.make_async_copy(down.at[at, :], down_buf.at[i], down_sem.at[i]))
        at = lanes(side * wide + piece * step, step)
        copies.append(pltpu.make_async_copy(up.at[:, at], up_buf.at[i], up_sem.at[i]))
    for copy in copies:
        copy.start()
    hat_own, _ = normalize(x_own[...].astype(f32))
    for copy in copies:
        copy.wait()
    out = sum(mm(act[:, i * step : (i + 1) * step], down_buf[i]) for i in range(4))
    ff_own[...] = out[:tokens]
    ff_oth[...] = out[tokens:]
    ds_mine = sum(mm(dh[:, i * step : (i + 1) * step], up_buf[i], NT) for i in range(4))
    ds_theirs = sum(
        mm(dh[:, i * step : (i + 1) * step], ref[...], NT) for i, ref in enumerate((up0, up1, up2, up3))
    )
    low = jnp.where(side == 0, ds_mine, ds_theirs)
    high = jnp.where(side == 0, ds_theirs, ds_mine)
    for part, ds in ((slice(0, half), low), (slice(half, width), high)):
        ds_own[:, part] = ds[:tokens]
        ds_oth[:, part] = ds[tokens:].astype(bf16)
        moved = ds[:tokens] * hat_own[:, part] + ds[tokens:] * hat_oth[:, part]
        sums[0:1, part] = jnp.sum(moved, axis=0, keepdims=True)
        sums[1:2, part] = jnp.sum(ds, axis=0, keepdims=True)
    split_rows(sums, 2, side, half, n_mine, n_send)


def split_rows(sums, count, side, half, mine, send):
    for ref, owner in ((mine, side), (send, 1 - side)):
        ref[...] = jnp.zeros_like(ref)
        for i in range(count):
            for k in range(half // 128):
                at = i * (half // 128) + k
                ref[at : at + 1, :] = sums[i : i + 1, lanes(owner * half + k * 128, 128)]


class Block:
    def __init__(self, stages, n_dev, docs, side, ids, len_ref):
        self.stages, self.n_dev, self.me, self.fsdp = stages, n_dev, ids[0], ids[1]
        self.block = ids[0] if side == 0 else 2 * n_dev - 1 - ids[0]
        self.rows = pl.ds(side * BLOCK, BLOCK)
        self.low = lax.broadcasted_iota(jnp.int32, (BLOCK, 128), 1) < 64
        base = self.block * BLOCK
        self.qpos = base + lax.broadcasted_iota(jnp.int32, (1, BLOCK), 1)
        total = first = jnp.int32(0)
        self.qstart = jnp.zeros((1, BLOCK), jnp.int32)
        for e in range(docs):
            size = len_ref[0, e]
            total = total + size
            self.qstart = self.qstart + jnp.where(total <= self.qpos, size, 0)
            first = first + jnp.where(total <= base, size, 0)
        self.steps = (base + BLOCK - first + 2 * BLOCK - 1) // (2 * BLOCK)

    def row_of(self, j):
        j = jnp.maximum(j, 0)
        dev = jnp.where(j < self.n_dev, j, 2 * self.n_dev - 1 - j)
        slot = slot_of(jnp.bitwise_xor(dev, self.me), self.stages)
        return pl.multiple_of((slot * 2 + jnp.where(j < self.n_dev, 0, 1)) * BLOCK, BLOCK)

    def columns(self, p, half):
        close = p < half // 128
        local = (p % (half // 128)) * 128
        return close, local, lanes((self.fsdp if close else 1 - self.fsdp) * half + local, 128)

    def half_turn(self, two):
        return pltpu.roll(two.astype(f32), 64, 1).astype(bf16)

    def spread_query(self, q_ref, qz):
        for p in range(q_ref.shape[1] // 128):
            two = q_ref[self.rows, self.columns(p, q_ref.shape[1] // 2)[2]]
            zero = jnp.zeros_like(two)
            qz[pl.ds(p * 256, 128), :] = jnp.where(self.low, two, zero)
            qz[pl.ds(p * 256 + 128, 128), :] = jnp.where(self.low, self.half_turn(two), zero)

    def load(self, t, kv_mine, kv_theirs, bias):
        middle = kv_mine.shape[0]
        parts, at = [], []
        hi = self.block - 2 * t
        for j in (hi - 1, hi):
            row = self.row_of(j)
            inner = pl.multiple_of(jnp.where(row < middle, row, row - middle), BLOCK)
            here = pl.ds(inner, BLOCK)
            parts.append(jnp.where(row < middle, kv_mine[here, :], kv_theirs[here, :]))
            at.append(row)
        kpos = (hi - 1) * BLOCK + lax.broadcasted_iota(jnp.int32, (2 * BLOCK, BLOCK), 0)
        ok = (kpos <= self.qpos) & (kpos >= self.qstart)
        bias[...] = jnp.where(ok, 0.0, -1e30)
        return jnp.concatenate(parts, axis=0), at


def attn_forward_kernel(
    stages, n_dev, docs, side, ids, len_ref, q_ref, kv_mine, kv_theirs, g_own, g_oth,
    o_own, o_oth, st, qz, ot, bias,
):
    me = Block(stages, n_dev, docs, side, ids, len_ref)
    half = q_ref.shape[1] // 2
    pairs = q_ref.shape[1] // 128
    me.spread_query(q_ref, qz)
    ot[...] = jnp.zeros_like(ot)
    st[0] = jnp.full(st.shape[1:], -1e30, f32)
    st[1] = jnp.zeros(st.shape[1:], f32)

    def forward(t, carry):
        kvb, _ = me.load(t, kv_mine, kv_theirs, bias)
        vt = kvb.astype(f32).T.astype(bf16)[64:]
        mask = bias[...]
        for p in range(pairs):
            s2 = mm(kvb, qz[pl.ds(p * 256, 256), :], NT)
            for i in range(2):
                h = 2 * p + i
                s = s2[:, i * 128 : (i + 1) * 128] + mask
                old = st[0, h : h + 1, :]
                new = jnp.maximum(old, jnp.max(s, axis=0, keepdims=True))
                e = jnp.exp(s - new)
                alpha = jnp.exp(old - new)
                st[0, h : h + 1, :] = new
                st[1, h : h + 1, :] = st[1, h : h + 1, :] * alpha + jnp.sum(e, axis=0, keepdims=True)
                hs = pl.ds(h * 64, 64)
                ot[hs, :] = ot[hs, :] * alpha + mm(vt, e.astype(bf16))
        return 0

    lax.fori_loop(0, me.steps, forward, 0)
    for p in range(pairs):
        close, local, _ = me.columns(p, half)
        gt = (g_own if close else g_oth)[me.rows, pl.ds(local, 128)].astype(f32).T
        halves = []
        for i in range(2):
            h = 2 * p + i
            l = st[1, h : h + 1, :]
            o = ot[pl.ds(h * 64, 64), :] / l
            halves.append(o)
            st[2, h : h + 1, :] = jnp.sum(o * gt[i * 64 : (i + 1) * 64], axis=0, keepdims=True)
            st[0, h : h + 1, :] = st[0, h : h + 1, :] + jnp.log(l)
        (o_own if close else o_oth)[:, pl.ds(local, 128)] = jnp.concatenate(halves, axis=0).T.astype(bf16)


def attn_backward_kernel(stages, n_dev, docs, side, last, *refs):
    ids, len_ref, q_ref, kv_mine, kv_theirs, g_own, g_oth, st, cos_ref, sin_ref = refs[:10]
    if not last:
        dm_ref, acc, qz, gz, dqt, bias, ds_sc, p_sc = refs[10:]
        acc[...] = jnp.zeros_like(acc)
    else:
        before, dm_ref, dkv_keep, dkv_send, qz, gz, dqt, bias, ds_sc, p_sc, acc = refs[10:]
        acc[...] = before[...]
    me = Block(stages, n_dev, docs, side, ids, len_ref)
    half = q_ref.shape[1] // 2
    pairs = q_ref.shape[1] // 128
    me.spread_query(q_ref, qz)
    for p in range(pairs):
        close, local, _ = me.columns(p, half)
        two = (g_own if close else g_oth)[me.rows, pl.ds(local, 128)]
        zero = jnp.zeros_like(two)
        gz[pl.ds(p * 256, 128), :] = jnp.where(me.low, zero, me.half_turn(two))
        gz[pl.ds(p * 256 + 128, 128), :] = jnp.where(me.low, zero, two)
    dqt[...] = jnp.zeros_like(dqt)

    def backward(t, carry):
        kvb, at = me.load(t, kv_mine, kv_theirs, bias)
        kt = kvb.astype(f32).T.astype(bf16)[:64]
        mask = bias[...]
        for p in range(pairs):
            s2 = mm(kvb, qz[pl.ds(p * 256, 256), :], NT)
            dp2 = mm(kvb, gz[pl.ds(p * 256, 256), :], NT)
            for i in range(2):
                h = 2 * p + i
                sl = slice(i * 128, (i + 1) * 128)
                pr = jnp.exp((s2[:, sl] + mask) - st[0, h : h + 1, :])
                ds = pr * (dp2[:, sl] - st[2, h : h + 1, :])
                ds_sc[:, h * 128 : (h + 1) * 128] = ds.astype(bf16)
                p_sc[:, h * 128 : (h + 1) * 128] = pr.astype(bf16)
        part = mm(ds_sc[...], qz[...]) + mm(p_sc[...], gz[...])
        for i in range(2):
            acc[pl.ds(at[i], BLOCK), :] += part[i * BLOCK : (i + 1) * BLOCK]
        dqt[...] += mm(kt, ds_sc[...])
        return 0

    lax.fori_loop(0, me.steps, backward, 0)
    cos = cos_ref[side]
    sin = sin_ref[side]
    for p in range(pairs):
        halves = []
        for i in range(2):
            h = 2 * p + i
            g = dqt[:, h * 128 : (h + 1) * 128] * 0.125
            g0, g1 = g[:8], g[8:16]
            halves += [g0 * cos + g1 * sin, g1 * cos - g0 * sin, g[16:]]
        dm_ref[:, me.columns(p, half)[2]] = jnp.concatenate(halves, axis=0).T.astype(bf16)
    if last:
        middle = dkv_keep.shape[0]
        dkv_keep[...] = acc[:middle].astype(bf16)
        dkv_send[...] = acc[middle:].astype(bf16)


def attn_forward(side, stages, n_dev, ids, lengths, q, kv, g_own, g_oth):
    width = q.shape[1]
    block = q.shape[0] // 2
    rows = width // 64 * 128
    kv = near(*kv) if n_dev <= LOW else kv
    return call(
        partial(attn_forward_kernel, stages, n_dev, lengths.shape[1], side),
        "attn_forward",
        [((block, width // 2), bf16, False), ((block, width // 2), bf16, True), ((3, 16, 128), f32, True)],
        (ids, lengths, *near(q), *kv, g_own, *near(g_oth)),
        scratch=[pltpu.VMEM((rows, 128), bf16), pltpu.VMEM((width, 128), f32), pltpu.VMEM((256, 128), f32)],
        room=6 + (0 if n_dev <= LOW else kv[0].size * 4 // 2**20),
    )


def attn_backward(side, stages, n_dev, ids, lengths, q, kv, g_own, g_oth, st, cos, sin, before=()):
    width = q.shape[1]
    block = q.shape[0] // 2
    middle = kv[0].shape[0]
    rows = width // 64 * 128
    small = n_dev <= LOW
    close = near if small else (lambda *values: values)
    outs = [((block, width), bf16, True)]
    last = len(before) > 0
    outs += [((middle, 128), bf16, True)] * 2 if last else [((2 * middle, 128), f32, small)]
    scratch = [
        pltpu.VMEM((rows, 128), bf16),
        pltpu.VMEM((rows, 128), bf16),
        pltpu.VMEM((64, rows), f32),
        pltpu.VMEM((256, 128), f32),
        pltpu.VMEM((256, rows), bf16),
        pltpu.VMEM((256, rows), bf16),
    ]
    if last:
        scratch += [pltpu.VMEM((2 * middle, 128), f32)]
    return call(
        partial(attn_backward_kernel, stages, n_dev, lengths.shape[1], side, last),
        "attn_backward",
        outs,
        (ids, lengths, *near(q), *close(*kv), g_own, *near(g_oth, st), cos, sin, *close(*before)),
        scratch=scratch,
        room=8 + 2 * middle * 128 * (4 if small else 7) // 2**20,
    )


def pile_kernel(a0, a1, b0, b1, c0, c1, *outs):
    for out, parts in zip(outs, ((a0, a1), (b0, b1), (c0, c1))):
        rows = parts[0].shape[0]
        out[:rows] = parts[0][...]
        out[rows:] = parts[1][...]


def mix_kernel(ff, o, w, out):
    out[...] = (ff[...] + mm(o[...], w[...])).astype(bf16)


def result_kernel(ids, x, ff, o, w, recv, p_own, p_oth, out):
    side = ids[1]
    half = x.shape[1] // 2
    own, other = p_own[half:].astype(f32), p_oth[half:].astype(f32)
    y = x[...].astype(f32) + (ff[...] + mm(o[...], w[...])) + recv[...].astype(f32)
    y += model_vector(side, own, other, 4) + model_vector(side, own, other, 5)
    out[...] = y.astype(bf16)


def dm_kv_kernel(*refs):
    later, c, s1, s2, out = refs[-5:]
    total = later[...]
    for ref in refs[:-5]:
        total = total + ref[...].astype(f32)
    c, s1, s2 = kv_tables(c[...], s1[...], s2[...])
    out[...] = turn(total, c, -s1, -s2).astype(bf16)


def x_grad_kernel(ids, x, dy, dm, dm_kv, w, w_oth, p_own, p_oth, ds, ds_recv, out, da):
    side = ids[1]
    width = x.shape[1]
    half = width // 2
    own, other = p_own[half:].astype(f32), p_oth[half:].astype(f32)
    mine, theirs = lanes(side * half, half), lanes((1 - side) * half, half)
    da[:, mine] = mm(dm[...], w[:, :width], NT) + mm(dm_kv[...], p_own[:half], NT)
    da[:, theirs] = mm(dm[...], w_oth[...], NT) + mm(dm_kv[...], p_oth[:half], NT)
    hat, root = normalize(x[...].astype(f32))
    total = dy[...].astype(f32)
    for i, grad in enumerate((da[...], ds[...] + ds_recv[...].astype(f32))):
        up = grad * model_vector(side, own, other, 2 * i)
        total += root * (
            up - jnp.mean(up, axis=-1, keepdims=True) - hat * jnp.mean(up * hat, axis=-1, keepdims=True)
        )
    out[...] = total


def pair_kernel(ids, f_own, f_oth, dm_own, dm_oth, o_own, o_oth, dy_own, dy_oth, keep, send, gq, go):
    side, core = ids[1], ids[2]
    half = f_own.shape[1] // 2
    mine = lanes(side * half, half)
    gq[...] = mm(f_own[:, mine], dm_own[...], TN) + mm(f_oth[:, mine], dm_oth[...], TN)
    go[...] = mm(o_own[...], dy_own[...], TN) + mm(o_oth[...], dy_oth[...], TN)
    rows = half // 8
    close = ids[0] % LOW // 2
    for ref, cb in ((keep, core), (send, 1 - core)):
        cols = lanes(cb * half, half)
        for k in range(8):
            at = pl.ds(pl.multiple_of(jnp.bitwise_xor(close, CHUNKS[k]) * rows, rows), rows)
            ref[k * rows : (k + 1) * rows, 0:half] = gq[at, cols].astype(bf16)
            ref[k * rows : (k + 1) * rows, half:] = go[at, cols].astype(bf16)


def tail_kernel(
    ids, f_own, f_oth, dm_own, dm_oth, dy_own, dy_oth, kv_own, kv_oth, n_mine, n_recv, up_sum,
    x_own, hat_half, w, p_own, out, tail, hat,
):
    side = ids[1]
    half = f_own.shape[1] // 2
    mine = lanes(side * half, half)
    tail[:half] = mm(f_own[:, mine], kv_own[...], TN) + mm(f_oth[:, mine], kv_oth[...], TN)
    tail[half:] = jnp.zeros((32, 128), f32)
    gain = shift = 0.0
    hat[...] = normalize(x_own[...].astype(f32))[0]
    for x, dm, kv in ((hat[:, mine], dm_own, kv_own), (hat_half[...], dm_oth, kv_oth)):
        grad = mm(dm[...], w[:, : 2 * half], NT) + mm(kv[...], p_own[:half], NT)
        gain += jnp.sum(grad * x, axis=0, keepdims=True)
        shift += jnp.sum(grad, axis=0, keepdims=True)
    row = half
    for v in (gain, shift):
        for k in range(3):
            tail[row + k : row + k + 1, :] = v[:, k * 128 : (k + 1) * 128]
        row += 3
    v = n_mine[...] + n_recv[...]
    tail[row : row + 6] = v[:6]
    row += 6

    def total(a, b):
        return jnp.sum(a.astype(f32), axis=0, keepdims=True) + jnp.sum(b.astype(f32), axis=0, keepdims=True)

    v = total(dy_own[:, mine], dy_oth[:, mine])
    for k in range(3):
        tail[row + k : row + k + 1, :] = v[:, k * 128 : (k + 1) * 128]
    row += 3
    v = jnp.concatenate([total(dm_own[...], dm_oth[...]), total(kv_own[...], kv_oth[...])], axis=1)
    moved = jnp.concatenate([v[:, 448:], v[:, :448]], axis=1)
    v = jnp.where(side == 0, v, moved)
    for k in range(4):
        tail[row + k : row + k + 1, :] = v[:, k * 128 : (k + 1) * 128]
    row += 4
    for k in range(12):
        tail[row + k : row + k + 1, :] = up_sum[:, k * 128 : (k + 1) * 128]
    out[...] = tail[...].astype(bf16)


def sum_kernel(*refs):
    total = refs[0][...].astype(f32)
    for ref in refs[1:-1]:
        total = total + ref[...].astype(f32)
    refs[-1][...] = total.astype(refs[-1].dtype)


def sum_of(first, second, name):
    return call(sum_kernel, name, [(first.shape, first.dtype, True)], near(first, second))[0]


def up_part_kernel(a, b, own, other):
    half = own.shape[-1]
    total = a[...].astype(f32) + b[...].astype(f32)
    own[...] = total[..., :half].astype(bf16)
    other[...] = total[..., half:].astype(bf16)


def up_join_kernel(own, other, out):
    half = own.shape[-1]
    out[..., :half] = own[...]
    out[..., half:] = other[...]


def chunk_of(ids, other_core, slot):
    core, near_y, far = ids[2], ids[3], ids[0] // 4 % 4
    piece = jnp.bitwise_xor(core, other_core) * 2 + jnp.bitwise_xor(near_y, slot >> 2)
    return piece, jnp.bitwise_xor(far, (slot & 1) * 2 + (slot >> 1 & 1))


def down_out_kernel(ids, mine, theirs, out):
    rows = mine.shape[1]
    for a, ref in enumerate((mine, theirs)):
        for k in range(8):
            piece, z = chunk_of(ids, a, k)
            out[pl.ds(pl.multiple_of((piece * 4 + z) * rows, rows), rows), :] = ref[k].astype(f32)


def up_out_kernel(ids, mine, theirs, out):
    side = ids[1]
    rows = mine.shape[1]
    half = mine.shape[2] // 2
    wide = out.shape[1] // 2
    for a, ref in enumerate((mine, theirs)):
        for k in range(8):
            piece, z = chunk_of(ids, a, k)
            at = pl.ds(pl.multiple_of(z * rows, rows), rows)
            for j, owner in ((0, side), (1, 1 - side)):
                part = ref[k, :, j * half : (j + 1) * half].astype(f32)
                out[at, lanes(owner * wide + piece * half, half)] = part


def attn_out_kernel(ids, p_mine, p_theirs, tail, g_qkv, g_out, n0, n1, n2, n3, qb, ob, ub, db):
    core = ids[2]
    close = ids[0] % LOW // 2
    half = g_qkv.shape[0]
    rows = half // 8
    for ref, cb in ((p_mine, core), (p_theirs, 1 - core)):
        cols = lanes(cb * half, half)
        for k in range(8):
            at = pl.ds(pl.multiple_of(jnp.bitwise_xor(close, CHUNKS[k]) * rows, rows), rows)
            part = ref[k * rows : (k + 1) * rows, :].astype(f32)
            g_qkv[at, cols] = part[:, :half]
            g_out[at, cols] = part[:, half:]
    g_qkv[:, 2 * half :] = tail[:half].astype(f32)
    small = tail[half:].astype(f32)
    for i, ref in enumerate((n0, n1, n2, n3, ob)):
        ref[...] = row_vector(small, 3 * i).reshape(half)
    db[...] = row_vector(small, 12).reshape(half)
    qb[...] = row_vector(small, 15, 4)[:, : qb.shape[0]].reshape(qb.shape[0])
    ub[...] = row_vector(small, 19, 12).reshape(ub.shape[0])


def body(
    layer_input, doc_lengths, ln1_gain, ln1_bias, ln2_gain, ln2_bias, qkv_weight, qkv_bias,
    out_weight, out_bias, up_weight, up_bias, down_weight, down_bias, out_grad, kv_grad_later,
):
    devices = lax.axis_size("ctx")
    me = lax.axis_index("ctx").astype(jnp.int32)
    side = lax.axis_index("fsdp").astype(jnp.int32)
    ids = jnp.stack([me, side, me % 2, me // 2 % 2])
    tokens, width = layer_input.shape[1:]
    half_rows = tokens // 2
    half = width // 2
    wide = up_weight.shape[1] // 2
    stages = stages_of(devices)
    x_own, dy_own = layer_input[0], out_grad[0]

    vectors = (ln1_gain, ln1_bias, ln2_gain, ln2_bias, out_bias, down_bias, qkv_bias)
    p_own, pu_own, xd_own = pack(ids, x_own, dy_own, qkv_weight, up_weight, vectors)
    pu_oth = swap_x(pu_own)
    xd = swap_x(after(xd_own, pu_oth))

    offsets = jnp.arange(half_rows, dtype=jnp.int32)
    places = jnp.concatenate([me * half_rows + offsets, (2 * devices - 1 - me) * half_rows + offsets]).astype(f32)
    half_rot = ROT // 2
    freq = 10000.0 ** (-jnp.arange(half_rot, dtype=f32) / half_rot)
    lane = np.arange(128)
    angles = places[:, None] * jnp.tile(freq, 128 // half_rot)[None, :]
    cosine, sine = jnp.cos(angles), jnp.sin(angles)
    tables = (
        jnp.where(lane % 64 < 16, cosine, 1.0),
        jnp.where(lane % 64 < 8, -sine, 0.0),
        jnp.where((lane % 64 >= 8) & (lane % 64 < 16), sine, 0.0),
    )
    t_angles = places.reshape(2, 1, half_rows) * freq[None, :, None]
    cos_t, sin_t = jnp.cos(t_angles), jnp.sin(t_angles)

    first_own, kv, p_oth, up0 = call(
        front_kernel,
        "front",
        [
            ((tokens, width), bf16, False), ((tokens, 128), bf16, True), (p_own.shape, bf16, False),
            ((half, half), bf16, True),
        ],
        (ids, x_own, p_own, *near(pu_oth), *tables),
    )
    up1, up2 = swap_ctx(up0, 2), swap_ctx(up0, 1)
    kv = gather_step(kv, stages[0][0], "kv_join")
    ups = (up0, up1, up2, swap_ctx(after(up1, kv), 1))
    for stride, _ in stages[1:-2]:
        kv = gather_step(kv, stride, "kv_join")
    kv_mine = gather_step(kv, 2, "kv_join")
    kv_theirs = swap_ctx(kv_mine, 1)

    g_own, g_send, q_mine = call(
        cotangent_kernel,
        "cotangent",
        [((tokens, half), bf16, False), ((tokens, half), bf16, True), ((half, half), bf16, True)],
        (dy_own, *near(xd), out_weight),
    )
    g_oth = swap_x(g_send)
    q_theirs = swap_ctx(q_mine, 1)

    rows = half // 4
    step = wide // 4
    chunks = ((8, rows, width), bf16, True)
    token_f32, token_low = ((tokens, width), f32, False), ((tokens, width), bf16, False)
    (
        keep_a, send_a, keep_b, send_b, act, dh, hat_oth, first_oth, hat_half, dy_far, up_sum,
    ) = call(
        ff_kernel,
        "ff",
        [
            chunks, chunks, chunks, chunks, ((2 * tokens, wide), bf16, True), ((2 * tokens, wide), bf16, True),
            token_f32, token_low, ((tokens, half), f32, False), token_low, ((1, wide), f32, False),
        ],
        (
            ids, x_own, *near(after(xd, kv_mine, g_send)), dy_own, Raw(up_weight), *near(*ups), Raw(down_weight),
            up_bias, p_own, p_oth,
        ),
        scratch=[
            pltpu.VMEM((2 * tokens, width), bf16),
            pltpu.VMEM((2 * tokens, width), bf16),
            pltpu.VMEM((1, wide), f32),
            pltpu.VMEM((half, width), bf16),
            pltpu.VMEM((half, width), bf16),
            pltpu.VMEM((4, half, step), bf16),
            pltpu.VMEM((4, step, width), bf16),
            pltpu.SemaphoreType.DMA((4,)),
            pltpu.SemaphoreType.DMA((4,)),
        ],
        room=16,
    )
    row_block = ((8, 128), f32, False)
    ff_own, ff_oth, ds_own, ds_oth, n_mine, n_send = call(
        ff_rest_kernel,
        "ff_rest",
        [token_f32, token_f32, token_f32, token_low, row_block, row_block],
        (ids, *near(act, dh), x_own, hat_oth, Raw(up_weight), *near(*ups), Raw(down_weight)),
        scratch=[
            pltpu.VMEM((8, width), f32),
            pltpu.VMEM((4, half, step), bf16),
            pltpu.VMEM((4, step, width), bf16),
            pltpu.SemaphoreType.DMA((4,)),
            pltpu.SemaphoreType.DMA((4,)),
        ],
        room=18,
    )
    n_recv = swap_x(n_send)
    ds_recv = swap_x(ds_oth)
    low = min(LOW, devices)
    keep_a, send_a = scatter_step(keep_a, send_a, 1, "down_add")
    keep_b, send_b = scatter_step(keep_b, send_b, 1, "up_add")
    q, q_far = call(
        query_kernel,
        "query",
        [((tokens, width), bf16, True), ((half, width), bf16, False)],
        (ids, first_own, qkv_weight, *near(q_mine, q_theirs), p_own, p_oth, *tables),
        scratch=[pltpu.VMEM((1, width), f32)],
    )
    pairs = (stages, devices, ids, doc_lengths)
    q = after(q, send_a, send_b)
    kv_all = (kv_mine, kv_theirs)
    o_own0, o_send0, st0 = attn_forward(0, *pairs, q, kv_all, g_own, g_oth)
    keep_a, send_a = scatter_step(after(keep_a, st0), send_a, 2, "down_add")
    dm_own0, dkv = attn_backward(0, *pairs, after(q, send_a), kv_all, g_own, g_oth, st0, cos_t, sin_t)
    keep_b, send_b = scatter_step(after(keep_b, dm_own0), send_b, 2, "up_add")
    o_own1, o_send1, st1 = attn_forward(1, *pairs, after(q, send_b), kv_all, g_own, g_oth)
    keep_a, send_a = scatter_step(after(keep_a, st1), send_a, 4, "down_add")
    if devices <= LOW:
        dm_own1, dkv_keep, dkv_send = attn_backward(
            1, *pairs, after(q, send_a), kv_all, g_own, g_oth, st1, cos_t, sin_t, before=(dkv,)
        )
    else:
        dm_own1, dkv_more = attn_backward(1, *pairs, after(q, send_a), kv_all, g_own, g_oth, st1, cos_t, sin_t)
        dkv = (dkv + dkv_more).astype(bf16)
        dkv_keep, dkv_send = dkv[: kv_mine.shape[0]], dkv[kv_mine.shape[0] :]
    keep_b, send_b = scatter_step(after(keep_b, dm_own1), send_b, 4, "up_add")
    down_part = high_sum(sum_of(*scatter(keep_a, send_a, low, "down_add", 8), "down_sum"))
    up_own, up_send = call(
        up_part_kernel,
        "up_part",
        [((1, rows, half), bf16, True), ((1, rows, half), bf16, True)],
        near(*scatter(keep_b, send_b, low, "up_add", 8)),
    )
    up_own, up_send = high_sum(up_own), high_sum(up_send)
    up_part = call(up_join_kernel, "up_join", [((1, rows, width), bf16, True)], near(up_own, swap_x(up_send)))[0]
    o_own, o_send, dm_own = call(
        pile_kernel,
        "pile",
        [((tokens, half), bf16, False), ((tokens, half), bf16, True), ((tokens, width), bf16, True)],
        (o_own0, o_own1, *near(o_send0, o_send1, dm_own0, dm_own1)),
    )
    kv_pieces = scatter(dkv_keep, dkv_send, devices, "kv_add")
    o_oth = swap_x(o_send)
    dm_oth = swap_x(dm_own)

    y_send = call(mix_kernel, "mix", [((tokens, width), bf16, True)], (ff_oth, *near(o_oth), out_weight))[0]
    y_recv = swap_x(y_send)
    result = call(
        result_kernel,
        "result",
        [((tokens, width), bf16, False)],
        (ids, x_own, ff_own, o_own, out_weight, *near(y_recv), p_own, p_oth),
    )[0]

    kv_pieces = (after(kv_pieces[0], ds_recv), kv_pieces[1])
    dm_kv = call(
        dm_kv_kernel, "dm_kv", [((tokens, 128), bf16, True)], (*near(*kv_pieces), kv_grad_later[0], *tables)
    )[0]
    dm_kv_oth = swap_x(dm_kv)
    grad_inputs = call(
        x_grad_kernel,
        "x_grad",
        [((tokens, width), f32, False)],
        (
            ids, x_own, dy_own, *near(dm_own, dm_kv), qkv_weight, q_far, p_own, p_oth, ds_own,
            *near(ds_recv),
        ),
        scratch=[pltpu.VMEM((tokens, width), f32)],
        room=8,
    )[0]
    keep, send = call(
        pair_kernel,
        "pair",
        [((half, width), bf16, True), ((half, width), bf16, True)],
        (ids, first_own, first_oth, *near(dm_own, dm_oth), o_own, *near(o_oth), dy_own, dy_far),
        scratch=[pltpu.VMEM((half, width), f32), pltpu.VMEM((half, width), f32)],
        room=8,
    )
    pieces = scatter(keep, send, low, "pair_add")
    pair = high_sum(sum_of(pieces[0], pieces[1], "pair_sum"))
    tail = call(
        tail_kernel,
        "tail",
        [((half + 32, 128), bf16, True)],
        (
            ids, first_own, first_oth, *near(dm_own, dm_oth), dy_own, dy_far, *near(dm_kv, dm_kv_oth), n_mine,
            *near(n_recv), up_sum, x_own, hat_half, qkv_weight, p_own,
        ),
        scratch=[pltpu.VMEM((half + 32, 128), f32), pltpu.VMEM((tokens, width), f32)],
        room=8,
    )[0]
    outs = []
    for value, name in ((down_part, "down_join"), (up_part, "up_join"), (pair, "pair_join")):
        for stride, _ in stages_of(low)[:-1]:
            value = gather_step(value, stride, name)
        outs.append(near(value, swap_ctx(value, 1)))
    g_down = call(down_out_kernel, "down_out", [((wide, width), f32, False)], (ids, *outs[0]), room=8)[0]
    g_up = call(up_out_kernel, "up_out", [((half, 2 * wide), f32, False)], (ids, *outs[1]), room=8)[0]
    for i, (stride, _) in enumerate(stages[::-1]):
        other = swap_ctx(tail, stride)
        if i == 2:
            tail = after(tail, result, grad_inputs)
        if i == 3:
            tail = after(tail, g_down, g_up)
        tail = sum_of(tail, other, "tail_sum")
    vec = ((half,), f32, False)
    g_qkv, g_out, *small = call(
        attn_out_kernel,
        "attn_out",
        [
            ((half, width + 128), f32, False), ((half, width), f32, False), vec, vec, vec, vec,
            (qkv_bias.shape, f32, False), vec, (up_bias.shape, f32, False), vec,
        ],
        (ids, *outs[2], *near(tail)),
        room=6,
    )
    n0, n1, n2, n3, qb, ob, ub, db = small
    return (result[None], grad_inputs[None], n0, n1, n2, n3, g_qkv, qb, g_out, ob, g_up, ub, g_down, db)


def solution(mesh):
    token = P("fsdp", "ctx", None)
    vec = P("fsdp")
    mat = P("fsdp", None)
    return jax.shard_map(
        body,
        mesh=mesh,
        in_specs=(token, mat, vec, vec, vec, vec, mat, vec, mat, vec, mat, vec, mat, vec, token, token),
        out_specs=(token, token, vec, vec, vec, vec, mat, vec, mat, vec, mat, vec, mat, vec),
        check_vma=False,
    )
```

```python
from functools import partial

import jax
import jax.numpy as jnp
import numpy as np
from jax import lax
from jax.experimental import pallas as pl
from jax.experimental.pallas import tpu as pltpu
from jax.sharding import PartitionSpec as P

ROT = 16
BLOCK = 128
LOW = 16
NT = (((1,), (1,)), ((), ()))
NN = (((1,), (0,)), ((), ()))
TN = (((0,), (0,)), ((), ()))
bf16 = jnp.bfloat16
f32 = jnp.float32
WEIGHT = {'pile': 8.0, 'up_add': 1.0, 'down_join': 6.0, 'dm_kv': 2.0, 'pair_sum': 4.0, 'ff_rest': 2.0, 'mix': 0.0, 'tail': 0.0}
TINY = pl.CostEstimate(flops=1, transcendentals=0, bytes_accessed=1)


def mm(left, right, dims=NN):
    return lax.dot_general(left, right, dims, preferred_element_type=f32)


def vmem():
    return pl.BlockSpec(memory_space=pltpu.VMEM)


def smem():
    return pl.BlockSpec(memory_space=pltpu.SMEM)


CHAIN = []


class Near:
    def __init__(self, value):
        self.value = value


class Raw(Near):
    pass


def near(*values):
    return tuple(Near(v) for v in values)


def call(kernel, name, outs, args, scratch=(), room=2):
    args = list(args)
    if CHAIN:
        at = next(i for i, v in enumerate(args) if not isinstance(v, Raw) and getattr(v, "dtype", f32) != jnp.int32)
        v = args[at]
        args[at] = Near(after(v.value, CHAIN[0])) if isinstance(v, Near) else after(v, CHAIN[0])
    specs = [vmem() for _ in args]
    values = list(args)
    for i, v in enumerate(args):
        if isinstance(v, Raw):
            values[i] = v.value
            specs[i] = pl.BlockSpec(memory_space=pl.ANY)
        elif isinstance(v, Near):
            values[i] = pltpu.with_memory_space_constraint(v.value, pltpu.VMEM)
        elif v.dtype == jnp.int32:
            specs[i] = smem()
    if lax.axis_size("ctx") > LOW and name[:4] != "attn":
        room += sum(int(np.prod(s)) * jnp.dtype(d).itemsize for s, d, _ in outs) >> 20
    results = pl.pallas_call(
        kernel,
        out_shape=tuple(pltpu.VMEM(s, d) if n else jax.ShapeDtypeStruct(s, d) for s, d, n in outs),
        in_specs=specs,
        out_specs=tuple(vmem() for _ in outs),
        scratch_shapes=list(scratch),
        name=name,
        cost_estimate=pl.CostEstimate(
            flops=int(WEIGHT.get(name, 0) * 1e9) + 1, transcendentals=0, bytes_accessed=1
        ),
        compiler_params=pltpu.CompilerParams(vmem_limit_bytes=room << 20),
    )(*values)
    CHAIN[:] = [results[0]]
    return results


def lanes(start, size):
    return pl.ds(pl.multiple_of(start, 128), size)


def swap_x(value):
    return lax.ppermute(value, "fsdp", [(0, 1), (1, 0)])


def swap_ctx(value, mask):
    devices = lax.axis_size("ctx")
    return lax.ppermute(value, "ctx", [(i, i ^ mask) for i in range(devices)])


def stages_of(devices):
    out, stride = [], 1
    while stride < devices:
        out.append((stride, 2))
        stride *= 2
    return out[::-1]


CHUNKS = [int(f"{k:03b}"[::-1], 2) for k in range(8)]


def slot_of(relative, stages):
    slot, count = relative * 0, 1
    for stride, size in stages:
        slot = slot + relative // stride % size * count
        count *= size
    return slot


def join_kernel(*refs):
    out = refs[-1]
    rows = refs[0].shape[0]
    for k, ref in enumerate(refs[:-1]):
        out[k * rows : (k + 1) * rows] = ref[...]


def join(first, second, name):
    shape = (2 * first.shape[0],) + first.shape[1:]
    return call(join_kernel, name, [(shape, first.dtype, True)], near(first, second))[0]


def gather_step(value, mask, name):
    return join(value, swap_ctx(value, mask), name)


def after(value, *others):
    return lax.optimization_barrier((value, *others))[0]


def add_split_kernel(a_ref, b_ref, keep, send):
    half = a_ref.shape[0] // 2
    for ref, part in ((keep, slice(0, half)), (send, slice(half, 2 * half))):
        ref[...] = (a_ref[part].astype(f32) + b_ref[part].astype(f32)).astype(ref.dtype)


def scatter_step(keep, send, mask, name):
    shape = (keep.shape[0] // 2,) + keep.shape[1:]
    out = (shape, keep.dtype, True)
    return call(add_split_kernel, name, [out, out], near(keep, swap_ctx(send, mask)))


def scatter(keep, send, devices, name, stride=1):
    while 2 * stride < devices:
        keep, send = scatter_step(keep, send, stride, name)
        stride *= 2
    return keep, swap_ctx(send, stride)


def high_sum(value):
    devices = lax.axis_size("ctx")
    if devices <= LOW:
        return value
    groups = [[h * LOW + l for h in range(devices // LOW)] for l in range(LOW)]
    return lax.psum(value, "ctx", axis_index_groups=groups)


def pack_kernel(ids, kv_w, up_w, g1, b1, g2, b2, ob, db, qb, small, first):
    small[:384, :] = kv_w[...]
    small[384:, :] = jnp.zeros((32, 128), bf16)
    row = 384
    for ref in (g1, b1, g2, b2, ob, db):
        v = ref[...].astype(f32).reshape(1, 384)
        for k in range(3):
            small[row : row + 1, :] = v[:, k * 128 : (k + 1) * 128].astype(bf16)
            row += 1
    v = qb[...].astype(f32).reshape(1, 448)
    for k in range(3):
        small[row + k : row + k + 1, :] = v[:, k * 128 : (k + 1) * 128].astype(bf16)
        small[row + 5 + k : row + 6 + k, :] = v[:, 64 + k * 128 : 64 + (k + 1) * 128].astype(bf16)
    small[row + 3 : row + 4, 0:64] = v[:, 384:448].astype(bf16)
    small[row + 4 : row + 5, 64:128] = v[:, 0:64].astype(bf16)
    first[:416, :] = small[...]
    for k in range(3):
        first[416 + 384 * k : 800 + 384 * k, :] = up_w[:, k * 128 : (k + 1) * 128]


def pack_tokens_kernel(ids, x, dy, q_w, xd):
    tokens = x.shape[0]
    xd[:tokens] = x[...]
    xd[tokens : 2 * tokens] = dy[...]
    rows = q_w.shape[0] // 2
    xd[2 * tokens :, : 2 * rows] = q_w[:rows]
    xd[2 * tokens :, 2 * rows :] = q_w[rows:]


def pack_call(kernel, name, ids, args, specs, outs):
    return pl.pallas_call(
        kernel,
        out_shape=tuple(jax.ShapeDtypeStruct(s, bf16) for s in outs),
        grid_spec=pltpu.PrefetchScalarGridSpec(
            num_scalar_prefetch=1,
            grid=(1,),
            in_specs=specs,
            out_specs=[pl.BlockSpec(s, lambda i, s: (0, 0)) for s in outs],
        ),
        name=name,
        cost_estimate=pl.CostEstimate(
            flops=int(WEIGHT.get(name, 0) * 1e9) + 1, transcendentals=0, bytes_accessed=1
        ),
    )(ids, *args)


def pack(ids, qkv_weight, up_weight, vectors):
    half, width = qkv_weight.shape[0], 2 * qkv_weight.shape[0]
    step = up_weight.shape[1] // 8
    specs = [
        pl.BlockSpec((half, 128), lambda i, s: (0, width // 128)),
        pl.BlockSpec((half, step), lambda i, s: (0, (1 - s[1]) * 4 + s[2] * 2 + s[3])),
    ] + [pl.BlockSpec(v.shape, lambda i, s: (0,)) for v in vectors]
    outs = ((half + 32, 128), (half + 32 + 3 * half, 128))
    return pack_call(pack_kernel, "pack", ids, (qkv_weight, up_weight, *vectors), specs, outs)


def pack_tokens(ids, x, dy, qkv_weight):
    half, width = qkv_weight.shape[0], 2 * qkv_weight.shape[0]
    token = pl.BlockSpec(x.shape, lambda i, s: (0, 0))
    specs = [token, token, pl.BlockSpec((half, half), lambda i, s: (0, s[2]))]
    outs = ((2 * x.shape[0] + half // 2, width),)
    return pack_call(pack_tokens_kernel, "pack_tokens", ids, (x, dy, qkv_weight), specs, outs)


def row_vector(block, first, count=3):
    return jnp.concatenate([block[first + k : first + k + 1] for k in range(count)], axis=1)


def natural(side, own, other):
    return jnp.concatenate(
        [jnp.where(side == 0, own, other), jnp.where(side == 0, other, own)], axis=1
    )


def model_vector(side, own, other, index):
    return natural(side, row_vector(own, 3 * index), row_vector(other, 3 * index))


def qkv_bias_tiles(side, own, other):
    low = jnp.where(side == 0, own[18:22], other[18:22])
    high = jnp.where(side == 0, other[22:26], own[22:26])
    tiles = [low[0:1], low[1:2], low[2:3], low[3:4] + high[0:1], high[1:2], high[2:3], high[3:4]]
    return tiles


def normalize(values):
    centred = values - jnp.mean(values, axis=-1, keepdims=True)
    root = lax.rsqrt(jnp.mean(centred * centred, axis=-1, keepdims=True) + 1e-05)
    return centred * root, root


def turn(m, c, s1, s2):
    return m * c + pltpu.roll(m, 120, 1) * s1 + pltpu.roll(m, 8, 1) * s2


def kv_tables(c, s1, s2):
    key = lax.broadcasted_iota(jnp.int32, c.shape, 1) < 64
    return jnp.where(key, c, 1.0), jnp.where(key, s1, 0.0), jnp.where(key, s2, 0.0)


def front_kernel(ids, x, p_own, pu, c, s1, s2, first, kv, p_copy, up0):
    p_oth = pu.at[: p_own.shape[0]]
    p_copy[...] = p_oth[...]
    for k in range(3):
        up0[:, k * 128 : (k + 1) * 128] = pu[416 + 384 * k : 800 + 384 * k, :]
    side = ids[1]
    half = x.shape[1] // 2
    own, other = p_own[half:].astype(f32), p_oth[half:].astype(f32)
    hat, _ = normalize(x[...].astype(f32))
    first[...] = (hat * model_vector(side, own, other, 0) + model_vector(side, own, other, 1)).astype(bf16)
    m = mm(first[:, lanes(side * half, half)], p_own[:half])
    m += mm(first[:, lanes((1 - side) * half, half)], p_oth[:half])
    m += qkv_bias_tiles(side, own, other)[6]
    kv[...] = turn(m, *kv_tables(c[...], s1[...], s2[...])).astype(bf16)


def query_kernel(ids, first, w, w_mine, w_theirs, p_own, p_oth, c, s1, s2, q, w_copy, bias):
    side, core = ids[1], ids[2]
    half = first.shape[1] // 2
    tiles = qkv_bias_tiles(side, p_own[half:].astype(f32), p_oth[half:].astype(f32))
    bias[...] = jnp.concatenate(tiles[:6], axis=1)
    for ref, cb in ((w_mine, core), (w_theirs, 1 - core)):
        col = cb * half
        w_copy[:, lanes(col, half)] = ref[...]
        m = mm(first[:, lanes(side * half, half)], w[:, lanes(col, half)])
        m += mm(first[:, lanes((1 - side) * half, half)], ref[...])
        m += bias[:, lanes(col, half)]
        for k in range(half // 128):
            low = turn(m[:, k * 128 : (k + 1) * 128], c[...], s1[...], s2[...]).astype(bf16)
            q[:, lanes(col + k * 128, 128)] = (low.astype(f32) * 0.125).astype(bf16)


def cotangent_kernel(dy_own, xd, w, g_own, g_oth, q_mine):
    rows = q_mine.shape[0] // 2
    q_mine[:rows] = xd[2 * dy_own.shape[0] :, : 2 * rows]
    q_mine[rows:] = xd[2 * dy_own.shape[0] :, 2 * rows :]
    g_own[...] = mm(dy_own[...], w[...], NT).astype(bf16)
    g_oth[...] = mm(xd[dy_own.shape[0] : 2 * dy_own.shape[0]], w[...], NT).astype(bf16)


def ff_kernel(
    ids, x_own, xd, dy_own, up, up0, up1, up2, up3, down, up_bias, p_own, p_oth,
    keep_a, send_a, keep_b, send_b, act, dh, hat_oth, first_oth, hat_half, dy_copy, up_sum,
    a2, dy, bias, g_down, g_up, up_buf, down_buf, up_sem, down_sem,
):
    side, core, near_y = ids[1], ids[2], ids[3]
    tokens, width = x_own.shape
    x_oth, dy_oth = xd.at[:tokens], xd.at[tokens : 2 * tokens]
    half = width // 2
    wide = act.shape[1]
    step = wide // 4
    pieces = [
        (ref, (jnp.bitwise_xor(core, a) * 2 + jnp.bitwise_xor(near_y, b)), a, b)
        for ref, a, b in ((up0, 0, 0), (up1, 0, 1), (up2, 1, 0), (up3, 1, 1))
    ]

    def up_copy(i, piece):
        at = lanes(side * wide + piece * step, step)
        return pltpu.make_async_copy(up.at[:, at], up_buf.at[i], up_sem.at[i])

    def down_copy(i, piece):
        at = pl.ds(pl.multiple_of(piece * step, step), step)
        return pltpu.make_async_copy(down.at[at, :], down_buf.at[i], down_sem.at[i])

    for i, (_, piece, _, _) in enumerate(pieces):
        up_copy(i, piece).start()
        down_copy(i, piece).start()
    own, other = p_own[half:].astype(f32), p_oth[half:].astype(f32)
    gain1, shift1 = model_vector(side, own, other, 0), model_vector(side, own, other, 1)
    gain2, shift2 = model_vector(side, own, other, 2), model_vector(side, own, other, 3)
    mine, theirs = lanes(side * half, half), lanes((1 - side) * half, half)
    hat_own, _ = normalize(x_own[...].astype(f32))
    a2[:tokens] = (hat_own * gain2 + shift2).astype(bf16)
    hat_other, _ = normalize(x_oth[...].astype(f32))
    hat_oth[...] = hat_other
    a2[tokens:] = (hat_other * gain2 + shift2).astype(bf16)
    first_oth[...] = (hat_other * gain1 + shift1).astype(bf16)
    hat_half[...] = jnp.where(side == 0, hat_other[:, :half], hat_other[:, half:])
    dy[:tokens] = dy_own[...]
    dy[tokens:] = dy_oth[...]
    dy_copy[...] = dy_oth[...]
    bias[...] = up_bias[...].astype(f32).reshape(1, wide)
    rows = half // 4
    far = ids[0] // 4 % 4
    for i, (ref, piece, a, b) in enumerate(pieces):
        up_copy(i, piece).wait()
        down_copy(i, piece).wait()
        cols = lanes(piece * step, step)
        h = mm(a2[:, mine], up_buf[i])
        h += mm(a2[:, theirs], ref[...])
        h += bias[:, cols]
        phi = 0.5 * (1.0 + lax.erf(h * 0.7071067811865476))
        slope = phi + h * jnp.exp(-0.5 * h * h) * 0.3989422804014327
        g = (h * phi).astype(bf16)
        act[:, i * step : (i + 1) * step] = g
        d = mm(dy[...], down_buf[i], NT)
        e = (d * slope).astype(bf16)
        dh[:, i * step : (i + 1) * step] = e
        up_sum[:, cols] = jnp.sum(e.astype(f32), axis=0, keepdims=True)
        g_down[...] = mm(g, dy[...], TN).astype(bf16)
        g_up[:, :half] = mm(a2[:, mine], e, TN).astype(bf16)
        g_up[:, half:] = mm(a2[:, theirs], e, TN).astype(bf16)
        for k in range(4):
            z = jnp.bitwise_xor(far, (k & 1) * 2 + (k >> 1))
            at = pl.ds(pl.multiple_of(z * rows, rows), rows)
            slot = b * 4 + k
            (send_a if a else keep_a)[slot] = g_down[at, :]
            (send_b if a else keep_b)[slot] = g_up[at, :]


def ff_rest_kernel(
    ids, act, dh, x_own, hat_oth, up, up0, up1, up2, up3, down,
    ff_own, ff_oth, ds_own, ds_oth, n_mine, n_send, sums, up_buf, down_buf, up_sem, down_sem,
):
    side, core, near_y = ids[1], ids[2], ids[3]
    tokens, width = x_own.shape
    half = width // 2
    wide = act.shape[1]
    step = wide // 4
    order = ((0, 0), (0, 1), (1, 0), (1, 1))
    pieces = [jnp.bitwise_xor(core, a) * 2 + jnp.bitwise_xor(near_y, b) for a, b in order]
    copies = []
    for i, piece in enumerate(pieces):
        at = pl.ds(pl.multiple_of(piece * step, step), step)
        copies.append(pltpu.make_async_copy(down.at[at, :], down_buf.at[i], down_sem.at[i]))
        at = lanes(side * wide + piece * step, step)
        copies.append(pltpu.make_async_copy(up.at[:, at], up_buf.at[i], up_sem.at[i]))
    for copy in copies:
        copy.start()
    hat_own, _ = normalize(x_own[...].astype(f32))
    for copy in copies:
        copy.wait()
    out = sum(mm(act[:, i * step : (i + 1) * step], down_buf[i]) for i in range(4))
    ff_own[...] = out[:tokens]
    ff_oth[...] = out[tokens:]
    ds_mine = sum(mm(dh[:, i * step : (i + 1) * step], up_buf[i], NT) for i in range(4))
    ds_theirs = sum(
        mm(dh[:, i * step : (i + 1) * step], ref[...], NT) for i, ref in enumerate((up0, up1, up2, up3))
    )
    low = jnp.where(side == 0, ds_mine, ds_theirs)
    high = jnp.where(side == 0, ds_theirs, ds_mine)
    for part, ds in ((slice(0, half), low), (slice(half, width), high)):
        ds_own[:, part] = ds[:tokens]
        ds_oth[:, part] = ds[tokens:].astype(bf16)
        moved = ds[:tokens] * hat_own[:, part] + ds[tokens:] * hat_oth[:, part]
        sums[0:1, part] = jnp.sum(moved, axis=0, keepdims=True)
        sums[1:2, part] = jnp.sum(ds, axis=0, keepdims=True)
    split_rows(sums, 2, side, half, n_mine, n_send)


def split_rows(sums, count, side, half, mine, send):
    for ref, owner in ((mine, side), (send, 1 - side)):
        ref[...] = jnp.zeros_like(ref)
        for i in range(count):
            for k in range(half // 128):
                at = i * (half // 128) + k
                ref[at : at + 1, :] = sums[i : i + 1, lanes(owner * half + k * 128, 128)]


class Block:
    def __init__(self, stages, n_dev, docs, side, ids, len_ref):
        self.stages, self.n_dev, self.me, self.fsdp = stages, n_dev, ids[0], ids[1]
        self.block = ids[0] if side == 0 else 2 * n_dev - 1 - ids[0]
        self.rows = pl.ds(side * BLOCK, BLOCK)
        self.low = lax.broadcasted_iota(jnp.int32, (BLOCK, 128), 1) < 64
        base = self.block * BLOCK
        self.qpos = base + lax.broadcasted_iota(jnp.int32, (1, BLOCK), 1)
        total = first = jnp.int32(0)
        self.qstart = jnp.zeros((1, BLOCK), jnp.int32)
        for e in range(docs):
            size = len_ref[0, e]
            total = total + size
            self.qstart = self.qstart + jnp.where(total <= self.qpos, size, 0)
            first = first + jnp.where(total <= base, size, 0)
        self.steps = (base + BLOCK - first + 2 * BLOCK - 1) // (2 * BLOCK)

    def row_of(self, j):
        j = jnp.maximum(j, 0)
        dev = jnp.where(j < self.n_dev, j, 2 * self.n_dev - 1 - j)
        slot = slot_of(jnp.bitwise_xor(dev, self.me), self.stages)
        return pl.multiple_of((slot * 2 + jnp.where(j < self.n_dev, 0, 1)) * BLOCK, BLOCK)

    def columns(self, p, half):
        close = p < half // 128
        local = (p % (half // 128)) * 128
        return close, local, lanes((self.fsdp if close else 1 - self.fsdp) * half + local, 128)

    def half_turn(self, two):
        return pltpu.roll(two.astype(f32), 64, 1).astype(bf16)

    def spread_query(self, q_ref, qz):
        for p in range(q_ref.shape[1] // 128):
            two = q_ref[self.rows, self.columns(p, q_ref.shape[1] // 2)[2]]
            zero = jnp.zeros_like(two)
            qz[pl.ds(p * 256, 128), :] = jnp.where(self.low, two, zero)
            qz[pl.ds(p * 256 + 128, 128), :] = jnp.where(self.low, self.half_turn(two), zero)

    def load(self, t, kv_mine, kv_theirs, bias):
        middle = kv_mine.shape[0]
        parts, at = [], []
        hi = self.block - 2 * t
        for j in (hi - 1, hi):
            row = self.row_of(j)
            inner = pl.multiple_of(jnp.where(row < middle, row, row - middle), BLOCK)
            here = pl.ds(inner, BLOCK)
            parts.append(jnp.where(row < middle, kv_mine[here, :], kv_theirs[here, :]))
            at.append(row)
        kpos = (hi - 1) * BLOCK + lax.broadcasted_iota(jnp.int32, (2 * BLOCK, BLOCK), 0)
        ok = (kpos <= self.qpos) & (kpos >= self.qstart)
        bias[...] = jnp.where(ok, 0.0, -1e30)
        return jnp.concatenate(parts, axis=0), at


def attn_forward_kernel(
    stages, n_dev, docs, side, ids, len_ref, q_ref, kv_mine, kv_theirs, g_own, g_oth,
    o_own, o_oth, st, qz, ot, bias,
):
    me = Block(stages, n_dev, docs, side, ids, len_ref)
    half = q_ref.shape[1] // 2
    pairs = q_ref.shape[1] // 128
    me.spread_query(q_ref, qz)
    ot[...] = jnp.zeros_like(ot)
    st[0] = jnp.full(st.shape[1:], -1e30, f32)
    st[1] = jnp.zeros(st.shape[1:], f32)

    def forward(t, carry):
        kvb, _ = me.load(t, kv_mine, kv_theirs, bias)
        vt = kvb.astype(f32).T.astype(bf16)[64:]
        mask = bias[...]
        for p in range(pairs):
            s2 = mm(kvb, qz[pl.ds(p * 256, 256), :], NT)
            for i in range(2):
                h = 2 * p + i
                s = s2[:, i * 128 : (i + 1) * 128] + mask
                old = st[0, h : h + 1, :]
                new = jnp.maximum(old, jnp.max(s, axis=0, keepdims=True))
                e = jnp.exp(s - new)
                alpha = jnp.exp(old - new)
                st[0, h : h + 1, :] = new
                st[1, h : h + 1, :] = st[1, h : h + 1, :] * alpha + jnp.sum(e, axis=0, keepdims=True)
                hs = pl.ds(h * 64, 64)
                ot[hs, :] = ot[hs, :] * alpha + mm(vt, e.astype(bf16))
        return 0

    lax.fori_loop(0, me.steps, forward, 0)
    for p in range(pairs):
        close, local, _ = me.columns(p, half)
        gt = (g_own if close else g_oth)[me.rows, pl.ds(local, 128)].astype(f32).T
        halves = []
        for i in range(2):
            h = 2 * p + i
            l = st[1, h : h + 1, :]
            o = ot[pl.ds(h * 64, 64), :] / l
            halves.append(o)
            st[2, h : h + 1, :] = jnp.sum(o * gt[i * 64 : (i + 1) * 64], axis=0, keepdims=True)
            st[0, h : h + 1, :] = st[0, h : h + 1, :] + jnp.log(l)
        (o_own if close else o_oth)[:, pl.ds(local, 128)] = jnp.concatenate(halves, axis=0).T.astype(bf16)


def attn_backward_kernel(stages, n_dev, docs, side, last, *refs):
    ids, len_ref, q_ref, kv_mine, kv_theirs, g_own, g_oth, st, cos_ref, sin_ref = refs[:10]
    if not last:
        dm_ref, acc, qz, gz, dqt, bias, ds_sc, p_sc = refs[10:]
        acc[...] = jnp.zeros_like(acc)
    else:
        before, dm_ref, dkv_keep, dkv_send, qz, gz, dqt, bias, ds_sc, p_sc, acc = refs[10:]
        acc[...] = before[...]
    me = Block(stages, n_dev, docs, side, ids, len_ref)
    half = q_ref.shape[1] // 2
    pairs = q_ref.shape[1] // 128
    me.spread_query(q_ref, qz)
    for p in range(pairs):
        close, local, _ = me.columns(p, half)
        two = (g_own if close else g_oth)[me.rows, pl.ds(local, 128)]
        zero = jnp.zeros_like(two)
        gz[pl.ds(p * 256, 128), :] = jnp.where(me.low, zero, me.half_turn(two))
        gz[pl.ds(p * 256 + 128, 128), :] = jnp.where(me.low, zero, two)
    dqt[...] = jnp.zeros_like(dqt)

    def backward(t, carry):
        kvb, at = me.load(t, kv_mine, kv_theirs, bias)
        kt = kvb.astype(f32).T.astype(bf16)[:64]
        mask = bias[...]
        for p in range(pairs):
            s2 = mm(kvb, qz[pl.ds(p * 256, 256), :], NT)
            dp2 = mm(kvb, gz[pl.ds(p * 256, 256), :], NT)
            for i in range(2):
                h = 2 * p + i
                sl = slice(i * 128, (i + 1) * 128)
                pr = jnp.exp((s2[:, sl] + mask) - st[0, h : h + 1, :])
                ds = pr * (dp2[:, sl] - st[2, h : h + 1, :])
                ds_sc[:, h * 128 : (h + 1) * 128] = ds.astype(bf16)
                p_sc[:, h * 128 : (h + 1) * 128] = pr.astype(bf16)
        part = mm(ds_sc[...], qz[...]) + mm(p_sc[...], gz[...])
        for i in range(2):
            acc[pl.ds(at[i], BLOCK), :] += part[i * BLOCK : (i + 1) * BLOCK]
        dqt[...] += mm(kt, ds_sc[...])
        return 0

    lax.fori_loop(0, me.steps, backward, 0)
    cos = cos_ref[side]
    sin = sin_ref[side]
    for p in range(pairs):
        halves = []
        for i in range(2):
            h = 2 * p + i
            g = dqt[:, h * 128 : (h + 1) * 128] * 0.125
            g0, g1 = g[:8], g[8:16]
            halves += [g0 * cos + g1 * sin, g1 * cos - g0 * sin, g[16:]]
        dm_ref[:, me.columns(p, half)[2]] = jnp.concatenate(halves, axis=0).T.astype(bf16)
    if last:
        middle = dkv_keep.shape[0]
        dkv_keep[...] = acc[:middle].astype(bf16)
        dkv_send[...] = acc[middle:].astype(bf16)


def attn_forward(side, stages, n_dev, ids, lengths, q, kv, g_own, g_oth):
    width = q.shape[1]
    block = q.shape[0] // 2
    rows = width // 64 * 128
    kv = near(*kv) if n_dev <= LOW else kv
    return call(
        partial(attn_forward_kernel, stages, n_dev, lengths.shape[1], side),
        "attn_forward",
        [((block, width // 2), bf16, False), ((block, width // 2), bf16, True), ((3, 16, 128), f32, True)],
        (ids, lengths, *near(q), *kv, g_own, *near(g_oth)),
        scratch=[pltpu.VMEM((rows, 128), bf16), pltpu.VMEM((width, 128), f32), pltpu.VMEM((256, 128), f32)],
        room=6 + (0 if n_dev <= LOW else kv[0].size * 4 // 2**20),
    )


def attn_backward(side, stages, n_dev, ids, lengths, q, kv, g_own, g_oth, st, cos, sin, before=()):
    width = q.shape[1]
    block = q.shape[0] // 2
    middle = kv[0].shape[0]
    rows = width // 64 * 128
    small = n_dev <= LOW
    close = near if small else (lambda *values: values)
    outs = [((block, width), bf16, True)]
    last = len(before) > 0
    outs += [((middle, 128), bf16, True)] * 2 if last else [((2 * middle, 128), f32, small)]
    scratch = [
        pltpu.VMEM((rows, 128), bf16),
        pltpu.VMEM((rows, 128), bf16),
        pltpu.VMEM((64, rows), f32),
        pltpu.VMEM((256, 128), f32),
        pltpu.VMEM((256, rows), bf16),
        pltpu.VMEM((256, rows), bf16),
    ]
    if last:
        scratch += [pltpu.VMEM((2 * middle, 128), f32)]
    return call(
        partial(attn_backward_kernel, stages, n_dev, lengths.shape[1], side, last),
        "attn_backward",
        outs,
        (ids, lengths, *near(q), *close(*kv), g_own, *near(g_oth, st), cos, sin, *close(*before)),
        scratch=scratch,
        room=8 + 2 * middle * 128 * (4 if small else 7) // 2**20,
    )


def pile_kernel(a0, a1, b0, b1, c0, c1, *outs):
    for out, parts in zip(outs, ((a0, a1), (b0, b1), (c0, c1))):
        rows = parts[0].shape[0]
        out[:rows] = parts[0][...]
        out[rows:] = parts[1][...]


def mix_kernel(ff, o, w, out):
    out[...] = (ff[...] + mm(o[...], w[...])).astype(bf16)


def result_kernel(ids, x, ff, o, w, recv, p_own, p_oth, out):
    side = ids[1]
    half = x.shape[1] // 2
    own, other = p_own[half:].astype(f32), p_oth[half:].astype(f32)
    y = x[...].astype(f32) + (ff[...] + mm(o[...], w[...])) + recv[...].astype(f32)
    y += model_vector(side, own, other, 4) + model_vector(side, own, other, 5)
    out[...] = y.astype(bf16)


def dm_kv_kernel(*refs):
    later, c, s1, s2, out = refs[-5:]
    total = later[...]
    for ref in refs[:-5]:
        total = total + ref[...].astype(f32)
    c, s1, s2 = kv_tables(c[...], s1[...], s2[...])
    out[...] = turn(total, c, -s1, -s2).astype(bf16)


def x_grad_kernel(ids, x, dy, dm, dm_kv, w, w_oth, p_own, p_oth, ds, ds_recv, out, da):
    side = ids[1]
    width = x.shape[1]
    half = width // 2
    own, other = p_own[half:].astype(f32), p_oth[half:].astype(f32)
    mine, theirs = lanes(side * half, half), lanes((1 - side) * half, half)
    da[:, mine] = mm(dm[...], w[:, :width], NT) + mm(dm_kv[...], p_own[:half], NT)
    da[:, theirs] = mm(dm[...], w_oth[...], NT) + mm(dm_kv[...], p_oth[:half], NT)
    hat, root = normalize(x[...].astype(f32))
    total = dy[...].astype(f32)
    for i, grad in enumerate((da[...], ds[...] + ds_recv[...].astype(f32))):
        up = grad * model_vector(side, own, other, 2 * i)
        total += root * (
            up - jnp.mean(up, axis=-1, keepdims=True) - hat * jnp.mean(up * hat, axis=-1, keepdims=True)
        )
    out[...] = total


def pair_kernel(ids, f_own, f_oth, dm_own, dm_oth, o_own, o_oth, dy_own, dy_oth, keep, send, gq, go):
    side, core = ids[1], ids[2]
    half = f_own.shape[1] // 2
    mine = lanes(side * half, half)
    gq[...] = mm(f_own[:, mine], dm_own[...], TN) + mm(f_oth[:, mine], dm_oth[...], TN)
    go[...] = mm(o_own[...], dy_own[...], TN) + mm(o_oth[...], dy_oth[...], TN)
    rows = half // 8
    close = ids[0] % LOW // 2
    for ref, cb in ((keep, core), (send, 1 - core)):
        cols = lanes(cb * half, half)
        for k in range(8):
            at = pl.ds(pl.multiple_of(jnp.bitwise_xor(close, CHUNKS[k]) * rows, rows), rows)
            ref[k * rows : (k + 1) * rows, 0:half] = gq[at, cols].astype(bf16)
            ref[k * rows : (k + 1) * rows, half:] = go[at, cols].astype(bf16)


def tail_kernel(
    ids, f_own, f_oth, dm_own, dm_oth, dy_own, dy_oth, kv_own, kv_oth, n_mine, n_recv, up_sum,
    x_own, hat_half, w, p_own, out, tail, hat,
):
    side = ids[1]
    half = f_own.shape[1] // 2
    mine = lanes(side * half, half)
    tail[:half] = mm(f_own[:, mine], kv_own[...], TN) + mm(f_oth[:, mine], kv_oth[...], TN)
    tail[half:] = jnp.zeros((32, 128), f32)
    gain = shift = 0.0
    hat[...] = normalize(x_own[...].astype(f32))[0]
    for x, dm, kv in ((hat[:, mine], dm_own, kv_own), (hat_half[...], dm_oth, kv_oth)):
        grad = mm(dm[...], w[:, : 2 * half], NT) + mm(kv[...], p_own[:half], NT)
        gain += jnp.sum(grad * x, axis=0, keepdims=True)
        shift += jnp.sum(grad, axis=0, keepdims=True)
    row = half
    for v in (gain, shift):
        for k in range(3):
            tail[row + k : row + k + 1, :] = v[:, k * 128 : (k + 1) * 128]
        row += 3
    v = n_mine[...] + n_recv[...]
    tail[row : row + 6] = v[:6]
    row += 6

    def total(a, b):
        return jnp.sum(a.astype(f32), axis=0, keepdims=True) + jnp.sum(b.astype(f32), axis=0, keepdims=True)

    v = total(dy_own[:, mine], dy_oth[:, mine])
    for k in range(3):
        tail[row + k : row + k + 1, :] = v[:, k * 128 : (k + 1) * 128]
    row += 3
    v = jnp.concatenate([total(dm_own[...], dm_oth[...]), total(kv_own[...], kv_oth[...])], axis=1)
    moved = jnp.concatenate([v[:, 448:], v[:, :448]], axis=1)
    v = jnp.where(side == 0, v, moved)
    for k in range(4):
        tail[row + k : row + k + 1, :] = v[:, k * 128 : (k + 1) * 128]
    row += 4
    for k in range(12):
        tail[row + k : row + k + 1, :] = up_sum[:, k * 128 : (k + 1) * 128]
    out[...] = tail[...].astype(bf16)


def sum_kernel(*refs):
    total = refs[0][...].astype(f32)
    for ref in refs[1:-1]:
        total = total + ref[...].astype(f32)
    refs[-1][...] = total.astype(refs[-1].dtype)


def sum_of(first, second, name):
    return call(sum_kernel, name, [(first.shape, first.dtype, True)], near(first, second))[0]


def up_part_kernel(a, b, own, other):
    half = own.shape[-1]
    total = a[...].astype(f32) + b[...].astype(f32)
    own[...] = total[..., :half].astype(bf16)
    other[...] = total[..., half:].astype(bf16)


def up_join_kernel(own, other, out):
    half = own.shape[-1]
    out[..., :half] = own[...]
    out[..., half:] = other[...]


def chunk_of(ids, other_core, slot):
    core, near_y, far = ids[2], ids[3], ids[0] // 4 % 4
    piece = jnp.bitwise_xor(core, other_core) * 2 + jnp.bitwise_xor(near_y, slot >> 2)
    return piece, jnp.bitwise_xor(far, (slot & 1) * 2 + (slot >> 1 & 1))


def down_out_kernel(ids, mine, theirs, out):
    rows = mine.shape[1]
    for a, ref in enumerate((mine, theirs)):
        for k in range(8):
            piece, z = chunk_of(ids, a, k)
            out[pl.ds(pl.multiple_of((piece * 4 + z) * rows, rows), rows), :] = ref[k].astype(f32)


def up_out_kernel(ids, mine, theirs, out):
    side = ids[1]
    rows = mine.shape[1]
    half = mine.shape[2] // 2
    wide = out.shape[1] // 2
    for a, ref in enumerate((mine, theirs)):
        for k in range(8):
            piece, z = chunk_of(ids, a, k)
            at = pl.ds(pl.multiple_of(z * rows, rows), rows)
            for j, owner in ((0, side), (1, 1 - side)):
                part = ref[k, :, j * half : (j + 1) * half].astype(f32)
                out[at, lanes(owner * wide + piece * half, half)] = part


def attn_out_kernel(ids, p_mine, p_theirs, tail, g_qkv, g_out, n0, n1, n2, n3, qb, ob, ub, db):
    core = ids[2]
    close = ids[0] % LOW // 2
    half = g_qkv.shape[0]
    rows = half // 8
    for ref, cb in ((p_mine, core), (p_theirs, 1 - core)):
        cols = lanes(cb * half, half)
        for k in range(8):
            at = pl.ds(pl.multiple_of(jnp.bitwise_xor(close, CHUNKS[k]) * rows, rows), rows)
            part = ref[k * rows : (k + 1) * rows, :].astype(f32)
            g_qkv[at, cols] = part[:, :half]
            g_out[at, cols] = part[:, half:]
    g_qkv[:, 2 * half :] = tail[:half].astype(f32)
    small = tail[half:].astype(f32)
    for i, ref in enumerate((n0, n1, n2, n3, ob)):
        ref[...] = row_vector(small, 3 * i).reshape(half)
    db[...] = row_vector(small, 12).reshape(half)
    qb[...] = row_vector(small, 15, 4)[:, : qb.shape[0]].reshape(qb.shape[0])
    ub[...] = row_vector(small, 19, 12).reshape(ub.shape[0])


class Values:
    pass


def body(
    layer_input, doc_lengths, ln1_gain, ln1_bias, ln2_gain, ln2_bias, qkv_weight, qkv_bias,
    out_weight, out_bias, up_weight, up_bias, down_weight, down_bias, out_grad, kv_grad_later,
):
    devices = lax.axis_size("ctx")
    me = lax.axis_index("ctx").astype(jnp.int32)
    side = lax.axis_index("fsdp").astype(jnp.int32)
    ids = jnp.stack([me, side, me % 2, me // 2 % 2])
    tokens, width = layer_input.shape[1:]
    half_rows = tokens // 2
    half = width // 2
    wide = up_weight.shape[1] // 2
    stages = stages_of(devices)
    x_own, dy_own = layer_input[0], out_grad[0]

    vectors = (ln1_gain, ln1_bias, ln2_gain, ln2_bias, out_bias, down_bias, qkv_bias)
    p_own, pu_own = pack(ids, qkv_weight, up_weight, vectors)
    pu_oth = swap_x(pu_own)
    xd_own = pack_tokens(ids, x_own, dy_own, after(qkv_weight, pu_own))[0]
    xd = swap_x(after(xd_own, pu_oth))

    offsets = jnp.arange(half_rows, dtype=jnp.int32)
    places = jnp.concatenate([me * half_rows + offsets, (2 * devices - 1 - me) * half_rows + offsets]).astype(f32)
    half_rot = ROT // 2
    freq = 10000.0 ** (-jnp.arange(half_rot, dtype=f32) / half_rot)
    lane = np.arange(128)
    angles = places[:, None] * jnp.tile(freq, 128 // half_rot)[None, :]
    cosine, sine = jnp.cos(angles), jnp.sin(angles)
    tables = (
        jnp.where(lane % 64 < 16, cosine, 1.0),
        jnp.where(lane % 64 < 8, -sine, 0.0),
        jnp.where((lane % 64 >= 8) & (lane % 64 < 16), sine, 0.0),
    )
    t_angles = places.reshape(2, 1, half_rows) * freq[None, :, None]
    cos_t, sin_t = jnp.cos(t_angles), jnp.sin(t_angles)

    low = min(LOW, devices)
    rows = half // 4
    step = wide // 4
    token_f32, token_low = ((tokens, width), f32, False), ((tokens, width), bf16, False)
    e = Values()
    e.o, e.o_send, e.st, e.dm = {}, {}, {}, {}
    e.down, e.up, e.kv, e.pair, e.tail = (Values() for _ in range(5))

    def front():
        e.first_own, kv, e.p_oth, up0 = call(
            front_kernel,
            "front",
            [
                ((tokens, width), bf16, False), ((tokens, 128), bf16, True), (p_own.shape, bf16, False),
                ((half, half), bf16, True),
            ],
            (ids, x_own, p_own, *near(pu_oth), *tables),
        )
        up1 = swap_ctx(up0, 2)
        e.ups = (up0, up1, swap_ctx(up0, 1), swap_ctx(up1, 1))
        for stride, _ in stages[:-1]:
            kv = gather_step(kv, stride, "kv_join")
        e.kv_all = (kv, swap_ctx(kv, 1))

    def cotangent():
        e.g_own, g_send, e.q_mine = call(
            cotangent_kernel,
            "cotangent",
            [((tokens, half), bf16, False), ((tokens, half), bf16, True), ((half, half), bf16, True)],
            (dy_own, *near(xd), out_weight),
        )
        e.g_oth = swap_x(g_send)
        e.q_theirs = swap_ctx(e.q_mine, 1)

    def ff():
        chunks = ((8, rows, width), bf16, True)
        (
            keep_a, send_a, keep_b, send_b, e.act, e.dh, e.hat_oth, e.first_oth, e.hat_half,
            e.dy_far, e.up_sum,
        ) = call(
            ff_kernel,
            "ff",
            [
                chunks, chunks, chunks, chunks, ((2 * tokens, wide), bf16, True), ((2 * tokens, wide), bf16, True),
                token_f32, token_low, ((tokens, half), f32, False), token_low, ((1, wide), f32, False),
            ],
            (
                ids, x_own, *near(xd), dy_own, Raw(up_weight), *near(*e.ups), Raw(down_weight), up_bias, p_own,
                e.p_oth,
            ),
            scratch=[
                pltpu.VMEM((2 * tokens, width), bf16),
                pltpu.VMEM((2 * tokens, width), bf16),
                pltpu.VMEM((1, wide), f32),
                pltpu.VMEM((half, width), bf16),
                pltpu.VMEM((half, width), bf16),
                pltpu.VMEM((4, half, step), bf16),
                pltpu.VMEM((4, step, width), bf16),
                pltpu.SemaphoreType.DMA((4,)),
                pltpu.SemaphoreType.DMA((4,)),
            ],
            room=16,
        )
        e.down.parts, e.up.parts = (keep_a, swap_ctx(send_a, 1)), (keep_b, swap_ctx(send_b, 1))

    def add_step(chain, mask, name):
        kept, arrived = chain.parts
        out = ((kept.shape[0] // 2,) + kept.shape[1:], kept.dtype, True)
        kept, send = call(add_split_kernel, name, [out, out], near(kept, arrived))
        chain.parts = (kept, swap_ctx(send, mask))

    def join_step(chain, mask, name):
        value, arrived = chain.parts
        value = join(value, arrived, name)
        chain.parts = (value, swap_ctx(value, mask))

    def query():
        e.q, e.q_far = call(
            query_kernel,
            "query",
            [((tokens, width), bf16, True), ((half, width), bf16, False)],
            (ids, e.first_own, qkv_weight, *near(e.q_mine, e.q_theirs), p_own, e.p_oth, *tables),
            scratch=[pltpu.VMEM((1, width), f32)],
        )

    pairs = (stages, devices, ids, doc_lengths)

    def forward(side):
        e.o[side], e.o_send[side], e.st[side] = attn_forward(
            side, *pairs, e.q, e.kv_all, e.g_own, e.g_oth
        )

    def backward(side):
        before = (e.dkv,) if side == 1 and devices <= LOW else ()
        e.dm[side], *dkv = attn_backward(
            side, *pairs, e.q, e.kv_all, e.g_own, e.g_oth, e.st[side], cos_t, sin_t, before=before
        )
        if side == 0:
            e.dkv = dkv[0]
            return
        if devices > LOW:
            dkv = (e.dkv + dkv[0]).astype(bf16)
            middle = dkv.shape[0] // 2
            dkv = (dkv[:middle], dkv[middle:])
        e.kv.parts = (dkv[0], swap_ctx(dkv[1], 1))

    def pile():
        e.o_own, o_send, e.dm_own = call(
            pile_kernel,
            "pile",
            [((tokens, half), bf16, False), ((tokens, half), bf16, True), ((tokens, width), bf16, True)],
            (e.o[0], e.o[1], *near(e.o_send[0], e.o_send[1], e.dm[0], e.dm[1])),
        )
        e.dm_oth, e.o_oth = swap_x(e.dm_own), swap_x(o_send)

    def kv_more():
        stride = 16
        while stride < devices:
            add_step(e.kv, stride, "kv_add")
            stride *= 2

    def ff_rest():
        row_block = ((8, 128), f32, False)
        e.ff_own, e.ff_oth, e.ds_own, ds_oth, e.n_mine, n_send = call(
            ff_rest_kernel,
            "ff_rest",
            [token_f32, token_f32, token_f32, token_low, row_block, row_block],
            (ids, *near(e.act, e.dh), x_own, e.hat_oth, Raw(up_weight), *near(*e.ups), Raw(down_weight)),
            scratch=[
                pltpu.VMEM((8, width), f32),
                pltpu.VMEM((4, half, step), bf16),
                pltpu.VMEM((4, step, width), bf16),
                pltpu.SemaphoreType.DMA((4,)),
                pltpu.SemaphoreType.DMA((4,)),
            ],
            room=18,
        )
        e.n_recv, e.ds_recv = swap_x(n_send), swap_x(ds_oth)

    def down_sum():
        value = high_sum(sum_of(*e.down.parts, "down_sum"))
        e.down.parts = (value, swap_ctx(value, low // 2))

    def up_part():
        part = ((1, rows, half), bf16, True)
        own, send = call(up_part_kernel, "up_part", [part, part], near(*e.up.parts))
        own, send = high_sum(own), high_sum(send)
        e.up.parts = (own, swap_x(send))

    def up_join():
        value = call(up_join_kernel, "up_join", [((1, rows, width), bf16, True)], near(*e.up.parts))[0]
        e.up.parts = (value, swap_ctx(value, low // 2))

    def pair():
        keep, send = call(
            pair_kernel,
            "pair",
            [((half, width), bf16, True), ((half, width), bf16, True)],
            (
                ids, e.first_own, e.first_oth, *near(e.dm_own, e.dm_oth), e.o_own, *near(e.o_oth),
                dy_own, e.dy_far,
            ),
            scratch=[pltpu.VMEM((half, width), f32), pltpu.VMEM((half, width), f32)],
            room=8,
        )
        e.pair.parts = (keep, swap_ctx(send, 1))

    def pair_sum():
        value = high_sum(sum_of(*e.pair.parts, "pair_sum"))
        e.pair.parts = (value, swap_ctx(value, low // 2))

    def mix():
        y_send = call(
            mix_kernel, "mix", [((tokens, width), bf16, True)], (e.ff_oth, *near(e.o_oth), out_weight)
        )[0]
        e.y_recv = swap_x(y_send)

    def result():
        e.result = call(
            result_kernel,
            "result",
            [token_low],
            (ids, x_own, e.ff_own, e.o_own, out_weight, *near(e.y_recv), p_own, e.p_oth),
        )[0]

    def dm_kv():
        e.dm_kv = call(
            dm_kv_kernel, "dm_kv", [((tokens, 128), bf16, True)], (*near(*e.kv.parts), kv_grad_later[0], *tables)
        )[0]
        e.dm_kv_oth = swap_x(e.dm_kv)

    def x_grad():
        e.x_grad = call(
            x_grad_kernel,
            "x_grad",
            [token_f32],
            (
                ids, x_own, dy_own, *near(e.dm_own, e.dm_kv), qkv_weight, e.q_far, p_own, e.p_oth,
                e.ds_own, *near(e.ds_recv),
            ),
            scratch=[pltpu.VMEM((tokens, width), f32)],
            room=8,
        )[0]

    def tail():
        value = call(
            tail_kernel,
            "tail",
            [((half + 32, 128), bf16, True)],
            (
                ids, e.first_own, e.first_oth, *near(e.dm_own, e.dm_oth), dy_own, e.dy_far,
                *near(e.dm_kv, e.dm_kv_oth), e.n_mine, *near(e.n_recv), e.up_sum, x_own,
                e.hat_half, qkv_weight, p_own,
            ),
            scratch=[pltpu.VMEM((half + 32, 128), f32), pltpu.VMEM((tokens, width), f32)],
            room=8,
        )[0]
        e.tail.parts = (value, swap_ctx(value, 1))

    def tail_step(stride):
        value = sum_of(*e.tail.parts, "tail_sum")
        e.tail.parts = (value, swap_ctx(value, stride)) if stride < devices else (value,)

    def tail_last():
        stride = 16
        while stride < devices:
            tail_step(stride)
            stride *= 2
        tail_step(devices)

    def down_out():
        e.g_down = call(down_out_kernel, "down_out", [((wide, width), f32, False)], (ids, *near(*e.down.parts)), room=8)[0]

    def up_out():
        e.g_up = call(up_out_kernel, "up_out", [((half, 2 * wide), f32, False)], (ids, *near(*e.up.parts)), room=8)[0]

    def attn_out():
        vec = ((half,), f32, False)
        e.small = call(
            attn_out_kernel,
            "attn_out",
            [
                ((half, width + 128), f32, False), ((half, width), f32, False), vec, vec, vec, vec,
                (qkv_bias.shape, f32, False), vec, (up_bias.shape, f32, False), vec,
            ],
            (ids, *near(*e.pair.parts), *near(*e.tail.parts)),
            room=6,
        )

    def steps(function, chain, masks, name):
        return [partial(function, chain, mask, name) for mask in masks]

    halves, shares = (2, 4, 8), (low // 4, low // 8, low // 16)
    down_add, up_add = steps(add_step, e.down, halves, "down_add"), steps(add_step, e.up, halves, "up_add")
    pair_add, kv_add = steps(add_step, e.pair, halves, "pair_add"), steps(add_step, e.kv, halves, "kv_add")
    down_join, up_join_steps = steps(join_step, e.down, shares, "down_join"), steps(join_step, e.up, shares, "up_join")
    pair_join = steps(join_step, e.pair, shares, "pair_join")
    tail_add = [partial(tail_step, mask) for mask in halves]
    order = [
        front, cotangent, ff, down_add[0], up_add[0], query, partial(forward, 0), down_add[1],
        partial(backward, 0), down_add[2], up_add[1], partial(forward, 1), partial(backward, 1), pile,
        kv_add[0], down_sum, up_add[2], ff_rest, kv_add[1], pair, up_part, down_join[0], mix, pair_add[0],
        kv_add[2], kv_more, up_join, dm_kv, pair_add[1], down_join[1], up_join_steps[0], pair_add[2], tail, x_grad,
        tail_add[0], pair_sum, up_join_steps[1], tail_add[1], result, down_join[2], pair_join[0], pair_join[1],
        tail_add[2], up_join_steps[2], tail_last, pair_join[2], attn_out, down_out, up_out,
    ]
    CHAIN.clear()
    for run in order:
        run()
    CHAIN.clear()
    result, grad_inputs, g_down, g_up = e.result, e.x_grad, e.g_down, e.g_up
    g_qkv, g_out, *small = e.small
    n0, n1, n2, n3, qb, ob, ub, db = small
    return (result[None], grad_inputs[None], n0, n1, n2, n3, g_qkv, qb, g_out, ob, g_up, ub, g_down, db)


def solution(mesh):
    token = P("fsdp", "ctx", None)
    vec = P("fsdp")
    mat = P("fsdp", None)
    return jax.shard_map(
        body,
        mesh=mesh,
        in_specs=(token, mat, vec, vec, vec, vec, mat, vec, mat, vec, mat, vec, mat, vec, token, token),
        out_specs=(token, token, vec, vec, vec, vec, mat, vec, mat, vec, mat, vec, mat, vec),
        check_vma=False,
    )
```

```python
from functools import partial

import jax
import jax.numpy as jnp
import numpy as np
from jax import lax
from jax.experimental import pallas as pl
from jax.experimental.pallas import tpu as pltpu
from jax.sharding import PartitionSpec as P

ROT = 16
BLOCK = 128
LOW = 16
NT = (((1,), (1,)), ((), ()))
NN = (((1,), (0,)), ((), ()))
TN = (((0,), (0,)), ((), ()))
bf16 = jnp.bfloat16
f32 = jnp.float32
WEIGHT = {'pile': 8.0, 'up_add': 1.0, 'down_join': 6.0, 'dm_kv': 2.0, 'pair_sum': 4.0, 'ff_rest': 2.0, 'mix': 0.0, 'tail': 0.0}
TINY = pl.CostEstimate(flops=1, transcendentals=0, bytes_accessed=1)


def mm(left, right, dims=NN):
    return lax.dot_general(left, right, dims, preferred_element_type=f32)


def vmem():
    return pl.BlockSpec(memory_space=pltpu.VMEM)


def smem():
    return pl.BlockSpec(memory_space=pltpu.SMEM)


CHAIN = []


class Near:
    def __init__(self, value):
        self.value = value


class Raw(Near):
    pass


def near(*values):
    return tuple(Near(v) for v in values)


def call(kernel, name, outs, args, scratch=(), room=2):
    args = list(args)
    if CHAIN:
        at = next(i for i, v in enumerate(args) if not isinstance(v, Raw) and getattr(v, "dtype", f32) != jnp.int32)
        v = args[at]
        args[at] = Near(after(v.value, CHAIN[0])) if isinstance(v, Near) else after(v, CHAIN[0])
    specs = [vmem() for _ in args]
    values = list(args)
    for i, v in enumerate(args):
        if isinstance(v, Raw):
            values[i] = v.value
            specs[i] = pl.BlockSpec(memory_space=pl.ANY)
        elif isinstance(v, Near):
            values[i] = pltpu.with_memory_space_constraint(v.value, pltpu.VMEM)
        elif v.dtype == jnp.int32:
            specs[i] = smem()
    if lax.axis_size("ctx") > LOW and name[:4] != "attn":
        room += sum(int(np.prod(s)) * jnp.dtype(d).itemsize for s, d, _ in outs) >> 20
    results = pl.pallas_call(
        kernel,
        out_shape=tuple(pltpu.VMEM(s, d) if n else jax.ShapeDtypeStruct(s, d) for s, d, n in outs),
        in_specs=specs,
        out_specs=tuple(vmem() for _ in outs),
        scratch_shapes=list(scratch),
        name=name,
        cost_estimate=pl.CostEstimate(
            flops=int(WEIGHT.get(name, 0) * 1e9) + 1, transcendentals=0, bytes_accessed=1
        ),
        compiler_params=pltpu.CompilerParams(vmem_limit_bytes=room << 20),
    )(*values)
    CHAIN[:] = [results[0]]
    return results


def lanes(start, size):
    return pl.ds(pl.multiple_of(start, 128), size)


def swap_x(value):
    return lax.ppermute(value, "fsdp", [(0, 1), (1, 0)])


def swap_ctx(value, mask):
    devices = lax.axis_size("ctx")
    return lax.ppermute(value, "ctx", [(i, i ^ mask) for i in range(devices)])


def stages_of(devices):
    out, stride = [], 1
    while stride < devices:
        out.append((stride, 2))
        stride *= 2
    return out[::-1]


CHUNKS = [int(f"{k:03b}"[::-1], 2) for k in range(8)]


def slot_of(relative, stages):
    slot, count = relative * 0, 1
    for stride, size in stages:
        slot = slot + relative // stride % size * count
        count *= size
    return slot


def join_kernel(*refs):
    out = refs[-1]
    rows = refs[0].shape[0]
    for k, ref in enumerate(refs[:-1]):
        out[k * rows : (k + 1) * rows] = ref[...]


def join(first, second, name):
    shape = (2 * first.shape[0],) + first.shape[1:]
    return call(join_kernel, name, [(shape, first.dtype, True)], near(first, second))[0]


def gather_step(value, mask, name):
    return join(value, swap_ctx(value, mask), name)


def after(value, *others):
    return lax.optimization_barrier((value, *others))[0]


def add_split_kernel(a_ref, b_ref, keep, send):
    half = a_ref.shape[0] // 2
    for ref, part in ((keep, slice(0, half)), (send, slice(half, 2 * half))):
        ref[...] = (a_ref[part].astype(f32) + b_ref[part].astype(f32)).astype(ref.dtype)


def scatter_step(keep, send, mask, name):
    shape = (keep.shape[0] // 2,) + keep.shape[1:]
    out = (shape, keep.dtype, True)
    return call(add_split_kernel, name, [out, out], near(keep, swap_ctx(send, mask)))


def scatter(keep, send, devices, name, stride=1):
    while 2 * stride < devices:
        keep, send = scatter_step(keep, send, stride, name)
        stride *= 2
    return keep, swap_ctx(send, stride)


def high_sum(value):
    devices = lax.axis_size("ctx")
    if devices <= LOW:
        return value
    groups = [[h * LOW + l for h in range(devices // LOW)] for l in range(LOW)]
    return lax.psum(value, "ctx", axis_index_groups=groups)


def pack_kernel(ids, kv_w, up_w, g1, b1, g2, b2, ob, db, qb, small, first):
    small[:384, :] = kv_w[...]
    small[384:, :] = jnp.zeros((32, 128), bf16)
    row = 384
    for ref in (g1, b1, g2, b2, ob, db):
        v = ref[...].astype(f32).reshape(1, 384)
        for k in range(3):
            small[row : row + 1, :] = v[:, k * 128 : (k + 1) * 128].astype(bf16)
            row += 1
    v = qb[...].astype(f32).reshape(1, 448)
    for k in range(3):
        small[row + k : row + k + 1, :] = v[:, k * 128 : (k + 1) * 128].astype(bf16)
        small[row + 5 + k : row + 6 + k, :] = v[:, 64 + k * 128 : 64 + (k + 1) * 128].astype(bf16)
    small[row + 3 : row + 4, 0:64] = v[:, 384:448].astype(bf16)
    small[row + 4 : row + 5, 64:128] = v[:, 0:64].astype(bf16)
    first[:416, :] = small[...]
    for k in range(3):
        first[416 + 384 * k : 800 + 384 * k, :] = up_w[:, k * 128 : (k + 1) * 128]


def pack_tokens_kernel(ids, x, dy, q_w, xd):
    tokens = x.shape[0]
    xd[:tokens] = x[...]
    xd[tokens : 2 * tokens] = dy[...]
    rows = q_w.shape[0] // 2
    xd[2 * tokens :, : 2 * rows] = q_w[:rows]
    xd[2 * tokens :, 2 * rows :] = q_w[rows:]


def pack_call(kernel, name, ids, args, specs, outs):
    return pl.pallas_call(
        kernel,
        out_shape=tuple(jax.ShapeDtypeStruct(s, bf16) for s in outs),
        grid_spec=pltpu.PrefetchScalarGridSpec(
            num_scalar_prefetch=1,
            grid=(1,),
            in_specs=specs,
            out_specs=[pl.BlockSpec(s, lambda i, s: (0, 0)) for s in outs],
        ),
        name=name,
        cost_estimate=pl.CostEstimate(
            flops=int(WEIGHT.get(name, 0) * 1e9) + 1, transcendentals=0, bytes_accessed=1
        ),
    )(ids, *args)


def pack(ids, qkv_weight, up_weight, vectors):
    half, width = qkv_weight.shape[0], 2 * qkv_weight.shape[0]
    step = up_weight.shape[1] // 8
    specs = [
        pl.BlockSpec((half, 128), lambda i, s: (0, width // 128)),
        pl.BlockSpec((half, step), lambda i, s: (0, (1 - s[1]) * 4 + s[2] * 2 + s[3])),
    ] + [pl.BlockSpec(v.shape, lambda i, s: (0,)) for v in vectors]
    outs = ((half + 32, 128), (half + 32 + 3 * half, 128))
    return pack_call(pack_kernel, "pack", ids, (qkv_weight, up_weight, *vectors), specs, outs)


def pack_tokens(ids, x, dy, qkv_weight):
    half, width = qkv_weight.shape[0], 2 * qkv_weight.shape[0]
    token = pl.BlockSpec(x.shape, lambda i, s: (0, 0))
    specs = [token, token, pl.BlockSpec((half, half), lambda i, s: (0, s[2]))]
    outs = ((2 * x.shape[0] + half // 2, width),)
    return pack_call(pack_tokens_kernel, "pack_tokens", ids, (x, dy, qkv_weight), specs, outs)


def row_vector(block, first, count=3):
    return jnp.concatenate([block[first + k : first + k + 1] for k in range(count)], axis=1)


def natural(side, own, other):
    return jnp.concatenate(
        [jnp.where(side == 0, own, other), jnp.where(side == 0, other, own)], axis=1
    )


def model_vector(side, own, other, index):
    return natural(side, row_vector(own, 3 * index), row_vector(other, 3 * index))


def qkv_bias_tiles(side, own, other):
    low = jnp.where(side == 0, own[18:22], other[18:22])
    high = jnp.where(side == 0, other[22:26], own[22:26])
    tiles = [low[0:1], low[1:2], low[2:3], low[3:4] + high[0:1], high[1:2], high[2:3], high[3:4]]
    return tiles


def normalize(values):
    centred = values - jnp.mean(values, axis=-1, keepdims=True)
    root = lax.rsqrt(jnp.mean(centred * centred, axis=-1, keepdims=True) + 1e-05)
    return centred * root, root


def turn(m, c, s1, s2):
    return m * c + pltpu.roll(m, 120, 1) * s1 + pltpu.roll(m, 8, 1) * s2


def kv_tables(c, s1, s2):
    key = lax.broadcasted_iota(jnp.int32, c.shape, 1) < 64
    return jnp.where(key, c, 1.0), jnp.where(key, s1, 0.0), jnp.where(key, s2, 0.0)


def front_kernel(ids, x, p_own, pu, c, s1, s2, first, kv, p_copy, up0):
    p_oth = pu.at[: p_own.shape[0]]
    p_copy[...] = p_oth[...]
    for k in range(3):
        up0[:, k * 128 : (k + 1) * 128] = pu[416 + 384 * k : 800 + 384 * k, :]
    side = ids[1]
    half = x.shape[1] // 2
    own, other = p_own[half:].astype(f32), p_oth[half:].astype(f32)
    hat, _ = normalize(x[...].astype(f32))
    first[...] = (hat * model_vector(side, own, other, 0) + model_vector(side, own, other, 1)).astype(bf16)
    m = mm(first[:, lanes(side * half, half)], p_own[:half])
    m += mm(first[:, lanes((1 - side) * half, half)], p_oth[:half])
    m += qkv_bias_tiles(side, own, other)[6]
    kv[...] = turn(m, *kv_tables(c[...], s1[...], s2[...])).astype(bf16)


def query_kernel(ids, first, w, w_mine, w_theirs, p_own, p_oth, c, s1, s2, q, w_copy, bias):
    side, core = ids[1], ids[2]
    half = first.shape[1] // 2
    tiles = qkv_bias_tiles(side, p_own[half:].astype(f32), p_oth[half:].astype(f32))
    bias[...] = jnp.concatenate(tiles[:6], axis=1)
    for ref, cb in ((w_mine, core), (w_theirs, 1 - core)):
        col = cb * half
        w_copy[:, lanes(col, half)] = ref[...]
        m = mm(first[:, lanes(side * half, half)], w[:, lanes(col, half)])
        m += mm(first[:, lanes((1 - side) * half, half)], ref[...])
        m += bias[:, lanes(col, half)]
        for k in range(half // 128):
            low = turn(m[:, k * 128 : (k + 1) * 128], c[...], s1[...], s2[...]).astype(bf16)
            q[:, lanes(col + k * 128, 128)] = (low.astype(f32) * 0.125).astype(bf16)


def cotangent_kernel(dy_own, xd, w, g_own, g_oth, q_mine):
    rows = q_mine.shape[0] // 2
    q_mine[:rows] = xd[2 * dy_own.shape[0] :, : 2 * rows]
    q_mine[rows:] = xd[2 * dy_own.shape[0] :, 2 * rows :]
    g_own[...] = mm(dy_own[...], w[...], NT).astype(bf16)
    g_oth[...] = mm(xd[dy_own.shape[0] : 2 * dy_own.shape[0]], w[...], NT).astype(bf16)


def ff_kernel(
    ids, x_own, xd, dy_own, up, up0, up1, up2, up3, down, up_bias, p_own, p_oth,
    keep_a, send_a, keep_b, send_b, act, dh, hat_oth, first_oth, hat_half, dy_copy, up_sum,
    a2, dy, bias, g_down, g_up, up_buf, down_buf, up_sem, down_sem,
):
    side, core, near_y = ids[1], ids[2], ids[3]
    tokens, width = x_own.shape
    x_oth, dy_oth = xd.at[:tokens], xd.at[tokens : 2 * tokens]
    half = width // 2
    wide = act.shape[1]
    step = wide // 4
    pieces = [
        (ref, (jnp.bitwise_xor(core, a) * 2 + jnp.bitwise_xor(near_y, b)), a, b)
        for ref, a, b in ((up0, 0, 0), (up1, 0, 1), (up2, 1, 0), (up3, 1, 1))
    ]

    def up_copy(i, piece):
        at = lanes(side * wide + piece * step, step)
        return pltpu.make_async_copy(up.at[:, at], up_buf.at[i], up_sem.at[i])

    def down_copy(i, piece):
        at = pl.ds(pl.multiple_of(piece * step, step), step)
        return pltpu.make_async_copy(down.at[at, :], down_buf.at[i], down_sem.at[i])

    for i, (_, piece, _, _) in enumerate(pieces):
        up_copy(i, piece).start()
        down_copy(i, piece).start()
    own, other = p_own[half:].astype(f32), p_oth[half:].astype(f32)
    gain1, shift1 = model_vector(side, own, other, 0), model_vector(side, own, other, 1)
    gain2, shift2 = model_vector(side, own, other, 2), model_vector(side, own, other, 3)
    mine, theirs = lanes(side * half, half), lanes((1 - side) * half, half)
    hat_own, _ = normalize(x_own[...].astype(f32))
    a2[:tokens] = (hat_own * gain2 + shift2).astype(bf16)
    hat_other, _ = normalize(x_oth[...].astype(f32))
    hat_oth[...] = hat_other
    a2[tokens:] = (hat_other * gain2 + shift2).astype(bf16)
    first_oth[...] = (hat_other * gain1 + shift1).astype(bf16)
    hat_half[...] = jnp.where(side == 0, hat_other[:, :half], hat_other[:, half:])
    dy[:tokens] = dy_own[...]
    dy[tokens:] = dy_oth[...]
    dy_copy[...] = dy_oth[...]
    bias[...] = up_bias[...].astype(f32).reshape(1, wide)
    rows = half // 4
    far = ids[0] // 4 % 4
    for i, (ref, piece, a, b) in enumerate(pieces):
        up_copy(i, piece).wait()
        down_copy(i, piece).wait()
        cols = lanes(piece * step, step)
        h = mm(a2[:, mine], up_buf[i])
        h += mm(a2[:, theirs], ref[...])
        h += bias[:, cols]
        phi = 0.5 * (1.0 + lax.erf(h * 0.7071067811865476))
        slope = phi + h * jnp.exp(-0.5 * h * h) * 0.3989422804014327
        g = (h * phi).astype(bf16)
        act[:, i * step : (i + 1) * step] = g
        d = mm(dy[...], down_buf[i], NT)
        e = (d * slope).astype(bf16)
        dh[:, i * step : (i + 1) * step] = e
        up_sum[:, cols] = jnp.sum(e.astype(f32), axis=0, keepdims=True)
        g_down[...] = mm(g, dy[...], TN).astype(bf16)
        g_up[:, :half] = mm(a2[:, mine], e, TN).astype(bf16)
        g_up[:, half:] = mm(a2[:, theirs], e, TN).astype(bf16)
        for k in range(4):
            z = jnp.bitwise_xor(far, (k & 1) * 2 + (k >> 1))
            at = pl.ds(pl.multiple_of(z * rows, rows), rows)
            slot = b * 4 + k
            (send_a if a else keep_a)[slot] = g_down[at, :]
            (send_b if a else keep_b)[slot] = g_up[at, :]


def ff_rest_kernel(
    ids, act, dh, x_own, hat_oth, up, up0, up1, up2, up3, down,
    ff_own, ff_oth, ds_own, ds_oth, n_mine, n_send, sums, up_buf, down_buf, up_sem, down_sem,
):
    side, core, near_y = ids[1], ids[2], ids[3]
    tokens, width = x_own.shape
    half = width // 2
    wide = act.shape[1]
    step = wide // 4
    order = ((0, 0), (0, 1), (1, 0), (1, 1))
    pieces = [jnp.bitwise_xor(core, a) * 2 + jnp.bitwise_xor(near_y, b) for a, b in order]
    copies = []
    for i, piece in enumerate(pieces):
        at = pl.ds(pl.multiple_of(piece * step, step), step)
        copies.append(pltpu.make_async_copy(down.at[at, :], down_buf.at[i], down_sem.at[i]))
        at = lanes(side * wide + piece * step, step)
        copies.append(pltpu.make_async_copy(up.at[:, at], up_buf.at[i], up_sem.at[i]))
    for copy in copies:
        copy.start()
    hat_own, _ = normalize(x_own[...].astype(f32))
    for copy in copies:
        copy.wait()
    out = sum(mm(act[:, i * step : (i + 1) * step], down_buf[i]) for i in range(4))
    ff_own[...] = out[:tokens]
    ff_oth[...] = out[tokens:]
    ds_mine = sum(mm(dh[:, i * step : (i + 1) * step], up_buf[i], NT) for i in range(4))
    ds_theirs = sum(
        mm(dh[:, i * step : (i + 1) * step], ref[...], NT) for i, ref in enumerate((up0, up1, up2, up3))
    )
    low = jnp.where(side == 0, ds_mine, ds_theirs)
    high = jnp.where(side == 0, ds_theirs, ds_mine)
    for part, ds in ((slice(0, half), low), (slice(half, width), high)):
        ds_own[:, part] = ds[:tokens]
        ds_oth[:, part] = ds[tokens:].astype(bf16)
        moved = ds[:tokens] * hat_own[:, part] + ds[tokens:] * hat_oth[:, part]
        sums[0:1, part] = jnp.sum(moved, axis=0, keepdims=True)
        sums[1:2, part] = jnp.sum(ds, axis=0, keepdims=True)
    split_rows(sums, 2, side, half, n_mine, n_send)


def split_rows(sums, count, side, half, mine, send):
    for ref, owner in ((mine, side), (send, 1 - side)):
        ref[...] = jnp.zeros_like(ref)
        for i in range(count):
            for k in range(half // 128):
                at = i * (half // 128) + k
                ref[at : at + 1, :] = sums[i : i + 1, lanes(owner * half + k * 128, 128)]


class Block:
    def __init__(self, stages, n_dev, docs, side, ids, len_ref):
        self.stages, self.n_dev, self.me, self.fsdp = stages, n_dev, ids[0], ids[1]
        self.block = ids[0] if side == 0 else 2 * n_dev - 1 - ids[0]
        self.rows = pl.ds(side * BLOCK, BLOCK)
        self.low = lax.broadcasted_iota(jnp.int32, (BLOCK, 128), 1) < 64
        base = self.block * BLOCK
        self.qpos = base + lax.broadcasted_iota(jnp.int32, (1, BLOCK), 1)
        total = first = jnp.int32(0)
        self.qstart = jnp.zeros((1, BLOCK), jnp.int32)
        for e in range(docs):
            size = len_ref[0, e]
            total = total + size
            self.qstart = self.qstart + jnp.where(total <= self.qpos, size, 0)
            first = first + jnp.where(total <= base, size, 0)
        self.steps = (base + BLOCK - first + 2 * BLOCK - 1) // (2 * BLOCK)

    def row_of(self, j):
        j = jnp.maximum(j, 0)
        dev = jnp.where(j < self.n_dev, j, 2 * self.n_dev - 1 - j)
        slot = slot_of(jnp.bitwise_xor(dev, self.me), self.stages)
        return pl.multiple_of((slot * 2 + jnp.where(j < self.n_dev, 0, 1)) * BLOCK, BLOCK)

    def columns(self, p, half):
        close = p < half // 128
        local = (p % (half // 128)) * 128
        return close, local, lanes((self.fsdp if close else 1 - self.fsdp) * half + local, 128)

    def half_turn(self, two):
        return pltpu.roll(two.astype(f32), 64, 1).astype(bf16)

    def spread_query(self, q_ref, qz):
        for p in range(q_ref.shape[1] // 128):
            two = q_ref[self.rows, self.columns(p, q_ref.shape[1] // 2)[2]]
            zero = jnp.zeros_like(two)
            qz[pl.ds(p * 256, 128), :] = jnp.where(self.low, two, zero)
            qz[pl.ds(p * 256 + 128, 128), :] = jnp.where(self.low, self.half_turn(two), zero)

    def load(self, t, kv_mine, kv_theirs, bias):
        middle = kv_mine.shape[0]
        parts, at = [], []
        hi = self.block - 2 * t
        for j in (hi - 1, hi):
            row = self.row_of(j)
            inner = pl.multiple_of(jnp.where(row < middle, row, row - middle), BLOCK)
            here = pl.ds(inner, BLOCK)
            parts.append(jnp.where(row < middle, kv_mine[here, :], kv_theirs[here, :]))
            at.append(row)
        kpos = (hi - 1) * BLOCK + lax.broadcasted_iota(jnp.int32, (2 * BLOCK, BLOCK), 0)
        ok = (kpos <= self.qpos) & (kpos >= self.qstart)
        bias[...] = jnp.where(ok, 0.0, -1e30)
        return jnp.concatenate(parts, axis=0), at


def attn_forward_kernel(
    stages, n_dev, docs, side, ids, len_ref, q_ref, kv_mine, kv_theirs, g_own, g_oth,
    o_own, o_oth, st, qz, ot, bias,
):
    me = Block(stages, n_dev, docs, side, ids, len_ref)
    half = q_ref.shape[1] // 2
    pairs = q_ref.shape[1] // 128
    me.spread_query(q_ref, qz)
    ot[...] = jnp.zeros_like(ot)
    st[0] = jnp.full(st.shape[1:], -1e30, f32)
    st[1] = jnp.zeros(st.shape[1:], f32)

    def forward(t, carry):
        kvb, _ = me.load(t, kv_mine, kv_theirs, bias)
        vt = kvb.astype(f32).T.astype(bf16)[64:]
        mask = bias[...]
        for p in range(pairs):
            s2 = mm(kvb, qz[pl.ds(p * 256, 256), :], NT)
            for i in range(2):
                h = 2 * p + i
                s = s2[:, i * 128 : (i + 1) * 128] + mask
                old = st[0, h : h + 1, :]
                new = jnp.maximum(old, jnp.max(s, axis=0, keepdims=True))
                e = jnp.exp(s - new)
                alpha = jnp.exp(old - new)
                st[0, h : h + 1, :] = new
                st[1, h : h + 1, :] = st[1, h : h + 1, :] * alpha + jnp.sum(e, axis=0, keepdims=True)
                hs = pl.ds(h * 64, 64)
                ot[hs, :] = ot[hs, :] * alpha + mm(vt, e.astype(bf16))
        return 0

    lax.fori_loop(0, me.steps, forward, 0)
    for p in range(pairs):
        close, local, _ = me.columns(p, half)
        gt = (g_own if close else g_oth)[me.rows, pl.ds(local, 128)].astype(f32).T
        halves = []
        for i in range(2):
            h = 2 * p + i
            l = st[1, h : h + 1, :]
            o = ot[pl.ds(h * 64, 64), :] / l
            halves.append(o)
            st[2, h : h + 1, :] = jnp.sum(o * gt[i * 64 : (i + 1) * 64], axis=0, keepdims=True)
            st[0, h : h + 1, :] = st[0, h : h + 1, :] + jnp.log(l)
        (o_own if close else o_oth)[:, pl.ds(local, 128)] = jnp.concatenate(halves, axis=0).T.astype(bf16)


def attn_backward_kernel(stages, n_dev, docs, side, last, *refs):
    ids, len_ref, q_ref, kv_mine, kv_theirs, g_own, g_oth, st, cos_ref, sin_ref = refs[:10]
    if not last:
        dm_ref, acc, qz, gz, dqt, bias, ds_sc, p_sc = refs[10:]
        acc[...] = jnp.zeros_like(acc)
    else:
        before, dm_ref, dkv_keep, dkv_send, qz, gz, dqt, bias, ds_sc, p_sc, acc = refs[10:]
        acc[...] = before[...]
    me = Block(stages, n_dev, docs, side, ids, len_ref)
    half = q_ref.shape[1] // 2
    pairs = q_ref.shape[1] // 128
    me.spread_query(q_ref, qz)
    for p in range(pairs):
        close, local, _ = me.columns(p, half)
        two = (g_own if close else g_oth)[me.rows, pl.ds(local, 128)]
        zero = jnp.zeros_like(two)
        gz[pl.ds(p * 256, 128), :] = jnp.where(me.low, zero, me.half_turn(two))
        gz[pl.ds(p * 256 + 128, 128), :] = jnp.where(me.low, zero, two)
    dqt[...] = jnp.zeros_like(dqt)

    def backward(t, carry):
        kvb, at = me.load(t, kv_mine, kv_theirs, bias)
        kt = kvb.astype(f32).T.astype(bf16)[:64]
        mask = bias[...]
        for p in range(pairs):
            s2 = mm(kvb, qz[pl.ds(p * 256, 256), :], NT)
            dp2 = mm(kvb, gz[pl.ds(p * 256, 256), :], NT)
            for i in range(2):
                h = 2 * p + i
                sl = slice(i * 128, (i + 1) * 128)
                pr = jnp.exp((s2[:, sl] + mask) - st[0, h : h + 1, :])
                ds = pr * (dp2[:, sl] - st[2, h : h + 1, :])
                ds_sc[:, h * 128 : (h + 1) * 128] = ds.astype(bf16)
                p_sc[:, h * 128 : (h + 1) * 128] = pr.astype(bf16)
        part = mm(ds_sc[...], qz[...]) + mm(p_sc[...], gz[...])
        for i in range(2):
            acc[pl.ds(at[i], BLOCK), :] += part[i * BLOCK : (i + 1) * BLOCK]
        dqt[...] += mm(kt, ds_sc[...])
        return 0

    lax.fori_loop(0, me.steps, backward, 0)
    cos = cos_ref[side]
    sin = sin_ref[side]
    for p in range(pairs):
        halves = []
        for i in range(2):
            h = 2 * p + i
            g = dqt[:, h * 128 : (h + 1) * 128] * 0.125
            g0, g1 = g[:8], g[8:16]
            halves += [g0 * cos + g1 * sin, g1 * cos - g0 * sin, g[16:]]
        dm_ref[:, me.columns(p, half)[2]] = jnp.concatenate(halves, axis=0).T.astype(bf16)
    if last:
        middle = dkv_keep.shape[0]
        dkv_keep[...] = acc[:middle].astype(bf16)
        dkv_send[...] = acc[middle:].astype(bf16)


def attn_forward(side, stages, n_dev, ids, lengths, q, kv, g_own, g_oth):
    width = q.shape[1]
    block = q.shape[0] // 2
    rows = width // 64 * 128
    kv = near(*kv) if n_dev <= LOW else kv
    return call(
        partial(attn_forward_kernel, stages, n_dev, lengths.shape[1], side),
        "attn_forward",
        [((block, width // 2), bf16, False), ((block, width // 2), bf16, True), ((3, 16, 128), f32, True)],
        (ids, lengths, *near(q), *kv, g_own, *near(g_oth)),
        scratch=[pltpu.VMEM((rows, 128), bf16), pltpu.VMEM((width, 128), f32), pltpu.VMEM((256, 128), f32)],
        room=6 + (0 if n_dev <= LOW else kv[0].size * 4 // 2**20),
    )


def attn_backward(side, stages, n_dev, ids, lengths, q, kv, g_own, g_oth, st, cos, sin, before=()):
    width = q.shape[1]
    block = q.shape[0] // 2
    middle = kv[0].shape[0]
    rows = width // 64 * 128
    small = n_dev <= LOW
    close = near if small else (lambda *values: values)
    outs = [((block, width), bf16, True)]
    last = len(before) > 0
    outs += [((middle, 128), bf16, True)] * 2 if last else [((2 * middle, 128), f32, small)]
    scratch = [
        pltpu.VMEM((rows, 128), bf16),
        pltpu.VMEM((rows, 128), bf16),
        pltpu.VMEM((64, rows), f32),
        pltpu.VMEM((256, 128), f32),
        pltpu.VMEM((256, rows), bf16),
        pltpu.VMEM((256, rows), bf16),
    ]
    if last:
        scratch += [pltpu.VMEM((2 * middle, 128), f32)]
    return call(
        partial(attn_backward_kernel, stages, n_dev, lengths.shape[1], side, last),
        "attn_backward",
        outs,
        (ids, lengths, *near(q), *close(*kv), g_own, *near(g_oth, st), cos, sin, *close(*before)),
        scratch=scratch,
        room=8 + 2 * middle * 128 * (4 if small else 7) // 2**20,
    )


def pile_kernel(a0, a1, b0, b1, c0, c1, *outs):
    for out, parts in zip(outs, ((a0, a1), (b0, b1), (c0, c1))):
        rows = parts[0].shape[0]
        out[:rows] = parts[0][...]
        out[rows:] = parts[1][...]


def mix_kernel(ff, o, w, out):
    out[...] = (ff[...] + mm(o[...], w[...])).astype(bf16)


def result_kernel(ids, x, ff, o, w, recv, p_own, p_oth, out):
    side = ids[1]
    half = x.shape[1] // 2
    own, other = p_own[half:].astype(f32), p_oth[half:].astype(f32)
    y = x[...].astype(f32) + (ff[...] + mm(o[...], w[...])) + recv[...].astype(f32)
    y += model_vector(side, own, other, 4) + model_vector(side, own, other, 5)
    out[...] = y.astype(bf16)


def dm_kv_kernel(*refs):
    later, c, s1, s2, out = refs[-5:]
    total = later[...]
    for ref in refs[:-5]:
        total = total + ref[...].astype(f32)
    c, s1, s2 = kv_tables(c[...], s1[...], s2[...])
    out[...] = turn(total, c, -s1, -s2).astype(bf16)


def x_grad_kernel(ids, x, dy, dm, dm_kv, w, w_oth, p_own, p_oth, ds, ds_recv, out, da):
    side = ids[1]
    width = x.shape[1]
    half = width // 2
    own, other = p_own[half:].astype(f32), p_oth[half:].astype(f32)
    mine, theirs = lanes(side * half, half), lanes((1 - side) * half, half)
    da[:, mine] = mm(dm[...], w[:, :width], NT) + mm(dm_kv[...], p_own[:half], NT)
    da[:, theirs] = mm(dm[...], w_oth[...], NT) + mm(dm_kv[...], p_oth[:half], NT)
    hat, root = normalize(x[...].astype(f32))
    total = dy[...].astype(f32)
    for i, grad in enumerate((da[...], ds[...] + ds_recv[...].astype(f32))):
        up = grad * model_vector(side, own, other, 2 * i)
        total += root * (
            up - jnp.mean(up, axis=-1, keepdims=True) - hat * jnp.mean(up * hat, axis=-1, keepdims=True)
        )
    out[...] = total


def pair_kernel(ids, f_own, f_oth, dm_own, dm_oth, o_own, o_oth, dy_own, dy_oth, keep, send, gq, go):
    side, core = ids[1], ids[2]
    half = f_own.shape[1] // 2
    mine = lanes(side * half, half)
    gq[...] = mm(f_own[:, mine], dm_own[...], TN) + mm(f_oth[:, mine], dm_oth[...], TN)
    go[...] = mm(o_own[...], dy_own[...], TN) + mm(o_oth[...], dy_oth[...], TN)
    rows = half // 8
    close = ids[0] % LOW // 2
    for ref, cb in ((keep, core), (send, 1 - core)):
        cols = lanes(cb * half, half)
        for k in range(8):
            at = pl.ds(pl.multiple_of(jnp.bitwise_xor(close, CHUNKS[k]) * rows, rows), rows)
            ref[k * rows : (k + 1) * rows, 0:half] = gq[at, cols].astype(bf16)
            ref[k * rows : (k + 1) * rows, half:] = go[at, cols].astype(bf16)


def tail_kernel(
    ids, f_own, f_oth, dm_own, dm_oth, dy_own, dy_oth, kv_own, kv_oth, n_mine, n_recv, up_sum,
    x_own, hat_half, w, p_own, out, tail, hat,
):
    side = ids[1]
    half = f_own.shape[1] // 2
    mine = lanes(side * half, half)
    tail[:half] = mm(f_own[:, mine], kv_own[...], TN) + mm(f_oth[:, mine], kv_oth[...], TN)
    tail[half:] = jnp.zeros((32, 128), f32)
    gain = shift = 0.0
    hat[...] = normalize(x_own[...].astype(f32))[0]
    for x, dm, kv in ((hat[:, mine], dm_own, kv_own), (hat_half[...], dm_oth, kv_oth)):
        grad = mm(dm[...], w[:, : 2 * half], NT) + mm(kv[...], p_own[:half], NT)
        gain += jnp.sum(grad * x, axis=0, keepdims=True)
        shift += jnp.sum(grad, axis=0, keepdims=True)
    row = half
    for v in (gain, shift):
        for k in range(3):
            tail[row + k : row + k + 1, :] = v[:, k * 128 : (k + 1) * 128]
        row += 3
    v = n_mine[...] + n_recv[...]
    tail[row : row + 6] = v[:6]
    row += 6

    def total(a, b):
        return jnp.sum(a.astype(f32), axis=0, keepdims=True) + jnp.sum(b.astype(f32), axis=0, keepdims=True)

    v = total(dy_own[:, mine], dy_oth[:, mine])
    for k in range(3):
        tail[row + k : row + k + 1, :] = v[:, k * 128 : (k + 1) * 128]
    row += 3
    v = jnp.concatenate([total(dm_own[...], dm_oth[...]), total(kv_own[...], kv_oth[...])], axis=1)
    moved = jnp.concatenate([v[:, 448:], v[:, :448]], axis=1)
    v = jnp.where(side == 0, v, moved)
    for k in range(4):
        tail[row + k : row + k + 1, :] = v[:, k * 128 : (k + 1) * 128]
    row += 4
    for k in range(12):
        tail[row + k : row + k + 1, :] = up_sum[:, k * 128 : (k + 1) * 128]
    out[...] = tail[...].astype(bf16)


def sum_kernel(*refs):
    total = refs[0][...].astype(f32)
    for ref in refs[1:-1]:
        total = total + ref[...].astype(f32)
    refs[-1][...] = total.astype(refs[-1].dtype)


def sum_of(first, second, name):
    return call(sum_kernel, name, [(first.shape, first.dtype, True)], near(first, second))[0]


def up_part_kernel(a, b, own, other):
    half = own.shape[-1]
    total = a[...].astype(f32) + b[...].astype(f32)
    own[...] = total[..., :half].astype(bf16)
    other[...] = total[..., half:].astype(bf16)


def up_join_kernel(own, other, out):
    half = own.shape[-1]
    out[..., :half] = own[...]
    out[..., half:] = other[...]


def chunk_of(ids, other_core, slot):
    core, near_y, far = ids[2], ids[3], ids[0] // 4 % 4
    piece = jnp.bitwise_xor(core, other_core) * 2 + jnp.bitwise_xor(near_y, slot >> 2)
    return piece, jnp.bitwise_xor(far, (slot & 1) * 2 + (slot >> 1 & 1))


def down_out_kernel(ids, mine, theirs, out):
    rows = mine.shape[1]
    for a, ref in enumerate((mine, theirs)):
        for k in range(8):
            piece, z = chunk_of(ids, a, k)
            out[pl.ds(pl.multiple_of((piece * 4 + z) * rows, rows), rows), :] = ref[k].astype(f32)


def up_out_kernel(ids, mine, theirs, out):
    side = ids[1]
    rows = mine.shape[1]
    half = mine.shape[2] // 2
    wide = out.shape[1] // 2
    for a, ref in enumerate((mine, theirs)):
        for k in range(8):
            piece, z = chunk_of(ids, a, k)
            at = pl.ds(pl.multiple_of(z * rows, rows), rows)
            for j, owner in ((0, side), (1, 1 - side)):
                part = ref[k, :, j * half : (j + 1) * half].astype(f32)
                out[at, lanes(owner * wide + piece * half, half)] = part


def attn_out_kernel(ids, p_mine, p_theirs, tail, g_qkv, g_out, n0, n1, n2, n3, qb, ob, ub, db):
    core = ids[2]
    close = ids[0] % LOW // 2
    half = g_qkv.shape[0]
    rows = half // 8
    for ref, cb in ((p_mine, core), (p_theirs, 1 - core)):
        cols = lanes(cb * half, half)
        for k in range(8):
            at = pl.ds(pl.multiple_of(jnp.bitwise_xor(close, CHUNKS[k]) * rows, rows), rows)
            part = ref[k * rows : (k + 1) * rows, :].astype(f32)
            g_qkv[at, cols] = part[:, :half]
            g_out[at, cols] = part[:, half:]
    g_qkv[:, 2 * half :] = tail[:half].astype(f32)
    small = tail[half:].astype(f32)
    for i, ref in enumerate((n0, n1, n2, n3, ob)):
        ref[...] = row_vector(small, 3 * i).reshape(half)
    db[...] = row_vector(small, 12).reshape(half)
    qb[...] = row_vector(small, 15, 4)[:, : qb.shape[0]].reshape(qb.shape[0])
    ub[...] = row_vector(small, 19, 12).reshape(ub.shape[0])


class Values:
    pass


def body(
    layer_input, doc_lengths, ln1_gain, ln1_bias, ln2_gain, ln2_bias, qkv_weight, qkv_bias,
    out_weight, out_bias, up_weight, up_bias, down_weight, down_bias, out_grad, kv_grad_later,
):
    devices = lax.axis_size("ctx")
    me = lax.axis_index("ctx").astype(jnp.int32)
    side = lax.axis_index("fsdp").astype(jnp.int32)
    ids = jnp.stack([me, side, me % 2, me // 2 % 2])
    tokens, width = layer_input.shape[1:]
    half_rows = tokens // 2
    half = width // 2
    wide = up_weight.shape[1] // 2
    stages = stages_of(devices)
    x_own, dy_own = layer_input[0], out_grad[0]

    vectors = (ln1_gain, ln1_bias, ln2_gain, ln2_bias, out_bias, down_bias, qkv_bias)
    p_own, pu_own = pack(ids, qkv_weight, up_weight, vectors)
    pu_oth = swap_x(pu_own)
    xd_own = pack_tokens(ids, x_own, dy_own, after(qkv_weight, pu_own))[0]
    xd = swap_x(xd_own)

    offsets = jnp.arange(half_rows, dtype=jnp.int32)
    places = jnp.concatenate([me * half_rows + offsets, (2 * devices - 1 - me) * half_rows + offsets]).astype(f32)
    half_rot = ROT // 2
    freq = 10000.0 ** (-jnp.arange(half_rot, dtype=f32) / half_rot)
    lane = np.arange(128)
    angles = places[:, None] * jnp.tile(freq, 128 // half_rot)[None, :]
    cosine, sine = jnp.cos(angles), jnp.sin(angles)
    tables = (
        jnp.where(lane % 64 < 16, cosine, 1.0),
        jnp.where(lane % 64 < 8, -sine, 0.0),
        jnp.where((lane % 64 >= 8) & (lane % 64 < 16), sine, 0.0),
    )
    t_angles = places.reshape(2, 1, half_rows) * freq[None, :, None]
    cos_t, sin_t = jnp.cos(t_angles), jnp.sin(t_angles)

    low = min(LOW, devices)
    rows = half // 4
    step = wide // 4
    token_f32, token_low = ((tokens, width), f32, False), ((tokens, width), bf16, False)
    e = Values()
    e.o, e.o_send, e.st, e.dm = {}, {}, {}, {}
    e.down, e.up, e.kv, e.pair, e.tail = (Values() for _ in range(5))

    def front():
        e.first_own, kv, e.p_oth, up0 = call(
            front_kernel,
            "front",
            [
                ((tokens, width), bf16, False), ((tokens, 128), bf16, True), (p_own.shape, bf16, False),
                ((half, half), bf16, True),
            ],
            (ids, x_own, p_own, *near(pu_oth), *tables),
        )
        up1 = swap_ctx(up0, 2)
        e.ups = (up0, up1, swap_ctx(up0, 1), swap_ctx(up1, 1))
        for stride, _ in stages[:-1]:
            kv = gather_step(kv, stride, "kv_join")
        e.kv_all = (kv, swap_ctx(kv, 1))

    def cotangent():
        e.g_own, g_send, e.q_mine = call(
            cotangent_kernel,
            "cotangent",
            [((tokens, half), bf16, False), ((tokens, half), bf16, True), ((half, half), bf16, True)],
            (dy_own, *near(xd), out_weight),
        )
        e.g_oth = swap_x(g_send)
        e.q_theirs = swap_ctx(e.q_mine, 1)

    def ff():
        chunks = ((8, rows, width), bf16, True)
        (
            keep_a, send_a, keep_b, send_b, e.act, e.dh, e.hat_oth, e.first_oth, e.hat_half,
            e.dy_far, e.up_sum,
        ) = call(
            ff_kernel,
            "ff",
            [
                chunks, chunks, chunks, chunks, ((2 * tokens, wide), bf16, True), ((2 * tokens, wide), bf16, True),
                token_f32, token_low, ((tokens, half), f32, False), token_low, ((1, wide), f32, False),
            ],
            (
                ids, x_own, *near(xd), dy_own, Raw(up_weight), *near(*e.ups), Raw(down_weight), up_bias, p_own,
                e.p_oth,
            ),
            scratch=[
                pltpu.VMEM((2 * tokens, width), bf16),
                pltpu.VMEM((2 * tokens, width), bf16),
                pltpu.VMEM((1, wide), f32),
                pltpu.VMEM((half, width), bf16),
                pltpu.VMEM((half, width), bf16),
                pltpu.VMEM((4, half, step), bf16),
                pltpu.VMEM((4, step, width), bf16),
                pltpu.SemaphoreType.DMA((4,)),
                pltpu.SemaphoreType.DMA((4,)),
            ],
            room=16,
        )
        e.down.parts, e.up.parts = (keep_a, swap_ctx(send_a, 1)), (keep_b, swap_ctx(send_b, 1))

    def add_step(chain, mask, name):
        kept, arrived = chain.parts
        out = ((kept.shape[0] // 2,) + kept.shape[1:], kept.dtype, True)
        kept, send = call(add_split_kernel, name, [out, out], near(kept, arrived))
        chain.parts = (kept, swap_ctx(send, mask))

    def join_step(chain, mask, name):
        value, arrived = chain.parts
        value = join(value, arrived, name)
        chain.parts = (value, swap_ctx(value, mask))

    def query():
        e.q, e.q_far = call(
            query_kernel,
            "query",
            [((tokens, width), bf16, True), ((half, width), bf16, False)],
            (ids, e.first_own, qkv_weight, *near(e.q_mine, e.q_theirs), p_own, e.p_oth, *tables),
            scratch=[pltpu.VMEM((1, width), f32)],
        )

    pairs = (stages, devices, ids, doc_lengths)

    def forward(side):
        e.o[side], e.o_send[side], e.st[side] = attn_forward(
            side, *pairs, e.q, e.kv_all, e.g_own, e.g_oth
        )

    def backward(side):
        before = (e.dkv,) if side == 1 and devices <= LOW else ()
        e.dm[side], *dkv = attn_backward(
            side, *pairs, e.q, e.kv_all, e.g_own, e.g_oth, e.st[side], cos_t, sin_t, before=before
        )
        if side == 0:
            e.dkv = dkv[0]
            return
        if devices > LOW:
            dkv = (e.dkv + dkv[0]).astype(bf16)
            middle = dkv.shape[0] // 2
            dkv = (dkv[:middle], dkv[middle:])
        e.kv.parts = (dkv[0], swap_ctx(dkv[1], 1))

    def pile():
        e.o_own, o_send, e.dm_own = call(
            pile_kernel,
            "pile",
            [((tokens, half), bf16, False), ((tokens, half), bf16, True), ((tokens, width), bf16, True)],
            (e.o[0], e.o[1], *near(e.o_send[0], e.o_send[1], e.dm[0], e.dm[1])),
        )
        e.dm_oth, e.o_oth = swap_x(e.dm_own), swap_x(o_send)

    def kv_more():
        stride = 16
        while stride < devices:
            add_step(e.kv, stride, "kv_add")
            stride *= 2

    def ff_rest():
        row_block = ((8, 128), f32, False)
        e.ff_own, e.ff_oth, e.ds_own, ds_oth, e.n_mine, n_send = call(
            ff_rest_kernel,
            "ff_rest",
            [token_f32, token_f32, token_f32, token_low, row_block, row_block],
            (ids, *near(e.act, e.dh), x_own, e.hat_oth, Raw(up_weight), *near(*e.ups), Raw(down_weight)),
            scratch=[
                pltpu.VMEM((8, width), f32),
                pltpu.VMEM((4, half, step), bf16),
                pltpu.VMEM((4, step, width), bf16),
                pltpu.SemaphoreType.DMA((4,)),
                pltpu.SemaphoreType.DMA((4,)),
            ],
            room=18,
        )
        e.n_recv, e.ds_recv = swap_x(n_send), swap_x(ds_oth)

    def down_sum():
        value = high_sum(sum_of(*e.down.parts, "down_sum"))
        e.down.parts = (value, swap_ctx(value, low // 2))

    def up_part():
        part = ((1, rows, half), bf16, True)
        own, send = call(up_part_kernel, "up_part", [part, part], near(*e.up.parts))
        own, send = high_sum(own), high_sum(send)
        e.up.parts = (own, swap_x(send))

    def up_join():
        value = call(up_join_kernel, "up_join", [((1, rows, width), bf16, True)], near(*e.up.parts))[0]
        e.up.parts = (value, swap_ctx(value, low // 2))

    def pair():
        keep, send = call(
            pair_kernel,
            "pair",
            [((half, width), bf16, True), ((half, width), bf16, True)],
            (
                ids, e.first_own, e.first_oth, *near(e.dm_own, e.dm_oth), e.o_own, *near(e.o_oth),
                dy_own, e.dy_far,
            ),
            scratch=[pltpu.VMEM((half, width), f32), pltpu.VMEM((half, width), f32)],
            room=8,
        )
        e.pair.parts = (keep, swap_ctx(send, 1))

    def pair_sum():
        value = high_sum(sum_of(*e.pair.parts, "pair_sum"))
        e.pair.parts = (value, swap_ctx(value, low // 2))

    def mix():
        y_send = call(
            mix_kernel, "mix", [((tokens, width), bf16, True)], (e.ff_oth, *near(e.o_oth), out_weight)
        )[0]
        e.y_recv = swap_x(y_send)

    def result():
        e.result = call(
            result_kernel,
            "result",
            [token_low],
            (ids, x_own, e.ff_own, e.o_own, out_weight, *near(e.y_recv), p_own, e.p_oth),
        )[0]

    def dm_kv():
        e.dm_kv = call(
            dm_kv_kernel, "dm_kv", [((tokens, 128), bf16, True)], (*near(*e.kv.parts), kv_grad_later[0], *tables)
        )[0]
        e.dm_kv_oth = swap_x(e.dm_kv)

    def x_grad():
        e.x_grad = call(
            x_grad_kernel,
            "x_grad",
            [token_f32],
            (
                ids, x_own, dy_own, *near(e.dm_own, e.dm_kv), qkv_weight, e.q_far, p_own, e.p_oth,
                e.ds_own, *near(e.ds_recv),
            ),
            scratch=[pltpu.VMEM((tokens, width), f32)],
            room=8,
        )[0]

    def tail():
        value = call(
            tail_kernel,
            "tail",
            [((half + 32, 128), bf16, True)],
            (
                ids, e.first_own, e.first_oth, *near(e.dm_own, e.dm_oth), dy_own, e.dy_far,
                *near(e.dm_kv, e.dm_kv_oth), e.n_mine, *near(e.n_recv), e.up_sum, x_own,
                e.hat_half, qkv_weight, p_own,
            ),
            scratch=[pltpu.VMEM((half + 32, 128), f32), pltpu.VMEM((tokens, width), f32)],
            room=8,
        )[0]
        e.tail.parts = (value, swap_ctx(value, 1))

    def tail_step(stride):
        value = sum_of(*e.tail.parts, "tail_sum")
        e.tail.parts = (value, swap_ctx(value, stride)) if stride < devices else (value,)

    def tail_last():
        stride = 16
        while stride < devices:
            tail_step(stride)
            stride *= 2
        tail_step(devices)

    def down_out():
        e.g_down = call(down_out_kernel, "down_out", [((wide, width), f32, False)], (ids, *near(*e.down.parts)), room=8)[0]

    def up_out():
        e.g_up = call(up_out_kernel, "up_out", [((half, 2 * wide), f32, False)], (ids, *near(*e.up.parts)), room=8)[0]

    def attn_out():
        vec = ((half,), f32, False)
        e.small = call(
            attn_out_kernel,
            "attn_out",
            [
                ((half, width + 128), f32, False), ((half, width), f32, False), vec, vec, vec, vec,
                (qkv_bias.shape, f32, False), vec, (up_bias.shape, f32, False), vec,
            ],
            (ids, *near(*e.pair.parts), *near(*e.tail.parts)),
            room=6,
        )

    def steps(function, chain, masks, name):
        return [partial(function, chain, mask, name) for mask in masks]

    halves, shares = (2, 4, 8), (low // 4, low // 8, low // 16)
    down_add, up_add = steps(add_step, e.down, halves, "down_add"), steps(add_step, e.up, halves, "up_add")
    pair_add, kv_add = steps(add_step, e.pair, halves, "pair_add"), steps(add_step, e.kv, halves, "kv_add")
    down_join, up_join_steps = steps(join_step, e.down, shares, "down_join"), steps(join_step, e.up, shares, "up_join")
    pair_join = steps(join_step, e.pair, shares, "pair_join")
    tail_add = [partial(tail_step, mask) for mask in halves]
    order = [
        front, cotangent, ff, down_add[0], up_add[0], query, partial(forward, 0), down_add[1],
        partial(backward, 0), down_add[2], up_add[1], partial(forward, 1), partial(backward, 1), pile,
        kv_add[0], down_sum, up_add[2], ff_rest, kv_add[1], pair, up_part, down_join[0], mix, pair_add[0],
        kv_add[2], kv_more, up_join, dm_kv, pair_add[1], down_join[1], up_join_steps[0], pair_add[2], tail, x_grad,
        tail_add[0], pair_sum, up_join_steps[1], tail_add[1], result, down_join[2], pair_join[0], pair_join[1],
        tail_add[2], up_join_steps[2], tail_last, pair_join[2], attn_out, down_out, up_out,
    ]
    CHAIN.clear()
    for run in order:
        run()
    CHAIN.clear()
    result, grad_inputs, g_down, g_up = e.result, e.x_grad, e.g_down, e.g_up
    g_qkv, g_out, *small = e.small
    n0, n1, n2, n3, qb, ob, ub, db = small
    return (result[None], grad_inputs[None], n0, n1, n2, n3, g_qkv, qb, g_out, ob, g_up, ub, g_down, db)


def solution(mesh):
    token = P("fsdp", "ctx", None)
    vec = P("fsdp")
    mat = P("fsdp", None)
    return jax.shard_map(
        body,
        mesh=mesh,
        in_specs=(token, mat, vec, vec, vec, vec, mat, vec, mat, vec, mat, vec, mat, vec, token, token),
        out_specs=(token, token, vec, vec, vec, vec, mat, vec, mat, vec, mat, vec, mat, vec),
        check_vma=False,
    )
```
